32 devices in a mesh: dp: 4 (over y, x), seq: 4 (over z), tensor: 2 (over core).
Axes of the slice: x: 2, y: 2, z: 4, core: 2. Of those that a mesh axis runs over, the one named last changes fastest.
Arguments:
- byte_ids: int32 [4, 4096], P('dp', 'seq'), may hold values from 0 to 255
- pad_lengths: int32 [4], P('dp'), may hold values from 0 to 2048
- table: bfloat16 [256, 2048], P(None, 'tensor'), may hold values from -6 to 6
- conv_weight: float32 [3, 2048], P(None, 'tensor'), may hold values from -4 to 4
- score_weight: float32 [2048], P('tensor'), may hold values from -0.25 to 0.25
- norm_gain: float32 [2048], P('tensor'), may hold values from 0.5 to 1.5
- query_weight: bfloat16 [2048, 1024], P('tensor'), may hold values from -0.125 to 0.125
- query_grad: bfloat16 [4, 2048, 1024], P('dp', 'seq'), may hold values from -6 to 6
Outputs:
- grad_table: bfloat16 [256, 2048], P(None, 'tensor')
- grad_conv: float32 [3, 2048], P(None, 'tensor')
- grad_score: float32 [2048], P('tensor')
- grad_gain: float32 [2048], P('tensor')
- grad_wq: bfloat16 [2048, 1024], P('tensor', 'seq')
The draws below stay inside these ranges and needn't reach their ends.
All inputs are finite; a program needn't handle non-finite values.
Results may differ from the reference program's by a relative error of at most 0.0095.
Values may be sent and summed in bfloat16 or wider, within the bound.
A program may use at most 128 MiB of HBM per device.

```python
import math
import jax
import jax.numpy as jnp
import numpy as np
from jax import lax

D = 2048
VOCAB = 256
BYTES_DEV = 1024
QW = 1024
DOCS = 4
BYTES = 4096
ROWS = 2048
N_SEQ = 4


def plant(entries, own_key, low, largest):
    shape = entries.shape
    place = [jax.random.randint(jax.random.fold_in(own_key, axis), (), 0, shape[axis]) for axis in range(len(shape))]
    entries = entries.at[tuple(place)].set(low)
    longest = shape.index(max(shape))
    place[longest] = (place[longest] + 1) % shape[longest]
    return entries.at[tuple(place)].set(largest)


def spiked(values, key, source, target, blocks, factor):
    owner, partner = [(jnp.arange(values.shape[position]) // (values.shape[position] // blocks)).reshape([-1 if axis == position else 1 for axis in range(values.ndim)]) for position in (source, target)]
    chosen = jax.random.permutation(key, blocks)[partner]
    strong = (owner == chosen) | (owner == (partner + blocks // 2) % blocks)
    return jnp.where(strong, factor * values, values)


def block_levels(rng, shape, split, smallest, largest):
    def one(position, shards_of):
        steps = jax.random.uniform(jax.random.fold_in(jax.random.fold_in(rng, 6), position), (shards_of,), jnp.float32, smallest / len(split), largest / len(split))
        return jnp.repeat(jnp.exp(steps), shape[position] // shards_of).reshape((-1,) + (1,) * (len(shape) - position - 1))

    level = one(*split[0])
    for cut in split[1:]:
        level = level * one(*cut)
    return level


def cumulative_ranks(number_of, slope):
    loads = [(1 << 20) // math.isqrt(rank ** slope) + 1 for rank in range(1, number_of + 1)]
    spread = 1 + sum(loads) // (1 << 30)
    return np.cumsum(np.array([max(1, weight // spread) for weight in loads]))


def skewed_ids(key, extent, count, skew):
    grid = cumulative_ranks(count, skew)
    ticket = jax.random.randint(jax.random.fold_in(key, 1), extent, 0, int(grid[count - 1]))
    rank = jnp.searchsorted(jnp.asarray(grid, jnp.int32), ticket, side="right")
    return jax.random.permutation(jax.random.fold_in(key, 2), count)[rank].astype(jnp.int32)


def noise(stream_key, extent, spread, reach, shards=(), held_as=jnp.bfloat16):
    gain = block_levels(stream_key, extent, shards, -0.22, 0.18) if shards else 1.0
    entries = jax.random.normal(stream_key, extent, jnp.float32) * spread * gain
    return jnp.minimum(jnp.maximum(entries, -reach), reach).astype(held_as)


def noise_with(key, shape, spread, reach, pieces, heavy, kind=jnp.bfloat16):
    array = spread * jax.random.normal(key, shape, jnp.float32)
    if pieces:
        array = array * block_levels(key, shape, pieces, -0.22, 0.18)
    return jnp.clip(spiked(array, jax.random.fold_in(key, 3), *heavy), -reach, reach).astype(kind)


def setup_inputs(seed: int = 0) -> dict:
    arg_keys = jax.random.split(jax.random.key(seed), 9)
    return {
        "byte_ids": plant(skewed_ids(arg_keys[0], (DOCS, BYTES), VOCAB, 2), jax.random.fold_in(arg_keys[0], 3), 0, VOCAB - 1).astype(jnp.int32),
        "pad_lengths": plant(jax.random.randint(arg_keys[1], (DOCS,), 0, BYTES // 2 + 1), jax.random.fold_in(arg_keys[1], 1), 0, (BYTES // 2 + 1) - 1).astype(jnp.int32),
        "table": noise(arg_keys[2], (VOCAB, D), 1.0, 6.0, ((1, 2),)),
        "conv_weight": noise(arg_keys[3], (3, D), 0.6, 4.0, ((1, 2),), jnp.float32),
        "score_weight": noise(arg_keys[4], (D,), (D // 4) ** -0.5, 0.25, ((0, 2),), jnp.float32),
        "norm_gain": jnp.clip(1.0 + 0.1 * jax.random.normal(arg_keys[5], (D,), jnp.float32), 0.5, 1.5),
        "query_weight": noise(arg_keys[6], (D, QW), D ** -0.5, 0.125, ((0, 2),)),
        "query_grad": noise_with(arg_keys[7], (DOCS, ROWS, QW), 1.0, 6.0, ((0, 4), (1, 4)), (1, 2, 4, 2.0)),
    }


EPS = 1e-06

def block_means(rows, width):
    count = rows.shape[0]
    chans = rows.shape[1]
    grouped = lax.optimization_barrier(jnp.mean(rows.reshape(count // width, width, chans), axis=1))
    return jnp.repeat(grouped, width, axis=0)

def piece_normed(embed, conv_weight, score_weight, norm_gain, start):
    count = embed.shape[0] - 6
    pos_c = start + jnp.arange(-2, count + 2, dtype=jnp.int32)
    valid_c = ((pos_c >= 0) & (pos_c < BYTES)).astype(jnp.float32)[:, None]
    conv = (conv_weight[0] * embed[0:count + 4] + conv_weight[1] * embed[1:count + 5] + conv_weight[2] * embed[2:count + 6]) * valid_c
    own = conv[2:count + 2]
    resid = (start + jnp.arange(count, dtype=jnp.int32)) % 3
    third = jnp.zeros_like(own)
    for shift in range(-2, 3):
        keep = ((resid >= -shift) & (resid <= 2 - shift)).astype(jnp.float32)[:, None]
        third = third + keep * conv[2 + shift:2 + shift + count] / 3.0
    cands = [own, block_means(own, 2), third, block_means(own, 4)]
    scores = jnp.stack([lax.optimization_barrier(jnp.sum(cand * score_weight, axis=1)) for cand in cands])
    expo = jnp.exp(scores)
    probs = expo / lax.optimization_barrier(jnp.sum(expo, axis=0, keepdims=True))
    mixed = probs[0][:, None] * cands[0]
    for block in range(1, 4):
        mixed = mixed + probs[block][:, None] * cands[block]
    pooled = lax.optimization_barrier(jnp.mean(mixed.reshape(count // 2, 2, mixed.shape[1]), axis=1))
    scale = lax.rsqrt(lax.optimization_barrier(jnp.mean(pooled * pooled, axis=1)) + EPS)[:, None]
    return pooled * scale * norm_gain

def reference(byte_ids, pad_lengths, table, conv_weight, score_weight, norm_gain, query_weight, query_grad):
    table_f = table.astype(jnp.float32)
    padded_ids = jnp.pad(byte_ids, ((0, 0), (3, 3)))
    half = BYTES_DEV // 2

    def one_piece(carry, item):
        table_acc, conv_acc, score_acc, gain_acc, query_acc = carry
        doc = (item // N_SEQ).astype(jnp.int32)
        start = (item % N_SEQ * BYTES_DEV).astype(jnp.int32)
        ids_ext = lax.dynamic_slice(padded_ids, (doc, start), (1, BYTES_DEV + 6))[0]
        limit = BYTES - pad_lengths[doc]
        pos_e = start + jnp.arange(-3, BYTES_DEV + 3, dtype=jnp.int32)
        valid_e = ((pos_e >= 0) & (pos_e < limit)).astype(jnp.float32)[:, None]
        embed = table_f[ids_ext] * valid_e
        row_pos = start // 2 + jnp.arange(half, dtype=jnp.int32)
        row_keep = (2 * row_pos < limit)[:, None]
        grads = lax.dynamic_slice(query_grad, (doc, start // 2, jnp.int32(0)), (1, half, QW))[0]
        grads = jnp.where(row_keep, grads, jnp.zeros_like(grads))

        def forward(emb, cw, sw, ng):
            return piece_normed(emb, cw, sw, ng, start)
        normed_f, pull = jax.vjp(forward, embed, conv_weight, score_weight, norm_gain)
        normed_grad = jnp.dot(grads, query_weight.T, preferred_element_type=jnp.float32)
        d_embed, d_conv, d_score, d_gain = pull(normed_grad)
        table_acc = table_acc.at[ids_ext].add(d_embed * valid_e)
        normed = normed_f.astype(jnp.bfloat16)
        query_acc = query_acc + jnp.dot(normed.T, grads, preferred_element_type=jnp.float32)
        return ((table_acc, conv_acc + d_conv, score_acc + d_score, gain_acc + d_gain, query_acc), None)
    init = (jnp.zeros((VOCAB, D), jnp.float32), jnp.zeros((3, D), jnp.float32), jnp.zeros((D,), jnp.float32), jnp.zeros((D,), jnp.float32), jnp.zeros((D, QW), jnp.float32))
    final, unused = lax.scan(one_piece, init, jnp.arange(DOCS * N_SEQ, dtype=jnp.int32))
    table_acc, conv_acc, score_acc, gain_acc, query_acc = final
    return (table_acc.astype(jnp.bfloat16), conv_acc, score_acc, gain_acc, query_acc.astype(jnp.bfloat16))
```

```python
import functools

import jax
import jax.numpy as jnp
from jax import lax
from jax.experimental import pallas as pl
from jax.experimental.pallas import tpu as pltpu
from jax.sharding import PartitionSpec as P

D = 2048
EPS = 1e-06
F32 = jnp.float32
BF16 = jnp.bfloat16
OFFS = range(-2, 4)
CHUNK = 256

NN = (((1,), (0,)), ((), ()))
NT = (((1,), (1,)), ((), ()))
TN = (((0,), (0,)), ((), ()))


def mm(lhs, rhs, dims):
    return lax.dot_general(lhs, rhs, dims, preferred_element_type=F32)


def block_weights(start, total, rows):
    i = lax.broadcasted_iota(jnp.int32, (1, rows), 1)
    even = (i % 2) == 0
    inside = {o: (start + 2 * i + o >= 0) & (start + 2 * i + o < total) for o in OFFS}
    table = []
    for b in range(4):
        for p in range(2):
            row = {}
            for o in OFFS:
                if b == 0:
                    if o == p:
                        row[o] = jnp.where(inside[o], 1.0, 0.0)
                elif b == 1:
                    if o in (0, 1):
                        row[o] = jnp.where(inside[o], 0.5, 0.0)
                elif b == 3:
                    if o in (0, 1):
                        row[o] = jnp.where(inside[o], 0.25, 0.0)
                    else:
                        row[o] = jnp.where(inside[o] & (even if o > 1 else ~even), 0.25, 0.0)
                else:
                    d = o - p
                    if -2 <= d <= 2:
                        r = (start + 2 * i + p) % 3
                        row[o] = jnp.where(inside[o] & (r >= -d) & (r <= 2 - d), 1.0 / 3.0, 0.0)
            table.append(row)
    return table


def spread(idm, rows_of, tap):
    rows = idm.shape[1]
    v = lax.broadcasted_iota(jnp.int32, (256, rows), 0)
    acc = None
    for o in OFFS:
        at = o + tap + 2
        term = jnp.where(idm[at : at + 1, :] == v, rows_of[o], 0.0)
        acc = term if acc is None else acc + term
    return acc


def forward_kernel(
    pos_ref, idm_ref, p_ref, table_ref, cw_ref, gain_ref, wq_ref, g_ref,
    pooled_ref, ng_ref, wt_ref, sums_ref, rows_ref, grads_ref,
    wh, wl, r1, r2, sq, rd,
):
    start, limit, total = pos_ref[0], pos_ref[1], pos_ref[2]
    rows = idm_ref.shape[1]
    chans = table_ref.shape[1]
    idm = idm_ref[...]
    v = lax.broadcasted_iota(jnp.int32, (256, rows), 0)
    p = p_ref[...]
    hi = p.astype(BF16)
    rest = p - hi.astype(F32)
    mid = rest.astype(BF16)
    low = (rest - mid.astype(F32)).astype(BF16)
    p3 = jnp.concatenate([hi.astype(F32), mid.astype(F32), low.astype(F32)], axis=0).astype(BF16)
    picks = []
    for j in range(8):
        hot = jnp.where(idm[j : j + 1, :] == v, 1.0, 0.0).astype(BF16)
        g = mm(p3, hot, NN)
        picks.append(g[0:8] + g[8:16] + g[16:24])
    s = {o: picks[o + 2][0:1] + picks[o + 3][1:2] + picks[o + 4][2:3] for o in OFFS}
    weights = block_weights(start, total, rows)
    expo = []
    for row in weights:
        score = None
        for o in row:
            score = row[o] * s[o] if score is None else score + row[o] * s[o]
        expo.append(jnp.exp(score))
    probs = []
    for n in range(8):
        whole = expo[n % 2] + expo[2 + n % 2] + expo[4 + n % 2] + expo[6 + n % 2]
        probs.append(expo[n] / whole)
    a = {}
    for o in OFFS:
        acc = None
        for n in range(8):
            if o in weights[n]:
                term = probs[n] * weights[n][o]
                acc = term if acc is None else acc + term
        a[o] = 0.5 * acc
    rows_ref[...] = jnp.concatenate(probs, axis=0)
    for k in range(3):
        w = spread(idm, a, k)
        wt_ref[k] = w.astype(BF16)
        wf = w.T
        top = wf.astype(BF16)
        wh[k] = top
        wl[k] = (wf - top.astype(F32)).astype(BF16)
    keep = (start + 2 * lax.broadcasted_iota(jnp.int32, g_ref.shape, 0)) < limit
    grads_ref[...] = jnp.where(keep, g_ref[...].astype(F32), 0.0).astype(BF16)
    r1[...] = jnp.zeros_like(r1)
    r2[...] = jnp.zeros_like(r2)
    sq[...] = jnp.zeros_like(sq)
    rd[...] = jnp.zeros_like(rd)

    def step(c, carry):
        at = pl.ds(pl.multiple_of(c * CHUNK, CHUNK), CHUNK)
        tab = table_ref[:, at]
        cw = cw_ref[:, at]
        ng = mm(grads_ref[...], wq_ref[at, :], NT)
        pooled = None
        for k in range(3):
            part = cw[k : k + 1] * (mm(wh[k], tab, NN) + mm(wl[k], tab, NN))
            pooled = part if pooled is None else pooled + part
        pooled_ref[:, at] = pooled
        ng_ref[:, at] = ng
        gained = ng * gain_ref[:, at]
        square = pooled * pooled
        inner = pooled * gained
        sq[...] += square[:, 0:128] + square[:, 128:256]
        rd[...] += inner[:, 0:128] + inner[:, 128:256]
        gb = gained.astype(BF16)
        pb = pooled.astype(BF16)
        for k in range(3):
            tk = (tab.astype(F32) * cw[k : k + 1]).astype(BF16)
            r1[k] += mm(tk, gb, NT)
            r2[k] += mm(tk, pb, NT)
        return carry

    lax.fori_loop(0, chans // CHUNK, step, 0)
    out = []
    for r in (r1, r2):
        for o in OFFS:
            acc = None
            for k in range(3):
                at = o + k + 2
                term = jnp.where(idm[at : at + 1, :] == v, r[k], 0.0)
                acc = term if acc is None else acc + term
            out.append(jnp.sum(acc, axis=0, keepdims=True))
    out.append(jnp.sum(sq[...].T, axis=0, keepdims=True))
    out.append(jnp.sum(rd[...].T, axis=0, keepdims=True))
    out.append(jnp.zeros((2, rows), F32))
    sums_ref[...] = jnp.concatenate(out, axis=0)


def backward_kernel(
    pos_ref, idm_ref, sums_ref, rows_ref, table_ref, cw_ref, sw_ref, gain_ref,
    pooled_ref, ng_ref, wt_ref, grads_ref,
    query_ref, tab_ref, small_ref,
):
    start, total = pos_ref[0], pos_ref[2]
    rows = idm_ref.shape[1]
    chans = table_ref.shape[1]
    idm = idm_ref[...]
    sums = sums_ref[...]
    probs = rows_ref[...]
    square, inner = sums[12:13], sums[13:14]
    scale = lax.rsqrt(square / D + EPS)
    pull = scale * scale * scale * (inner / D)
    q = {o: scale * sums[o + 2 : o + 3] - pull * sums[o + 8 : o + 9] for o in OFFS}
    weights = block_weights(start, total, rows)
    pgrad = []
    for row in weights:
        acc = None
        for o in row:
            acc = row[o] * q[o] if acc is None else acc + row[o] * q[o]
        pgrad.append(0.5 * acc)
    sgrad = []
    for n in range(8):
        mean = None
        for m in range(n % 2, 8, 2):
            term = probs[m : m + 1] * pgrad[m]
            mean = term if mean is None else mean + term
        sgrad.append(probs[n : n + 1] * (pgrad[n] - mean))
    ds = {}
    for o in OFFS:
        acc = None
        for n in range(8):
            if o in weights[n]:
                term = sgrad[n] * weights[n][o]
                acc = term if acc is None else acc + term
        ds[o] = acc
    hist = [jnp.sum(spread(idm, ds, k), axis=1, keepdims=True) for k in range(3)]
    cols = jnp.concatenate([scale, pull, jnp.zeros((6, rows), F32)], axis=0).T
    scale_c, pull_c = cols[:, 0:1], cols[:, 1:2]

    for c in range(chans // CHUNK):
        at = pl.ds(c * CHUNK, CHUNK)
        tab = table_ref[:, at].astype(F32)
        cw = cw_ref[:, at]
        sw = sw_ref[:, at]
        gain = gain_ref[:, at]
        ps = pooled_ref[:, at] * scale_c
        ng = ng_ref[:, at]
        gain_term = jnp.sum(ng * ps, axis=0, keepdims=True)
        normed = (ps * gain).astype(BF16)
        query_ref[at, :] = mm(normed, grads_ref[...], TN).astype(query_ref.dtype)
        pg = (ng * gain * scale_c - pull_c * pooled_ref[:, at]).astype(BF16)
        total_t = None
        outs = []
        score = None
        for k in range(3):
            full = mm(wt_ref[k], pg, NN) + hist[k] * sw
            term = cw[k : k + 1] * full
            total_t = term if total_t is None else total_t + term
            outs.append(jnp.sum(full * tab, axis=0, keepdims=True))
            term = cw[k : k + 1] * jnp.sum(hist[k] * tab, axis=0, keepdims=True)
            score = term if score is None else score + term
        tab_ref[:, at] = total_t.astype(tab_ref.dtype)
        small_ref[:, at] = jnp.concatenate(
            outs + [score, gain_term, jnp.zeros((3, CHUNK), F32)], axis=0
        )


def body(
    byte_ids, pad_lengths, table, conv_weight, score_weight, norm_gain, query_weight, query_grad
):
    ids = byte_ids[0]
    count = ids.shape[0]
    rows = count // 2
    vocab, chans = table.shape
    width = query_grad.shape[2]
    n_seq = lax.axis_size("seq")
    total = count * n_seq
    start = lax.axis_index("seq") * count
    limit = total - pad_lengths[0]
    ends = n_seq - 1
    up = [(i, i + 1) for i in range(ends)]
    down = [(i + 1, i) for i in range(ends)]
    ids_ext = jnp.concatenate(
        [lax.ppermute(ids[count - 3 :], "seq", up), ids, lax.ppermute(ids[:3], "seq", down)]
    )
    pos_e = start + jnp.arange(-3, count + 3, dtype=jnp.int32)
    ids_ext = jnp.where((pos_e >= 0) & (pos_e < limit), ids_ext, -1)
    halves = ids_ext.reshape(rows + 3, 2).T
    idm = jnp.stack([halves[j % 2, j // 2 : j // 2 + rows] for j in range(8)])
    pos = jnp.stack([start, limit, jnp.full_like(start, total)]).astype(jnp.int32)

    part = jnp.dot(
        conv_weight * score_weight, table.astype(F32).T, precision=lax.Precision.HIGHEST
    )
    p = jnp.pad(lax.psum(part, "tensor"), ((0, 5), (0, 0)))

    vm = pl.BlockSpec(memory_space=pltpu.VMEM)
    sm = pl.BlockSpec(memory_space=pltpu.SMEM)
    sw = score_weight[None, :]
    gain = norm_gain[None, :]
    pooled, ng, wt, sums, probs, grads = pl.pallas_call(
        forward_kernel,
        out_shape=(
            jax.ShapeDtypeStruct((rows, chans), F32),
            jax.ShapeDtypeStruct((rows, chans), F32),
            jax.ShapeDtypeStruct((3, vocab, rows), BF16),
            jax.ShapeDtypeStruct((16, rows), F32),
            jax.ShapeDtypeStruct((8, rows), F32),
            jax.ShapeDtypeStruct((rows, width), BF16),
        ),
        in_specs=[sm] + [vm] * 7,
        out_specs=(vm,) * 6,
        scratch_shapes=[
            pltpu.VMEM((3, rows, vocab), BF16),
            pltpu.VMEM((3, rows, vocab), BF16),
            pltpu.VMEM((3, vocab, rows), F32),
            pltpu.VMEM((3, vocab, rows), F32),
            pltpu.VMEM((rows, 128), F32),
            pltpu.VMEM((rows, 128), F32),
        ],
        name="forward",
    )(pos, idm, p, table, conv_weight, gain, query_weight, query_grad[0])
    sums = lax.psum(sums, "tensor")
    query, tab, small = pl.pallas_call(
        backward_kernel,
        out_shape=(
            jax.ShapeDtypeStruct((chans, width), BF16),
            jax.ShapeDtypeStruct((vocab, chans), BF16),
            jax.ShapeDtypeStruct((8, chans), F32),
        ),
        in_specs=[sm] + [vm] * 11,
        out_specs=(vm,) * 3,
        name="backward",
    )(pos, idm, sums, probs, table, conv_weight, sw, gain, pooled, ng, wt, grads)

    share = lax.psum_scatter(query, "seq", scatter_dimension=1, tiled=True)
    query_out = lax.psum(share, "dp")
    tab_out = lax.psum(tab, ("dp", "seq"))
    small_out = lax.psum(small, ("dp", "seq"))
    return (tab_out, small_out[0:3], small_out[3], small_out[4], query_out)


MESH = pl.DeviceIdType.MESH
BLOCK = 16
TILE = 256


def stacked(value):
    hi = value.astype(BF16)
    rest = value - hi.astype(F32)
    mid = rest.astype(BF16)
    low = (rest - mid.astype(F32)).astype(BF16)
    return jnp.concatenate([hi.astype(F32), mid.astype(F32), low.astype(F32)], axis=0).astype(BF16)


def packed_weights(start, total, rows):
    n = lax.broadcasted_iota(jnp.int32, (8, rows), 0)
    i = lax.broadcasted_iota(jnp.int32, (8, rows), 1)
    b, p = n // 2, n % 2
    even = (i % 2) == 0
    r = (start + 2 * i + p) % 3
    table = []
    for o in OFFS:
        at = start + 2 * i + o
        inside = (at >= 0) & (at < total)
        d = o - p
        near = (d >= -2) & (d <= 2) & (r >= -d) & (r <= 2 - d)
        w = jnp.where((b == 2) & near, 1.0 / 3.0, 0.0)
        w = jnp.where((b == 0) & (p == o), 1.0, w)
        if o in (0, 1):
            w = jnp.where(b == 1, 0.5, w)
            w = jnp.where(b == 3, 0.25, w)
        else:
            w = jnp.where((b == 3) & (even if o > 1 else ~even), 0.25, w)
        table.append(jnp.where(inside, w, 0.0))
    return table


def over_blocks(value):
    return value + pltpu.roll(value, 2, 0) + pltpu.roll(value, 4, 0) + pltpu.roll(value, 6, 0)


def fused_kernel(
    pad_ref, eo_ref, table_ref, cw_ref, sw_ref, gain_ref, wq_hbm, g_hbm,
    tab_ref, small_ref, query_ref,
    wq, g, tk, wt, wcat, pooled, ng, gb, pb, q, idm_s, w8_s, probs_s, hist, rr, lanes,
    p_own, p_in, halo, x1_own, x1_in, x2_own, x2_in,
    r1, s2, r2, zb, zr, own_z, tb, tr, ts, tz, sm, sz, sd,
    in_sem, s_halo, r_halo, s_core, r_core, s_p1, r_p1, s_p2, r_p2, s_z, r_z, s_ag, r_ag,
    s_t, r_t, s_sm, r_sm,
):
    d, s, t = lax.axis_index("dp"), lax.axis_index("seq"), lax.axis_index("tensor")
    n_seq = lax.axis_size("seq")
    x, y = d % 2, d // 2
    x_near = y * 2 + (1 - x)
    y_near = (1 - y) * 2 + x
    corner = (1 - y) * 2 + (1 - x)
    dp_peers = (x_near, y_near, corner)
    seq_peers = [(s + e) % n_seq for e in range(1, n_seq)]
    rows = eo_ref.shape[1]
    vocab, chans = table_ref.shape
    width = g.shape[1]
    count = 2 * rows
    total = count * n_seq
    start = s * count
    limit = total - pad_ref[0]
    half, quarter, eighth = chans // 2, chans // 4, chans // 8
    cols = width // n_seq
    t_dp, t_seq = vocab // 4, vocab // 4 // n_seq

    def remote(src, dst, send, recv, to):
        return pltpu.make_async_remote_copy(
            src_ref=src, dst_ref=dst, send_sem=send, recv_sem=recv,
            device_id=to, device_id_type=MESH,
        )

    take_g = pltpu.make_async_copy(g_hbm, g, in_sem.at[0])
    take_w = pltpu.make_async_copy(wq_hbm, wq, in_sem.at[1])
    take_g.start()
    take_w.start()

    barrier = pltpu.get_barrier_semaphore()
    peers = [(dd, s, t) for dd in dp_peers] + [(d, ss, t) for ss in seq_peers] + [(d, s, 1 - t)]
    for peer in peers:
        pl.semaphore_signal(barrier, inc=1, device_id=peer, device_id_type=MESH)

    cs = cw_ref[...] * sw_ref[...]
    p_own[...] = sum_parts(mm(stacked(pad8(cs)), table_ref[...], NT))
    pl.semaphore_wait(barrier, len(peers))

    put_p = remote(p_own, p_in, s_core.at[0], r_core.at[0], (d, s, 1 - t))
    put_p.start()
    edge = eo_ref.shape[0]
    to_left = remote(
        eo_ref.at[:, pl.ds(0, 128)], halo.at[1], s_halo.at[0], r_halo.at[1],
        (d, jnp.maximum(s - 1, 0), t),
    )
    to_right = remote(
        eo_ref.at[:, pl.ds(rows - 128, 128)], halo.at[0], s_halo.at[1], r_halo.at[0],
        (d, jnp.minimum(s + 1, n_seq - 1), t),
    )

    @pl.when(s > 0)
    def _():
        to_left.start()

    @pl.when(s < n_seq - 1)
    def _():
        to_right.start()

    @pl.when(s == 0)
    def _():
        halo[0] = jnp.zeros((edge, 128), jnp.int32)

    @pl.when(s == n_seq - 1)
    def _():
        halo[1] = jnp.zeros((edge, 128), jnp.int32)

    for k in range(3):
        def spell(c, carry, k=k):
            at = pl.ds(pl.multiple_of(c * TILE, TILE), TILE)
            tk[k * vocab : (k + 1) * vocab, at] = (
                table_ref[:, at].astype(F32) * cw_ref[k : k + 1, at]
            ).astype(BF16)
            return carry

        lax.fori_loop(0, chans // TILE, spell, 0)
    take_g.wait()

    def mask(c, carry):
        at = pl.ds(pl.multiple_of(c * 64, 64), 64)
        i = lax.broadcasted_iota(jnp.int32, (64, width), 0) + c * 64
        g[at, :] = jnp.where(start + 2 * i < limit, g[at, :].astype(F32), 0.0).astype(BF16)
        return carry

    lax.fori_loop(0, rows // 64, mask, 0)

    @pl.when(s > 0)
    def _():
        to_right.wait_recv()
        to_left.wait_send()

    @pl.when(s < n_seq - 1)
    def _():
        to_left.wait_recv()
        to_right.wait_send()

    put_p.wait()

    wide = rows + 256
    cat = jnp.concatenate([halo[0], eo_ref[...], halo[1]], axis=1)
    lane = lax.broadcasted_iota(jnp.int32, cat.shape, 1)
    row = lax.broadcasted_iota(jnp.int32, cat.shape, 0)
    at_byte = start + 2 * (lane - 128) + row
    cat = jnp.where((at_byte >= 0) & (at_byte < limit) & (row < 2), cat, -1)
    core = slice(128, 128 + rows)
    p3 = stacked(p_own[...] + p_in[...])
    v_wide = lax.broadcasted_iota(jnp.int32, (vocab, wide), 0)

    def picked(line):
        hot = jnp.where(line == v_wide, 1.0, 0.0).astype(BF16)
        return sum_parts(mm(p3, hot, NN))

    even, odd = picked(cat[0:1]), picked(cat[1:2])
    sc_even = pltpu.roll(odd, 1, 1)[0:1] + even[1:2] + odd[2:3]
    sc_odd = even[0:1] + odd[1:2] + pltpu.roll(even, wide - 1, 1)[2:3]
    se = jnp.broadcast_to(sc_even, (8, wide))
    so = jnp.broadcast_to(sc_odd, (8, wide))
    scores = [
        pltpu.roll(se, 1, 1)[:, core], pltpu.roll(so, 1, 1)[:, core], se[:, core], so[:, core],
        pltpu.roll(se, wide - 1, 1)[:, core], pltpu.roll(so, wide - 1, 1)[:, core],
    ]
    w8 = packed_weights(start, total, rows)
    score = w8[0] * scores[0]
    for n in range(1, 6):
        score = score + w8[n] * scores[n]
    expo = jnp.exp(score)
    probs = expo / over_blocks(expo)
    a = [0.5 * jnp.sum(probs * w, axis=0, keepdims=True) for w in w8]
    probs_s[...] = probs
    for n in range(6):
        w8_s[n] = w8[n]
    back = [pltpu.roll(cat, n, 1)[:, core] for n in (2, 1)]
    fore = [pltpu.roll(cat, wide - n, 1)[:, core] for n in (1, 2)]
    here = cat[:, core]
    idm_s[...] = jnp.concatenate(
        [back[0][1:2], back[1][0:2], here[0:2], fore[0][0:2], fore[1][0:1]], axis=0
    )

    def spread_in(n, carry):
        at = pl.ds(pl.multiple_of(n * BLOCK, BLOCK), BLOCK)
        v = lax.broadcasted_iota(jnp.int32, (BLOCK, rows), 0) + n * BLOCK
        hits = [idm_s[j : j + 1, :] == v for j in range(8)]
        for k in range(3):
            acc = jnp.where(hits[k], a[0], 0.0)
            for o in range(1, 6):
                acc = acc + jnp.where(hits[o + k], a[o], 0.0)
            wt[k, at, :] = acc.astype(BF16)
        return carry

    lax.fori_loop(0, vocab // BLOCK, spread_in, 0)
    for k in range(3):
        wcat[:, k * vocab : (k + 1) * vocab] = wt[k].astype(F32).T.astype(BF16)

    lanes[...] = jnp.zeros_like(lanes)

    def pool(c, carry):
        at = pl.ds(pl.multiple_of(c * TILE, TILE), TILE)
        part = mm(wcat[...], tk[:, at], NN)
        pooled[:, at] = part
        pb[:, at] = part.astype(BF16)
        square = part * part
        lanes[...] += square[:, 0:128] + square[:, 128:256]
        return carry

    lax.fori_loop(0, chans // TILE, pool, 0)
    x1_own[...] = jnp.broadcast_to(jnp.sum(lanes[...].T, axis=0, keepdims=True), (8, rows))
    put_1 = remote(x1_own, x1_in, s_core.at[1], r_core.at[1], (d, s, 1 - t))
    put_1.start()
    put_1.wait()
    scale = lax.rsqrt((x1_own[...] + x1_in[...]) / D + EPS)
    scale_c = scale.T[:, 0:1]

    def product(at_row):
        at = pl.ds(pl.multiple_of(at_row, 128), quarter)
        normed = (pooled[:, at] * scale_c * gain_ref[:, at]).astype(BF16)
        q[at, :] = mm(normed, g[...], TN).astype(BF16)

    bit1, bit2 = (x, y), (y, x)
    near1 = ((x_near, s, t), (y_near, s, t))
    near2 = ((y_near, s, t), (x_near, s, t))

    def q_rows(h, first, second):
        return pl.ds(pl.multiple_of(h * half + first * quarter + second * eighth, eighth), eighth)

    p1 = {}
    for h in range(2):
        product(h * half + (1 - bit1[h]) * quarter)
        for part in range(2):
            second = bit2[h] if part else 1 - bit2[h]
            p1[h, part] = remote(
                q.at[q_rows(h, 1 - bit1[h], second)], r1.at[h, part],
                s_p1.at[h, part], r_p1.at[h, part], near1[h],
            )
            p1[h, part].start()
    for h in range(2):
        product(h * half + bit1[h] * quarter)

    take_w.wait()
    lanes[...] = jnp.zeros_like(lanes)

    def pull_back(c, carry):
        at = pl.ds(pl.multiple_of(c * TILE, TILE), TILE)
        part = mm(g[...], wq[at, :], NT)
        ng[:, at] = part
        gained = part * gain_ref[:, at]
        gb[:, at] = gained.astype(BF16)
        inner = pooled[:, at] * gained
        lanes[...] += inner[:, 0:128] + inner[:, 128:256]
        return carry

    lax.fori_loop(0, chans // TILE, pull_back, 0)
    found = []
    for source in (gb, pb):
        sums = tuple(jnp.zeros((8, rows), F32) for o in range(6))
        for k in range(3):
            rr[...] = mm(tk[k * vocab : (k + 1) * vocab, :], source[...], NT)

            def select(n, accs, k=k):
                line = rr[pl.ds(pl.multiple_of(n * 8, 8), 8), :]
                v = lax.broadcasted_iota(jnp.int32, (8, rows), 0) + n * 8
                return tuple(
                    accs[o] + jnp.where(idm_s[o + k : o + k + 1, :] == v, line, 0.0)
                    for o in range(6)
                )

            sums = lax.fori_loop(0, vocab // 8, select, sums)
        found += [jnp.sum(acc, axis=0, keepdims=True) for acc in sums]
    found.append(jnp.sum(lanes[...].T, axis=0, keepdims=True))
    found.append(jnp.zeros((3, rows), F32))
    x2_own[...] = jnp.concatenate(found, axis=0)
    put_2 = remote(x2_own, x2_in, s_core.at[2], r_core.at[2], (d, s, 1 - t))
    put_2.start()

    p2 = {}
    for h in range(2):
        p1[h, 0].wait_recv()
        rows_h = q_rows(h, bit1[h], 1 - bit2[h])
        s2[h] = (q[rows_h, :].astype(F32) + r1[h, 0].astype(F32)).astype(BF16)
        for e in range(n_seq):
            at = pl.ds(pl.multiple_of((s + e + 1) % n_seq * cols, 128), cols)
            p2[h, e] = remote(
                s2.at[h, :, at], r2.at[h, :, at], s_p2.at[h, e], r_p2.at[h, e], near2[h]
            )
            p2[h, e].start()

    put_2.wait()
    sums = x2_own[...] + x2_in[...]
    pull = scale[0:1] * scale[0:1] * scale[0:1] * (sums[12:13] / D)
    w8 = [w8_s[n] for n in range(6)]
    probs = probs_s[...]
    pgrad = None
    for o in range(6):
        term = w8[o] * (scale[0:1] * sums[o : o + 1] - pull * sums[o + 6 : o + 7])
        pgrad = term if pgrad is None else pgrad + term
    pgrad = 0.5 * pgrad
    sgrad = probs * (pgrad - over_blocks(probs * pgrad))
    ds = [jnp.sum(sgrad * w, axis=0, keepdims=True) for w in w8]

    def count_in(n, carry):
        at = pl.ds(pl.multiple_of(n * BLOCK, BLOCK), BLOCK)
        v = lax.broadcasted_iota(jnp.int32, (BLOCK, rows), 0) + n * BLOCK
        hits = [idm_s[j : j + 1, :] == v for j in range(8)]
        for k in range(3):
            acc = jnp.where(hits[k], ds[0], 0.0)
            for o in range(1, 6):
                acc = acc + jnp.where(hits[o + k], ds[o], 0.0)
            hist[k, at, :] = jnp.broadcast_to(jnp.sum(acc, axis=1, keepdims=True), (BLOCK, 128))
        return carry

    lax.fori_loop(0, vocab // BLOCK, count_in, 0)
    pull_c = jnp.broadcast_to(pull, (8, rows)).T[:, 0:1]

    def table_step(c, carry):
        at = pl.ds(pl.multiple_of(c * TILE, TILE), TILE)
        tab = table_ref[:, at].astype(F32)
        cw, sw, gain = cw_ref[:, at], sw_ref[:, at], gain_ref[:, at]
        ngc, pc = ng[:, at], pooled[:, at]
        scaled = ngc * scale_c
        gain_term = jnp.sum(scaled * pc, axis=0, keepdims=True)
        pg = (scaled * gain - pull_c * pc).astype(BF16)
        whole, outs, score = None, [], None
        for k in range(3):
            hist_k = hist[k][:, 0:1]
            full = mm(wt[k], pg, NN) + hist_k * sw
            term = cw[k : k + 1] * full
            whole = term if whole is None else whole + term
            outs.append(jnp.sum(full * tab, axis=0, keepdims=True))
            term = cw[k : k + 1] * jnp.sum(hist_k * tab, axis=0, keepdims=True)
            score = term if score is None else score + term
        tb[:, at] = whole.astype(BF16)
        sm[:, at] = jnp.concatenate(outs + [score, gain_term, jnp.zeros((3, TILE), F32)], axis=0)
        return carry

    lax.fori_loop(0, chans // TILE, table_step, 0)

    t_rs, sm_z = [], []
    for e, dd in enumerate(dp_peers):
        block = tb.at[pl.ds(pl.multiple_of(dd * t_dp, t_dp), t_dp)]
        t_rs.append(remote(block, tr.at[d], s_t.at[e], r_t.at[e], (dd, s, t)))
        t_rs[-1].start()
    for e, ss in enumerate(seq_peers):
        sm_z.append(remote(sm, sz.at[s], s_sm.at[e], r_sm.at[e], (d, ss, t)))
        sm_z[-1].start()
    tr[d] = tb[pl.ds(pl.multiple_of(d * t_dp, t_dp), t_dp), :]
    sz[s] = sm[...]

    for h in range(2):
        p1[h, 1].wait_recv()
    q_z = {}
    for e in range(n_seq):
        j = (s + e + 1) % n_seq
        at = pl.ds(pl.multiple_of(j * cols, 128), cols)
        for h in range(2):
            p2[h, e].wait_recv()
            rows_h = q_rows(h, bit1[h], bit2[h])
            block = q[rows_h, at].astype(F32) + r1[h, 1, :, at].astype(F32)
            block = block + r2[h, :, at].astype(F32)
            if e < n_seq - 1:
                zb[h, e] = block.astype(BF16)
                q_z[h, e] = remote(
                    zb.at[h, e], zr.at[h, e], s_z.at[h, e], r_z.at[h, e], (d, j, t)
                )
                q_z[h, e].start()
            else:
                own_z[h] = block

    for copy in t_rs:
        copy.wait_recv()
    acc = tr[0].astype(F32)
    for n in range(1, 4):
        acc = acc + tr[n].astype(F32)
    ts[...] = acc.astype(BF16)
    t_z = []
    for e, ss in enumerate(seq_peers):
        block = ts.at[pl.ds(pl.multiple_of(ss * t_seq, t_seq), t_seq)]
        t_z.append(remote(block, tz.at[s], s_t.at[3 + e], r_t.at[3 + e], (d, ss, t)))
        t_z[-1].start()
    tz[s] = ts[pl.ds(pl.multiple_of(s * t_seq, t_seq), t_seq), :]

    for copy in sm_z:
        copy.wait_recv()
    acc = sz[0]
    for n in range(1, n_seq):
        acc = acc + sz[n]
    sd[d] = acc
    sm_d = []
    for e, dd in enumerate(dp_peers):
        sm_d.append(remote(sd.at[d], sd.at[d], s_sm.at[3 + e], r_sm.at[3 + e], (dd, s, t)))
        sm_d[-1].start()

    q_ag = []
    for h in range(2):
        block = own_z[h]
        for e in range(n_seq - 1):
            q_z[h, e].wait_recv()
            block = block + zr[h, e].astype(F32)
        mine = q_rows(h, bit1[h], bit2[h])
        query_ref[mine, :] = block.astype(BF16)
        for e, dd in enumerate(dp_peers):
            q_ag.append(
                remote(
                    query_ref.at[mine], query_ref.at[mine], s_ag.at[h, e], r_ag.at[h, e], (dd, s, t)
                )
            )
            q_ag[-1].start()

    for copy in t_z:
        copy.wait_recv()
    acc = tz[0].astype(F32)
    for n in range(1, n_seq):
        acc = acc + tz[n].astype(F32)
    mine = pl.ds(pl.multiple_of(d * t_dp + s * t_seq, t_seq), t_seq)
    tab_ref[mine, :] = acc.astype(BF16)
    t_back = []
    for e, ss in enumerate(seq_peers):
        t_back.append(
            remote(tab_ref.at[mine], tab_ref.at[mine], s_t.at[6 + e], r_t.at[6 + e], (d, ss, t))
        )
        t_back[-1].start()
    for copy in t_back:
        copy.wait_recv()
    t_ag = []
    mine = pl.ds(pl.multiple_of(d * t_dp, t_dp), t_dp)
    for e, dd in enumerate(dp_peers):
        t_ag.append(
            remote(tab_ref.at[mine], tab_ref.at[mine], s_t.at[9 + e], r_t.at[9 + e], (dd, s, t))
        )
        t_ag[-1].start()

    for copy in sm_d:
        copy.wait_recv()
    small_ref[...] = (sd[0] + sd[1]) + (sd[2] + sd[3])
    for copy in q_ag + t_ag:
        copy.wait_recv()
    started = list(p1.values()) + list(p2.values()) + list(q_z.values())
    for copy in started + t_rs + t_z + t_back + t_ag + sm_z + sm_d + q_ag:
        copy.wait_send()


def pad8(value):
    return jnp.concatenate([value, jnp.zeros((8 - value.shape[0], value.shape[1]), F32)], axis=0)


def sum_parts(value):
    return value[0:8] + value[8:16] + value[16:24]


def fused_body(
    byte_ids, pad_lengths, table, conv_weight, score_weight, norm_gain, query_weight, query_grad
):
    count = byte_ids.shape[1]
    rows = count // 2
    vocab, chans = table.shape
    width = query_grad.shape[2]
    n_seq = lax.axis_size("seq")
    cols = width // n_seq
    part, t_dp = chans // 8, vocab // 4
    eo = jnp.pad(byte_ids[0].reshape(rows, 2).T, ((0, 6), (0, 0)))
    vm = pl.BlockSpec(memory_space=pltpu.VMEM)
    sm = pl.BlockSpec(memory_space=pltpu.SMEM)
    hbm = pl.BlockSpec(memory_space=pl.ANY)
    V, DMA = pltpu.VMEM, pltpu.SemaphoreType.DMA
    tab, small, query = pl.pallas_call(
        fused_kernel,
        out_shape=(
            jax.ShapeDtypeStruct((vocab, chans), BF16),
            jax.ShapeDtypeStruct((8, chans), F32),
            jax.ShapeDtypeStruct((chans, cols), BF16),
        ),
        in_specs=[sm] + [vm] * 5 + [hbm] * 2,
        out_specs=(vm,) * 3,
        scratch_shapes=[
            V((chans, width), BF16), V((rows, width), BF16), V((3 * vocab, chans), BF16),
            V((3, vocab, rows), BF16), V((rows, 3 * vocab), BF16), V((rows, chans), F32),
            V((rows, chans), F32), V((rows, chans), BF16), V((rows, chans), BF16),
            V((chans, width), BF16), V((8, rows), jnp.int32), V((6, 8, rows), F32),
            V((8, rows), F32), V((3, vocab, 128), F32), V((vocab, rows), F32), V((rows, 128), F32),
            V((8, vocab), F32), V((8, vocab), F32), V((2, 8, 128), jnp.int32),
            V((8, rows), F32), V((8, rows), F32), V((16, rows), F32), V((16, rows), F32),
            V((2, 2, part, width), BF16), V((2, part, width), BF16), V((2, part, width), BF16),
            V((2, n_seq - 1, part, cols), BF16), V((2, n_seq - 1, part, cols), BF16),
            V((2, part, cols), F32), V((vocab, chans), BF16), V((4, t_dp, chans), BF16),
            V((t_dp, chans), BF16), V((n_seq, t_dp // n_seq, chans), BF16),
            V((8, chans), F32), V((n_seq, 8, chans), F32), V((4, 8, chans), F32),
            DMA((2,)), DMA((2,)), DMA((2,)), DMA((3,)), DMA((3,)),
            DMA((2, 2)), DMA((2, 2)), DMA((2, n_seq)), DMA((2, n_seq)),
            DMA((2, n_seq - 1)), DMA((2, n_seq - 1)), DMA((2, 3)), DMA((2, 3)),
            DMA((12,)), DMA((12,)), DMA((6,)), DMA((6,)),
        ],
        compiler_params=pltpu.CompilerParams(collective_id=0, has_side_effects=True),
        name="fused",
    )(
        pad_lengths, eo, table, conv_weight, score_weight[None, :], norm_gain[None, :],
        query_weight, query_grad[0],
    )
    return (tab, small[0:3], small[3], small[4], query)


def fits(mesh):
    return mesh.shape["dp"] == 4 and mesh.shape["seq"] == 4 and mesh.shape["tensor"] == 2


def solution(mesh):
    return jax.shard_map(
        fused_body if fits(mesh) else body,
        mesh=mesh,
        in_specs=(
            P("dp", "seq"),
            P("dp"),
            P(None, "tensor"),
            P(None, "tensor"),
            P("tensor"),
            P("tensor"),
            P("tensor", None),
            P("dp", "seq", None),
        ),
        out_specs=(
            P(None, "tensor"),
            P(None, "tensor"),
            P("tensor"),
            P("tensor"),
            P("tensor", "seq"),
        ),
        check_vma=False,
    )
```

```python
import functools

import jax
import jax.numpy as jnp
from jax import lax
from jax.experimental import pallas as pl
from jax.experimental.pallas import tpu as pltpu
from jax.sharding import PartitionSpec as P

D = 2048
EPS = 1e-06
F32 = jnp.float32
BF16 = jnp.bfloat16
OFFS = range(-2, 4)
CHUNK = 256

NN = (((1,), (0,)), ((), ()))
NT = (((1,), (1,)), ((), ()))
TN = (((0,), (0,)), ((), ()))


def mm(lhs, rhs, dims):
    return lax.dot_general(lhs, rhs, dims, preferred_element_type=F32)


def block_weights(start, total, rows):
    i = lax.broadcasted_iota(jnp.int32, (1, rows), 1)
    even = (i % 2) == 0
    inside = {o: (start + 2 * i + o >= 0) & (start + 2 * i + o < total) for o in OFFS}
    table = []
    for b in range(4):
        for p in range(2):
            row = {}
            for o in OFFS:
                if b == 0:
                    if o == p:
                        row[o] = jnp.where(inside[o], 1.0, 0.0)
                elif b == 1:
                    if o in (0, 1):
                        row[o] = jnp.where(inside[o], 0.5, 0.0)
                elif b == 3:
                    if o in (0, 1):
                        row[o] = jnp.where(inside[o], 0.25, 0.0)
                    else:
                        row[o] = jnp.where(inside[o] & (even if o > 1 else ~even), 0.25, 0.0)
                else:
                    d = o - p
                    if -2 <= d <= 2:
                        r = (start + 2 * i + p) % 3
                        row[o] = jnp.where(inside[o] & (r >= -d) & (r <= 2 - d), 1.0 / 3.0, 0.0)
            table.append(row)
    return table


def spread(idm, rows_of, tap):
    rows = idm.shape[1]
    v = lax.broadcasted_iota(jnp.int32, (256, rows), 0)
    acc = None
    for o in OFFS:
        at = o + tap + 2
        term = jnp.where(idm[at : at + 1, :] == v, rows_of[o], 0.0)
        acc = term if acc is None else acc + term
    return acc


def forward_kernel(
    pos_ref, idm_ref, p_ref, table_ref, cw_ref, gain_ref, wq_ref, g_ref,
    pooled_ref, ng_ref, wt_ref, sums_ref, rows_ref, grads_ref,
    wh, wl, r1, r2, sq, rd,
):
    start, limit, total = pos_ref[0], pos_ref[1], pos_ref[2]
    rows = idm_ref.shape[1]
    chans = table_ref.shape[1]
    idm = idm_ref[...]
    v = lax.broadcasted_iota(jnp.int32, (256, rows), 0)
    p = p_ref[...]
    hi = p.astype(BF16)
    rest = p - hi.astype(F32)
    mid = rest.astype(BF16)
    low = (rest - mid.astype(F32)).astype(BF16)
    p3 = jnp.concatenate([hi.astype(F32), mid.astype(F32), low.astype(F32)], axis=0).astype(BF16)
    picks = []
    for j in range(8):
        hot = jnp.where(idm[j : j + 1, :] == v, 1.0, 0.0).astype(BF16)
        g = mm(p3, hot, NN)
        picks.append(g[0:8] + g[8:16] + g[16:24])
    s = {o: picks[o + 2][0:1] + picks[o + 3][1:2] + picks[o + 4][2:3] for o in OFFS}
    weights = block_weights(start, total, rows)
    expo = []
    for row in weights:
        score = None
        for o in row:
            score = row[o] * s[o] if score is None else score + row[o] * s[o]
        expo.append(jnp.exp(score))
    probs = []
    for n in range(8):
        whole = expo[n % 2] + expo[2 + n % 2] + expo[4 + n % 2] + expo[6 + n % 2]
        probs.append(expo[n] / whole)
    a = {}
    for o in OFFS:
        acc = None
        for n in range(8):
            if o in weights[n]:
                term = probs[n] * weights[n][o]
                acc = term if acc is None else acc + term
        a[o] = 0.5 * acc
    rows_ref[...] = jnp.concatenate(probs, axis=0)
    for k in range(3):
        w = spread(idm, a, k)
        wt_ref[k] = w.astype(BF16)
        wf = w.T
        top = wf.astype(BF16)
        wh[k] = top
        wl[k] = (wf - top.astype(F32)).astype(BF16)
    keep = (start + 2 * lax.broadcasted_iota(jnp.int32, g_ref.shape, 0)) < limit
    grads_ref[...] = jnp.where(keep, g_ref[...].astype(F32), 0.0).astype(BF16)
    r1[...] = jnp.zeros_like(r1)
    r2[...] = jnp.zeros_like(r2)
    sq[...] = jnp.zeros_like(sq)
    rd[...] = jnp.zeros_like(rd)

    def step(c, carry):
        at = pl.ds(pl.multiple_of(c * CHUNK, CHUNK), CHUNK)
        tab = table_ref[:, at]
        cw = cw_ref[:, at]
        ng = mm(grads_ref[...], wq_ref[at, :], NT)
        pooled = None
        for k in range(3):
            part = cw[k : k + 1] * (mm(wh[k], tab, NN) + mm(wl[k], tab, NN))
            pooled = part if pooled is None else pooled + part
        pooled_ref[:, at] = pooled
        ng_ref[:, at] = ng
        gained = ng * gain_ref[:, at]
        square = pooled * pooled
        inner = pooled * gained
        sq[...] += square[:, 0:128] + square[:, 128:256]
        rd[...] += inner[:, 0:128] + inner[:, 128:256]
        gb = gained.astype(BF16)
        pb = pooled.astype(BF16)
        for k in range(3):
            tk = (tab.astype(F32) * cw[k : k + 1]).astype(BF16)
            r1[k] += mm(tk, gb, NT)
            r2[k] += mm(tk, pb, NT)
        return carry

    lax.fori_loop(0, chans // CHUNK, step, 0)
    out = []
    for r in (r1, r2):
        for o in OFFS:
            acc = None
            for k in range(3):
                at = o + k + 2
                term = jnp.where(idm[at : at + 1, :] == v, r[k], 0.0)
                acc = term if acc is None else acc + term
            out.append(jnp.sum(acc, axis=0, keepdims=True))
    out.append(jnp.sum(sq[...].T, axis=0, keepdims=True))
    out.append(jnp.sum(rd[...].T, axis=0, keepdims=True))
    out.append(jnp.zeros((2, rows), F32))
    sums_ref[...] = jnp.concatenate(out, axis=0)


def backward_kernel(
    pos_ref, idm_ref, sums_ref, rows_ref, table_ref, cw_ref, sw_ref, gain_ref,
    pooled_ref, ng_ref, wt_ref, grads_ref,
    query_ref, tab_ref, small_ref,
):
    start, total = pos_ref[0], pos_ref[2]
    rows = idm_ref.shape[1]
    chans = table_ref.shape[1]
    idm = idm_ref[...]
    sums = sums_ref[...]
    probs = rows_ref[...]
    square, inner = sums[12:13], sums[13:14]
    scale = lax.rsqrt(square / D + EPS)
    pull = scale * scale * scale * (inner / D)
    q = {o: scale * sums[o + 2 : o + 3] - pull * sums[o + 8 : o + 9] for o in OFFS}
    weights = block_weights(start, total, rows)
    pgrad = []
    for row in weights:
        acc = None
        for o in row:
            acc = row[o] * q[o] if acc is None else acc + row[o] * q[o]
        pgrad.append(0.5 * acc)
    sgrad = []
    for n in range(8):
        mean = None
        for m in range(n % 2, 8, 2):
            term = probs[m : m + 1] * pgrad[m]
            mean = term if mean is None else mean + term
        sgrad.append(probs[n : n + 1] * (pgrad[n] - mean))
    ds = {}
    for o in OFFS:
        acc = None
        for n in range(8):
            if o in weights[n]:
                term = sgrad[n] * weights[n][o]
                acc = term if acc is None else acc + term
        ds[o] = acc
    hist = [jnp.sum(spread(idm, ds, k), axis=1, keepdims=True) for k in range(3)]
    cols = jnp.concatenate([scale, pull, jnp.zeros((6, rows), F32)], axis=0).T
    scale_c, pull_c = cols[:, 0:1], cols[:, 1:2]

    for c in range(chans // CHUNK):
        at = pl.ds(c * CHUNK, CHUNK)
        tab = table_ref[:, at].astype(F32)
        cw = cw_ref[:, at]
        sw = sw_ref[:, at]
        gain = gain_ref[:, at]
        ps = pooled_ref[:, at] * scale_c
        ng = ng_ref[:, at]
        gain_term = jnp.sum(ng * ps, axis=0, keepdims=True)
        normed = (ps * gain).astype(BF16)
        query_ref[at, :] = mm(normed, grads_ref[...], TN).astype(query_ref.dtype)
        pg = (ng * gain * scale_c - pull_c * pooled_ref[:, at]).astype(BF16)
        total_t = None
        outs = []
        score = None
        for k in range(3):
            full = mm(wt_ref[k], pg, NN) + hist[k] * sw
            term = cw[k : k + 1] * full
            total_t = term if total_t is None else total_t + term
            outs.append(jnp.sum(full * tab, axis=0, keepdims=True))
            term = cw[k : k + 1] * jnp.sum(hist[k] * tab, axis=0, keepdims=True)
            score = term if score is None else score + term
        tab_ref[:, at] = total_t.astype(tab_ref.dtype)
        small_ref[:, at] = jnp.concatenate(
            outs + [score, gain_term, jnp.zeros((3, CHUNK), F32)], axis=0
        )


def body(
    byte_ids, pad_lengths, table, conv_weight, score_weight, norm_gain, query_weight, query_grad
):
    ids = byte_ids[0]
    count = ids.shape[0]
    rows = count // 2
    vocab, chans = table.shape
    width = query_grad.shape[2]
    n_seq = lax.axis_size("seq")
    total = count * n_seq
    start = lax.axis_index("seq") * count
    limit = total - pad_lengths[0]
    ends = n_seq - 1
    up = [(i, i + 1) for i in range(ends)]
    down = [(i + 1, i) for i in range(ends)]
    ids_ext = jnp.concatenate(
        [lax.ppermute(ids[count - 3 :], "seq", up), ids, lax.ppermute(ids[:3], "seq", down)]
    )
    pos_e = start + jnp.arange(-3, count + 3, dtype=jnp.int32)
    ids_ext = jnp.where((pos_e >= 0) & (pos_e < limit), ids_ext, -1)
    halves = ids_ext.reshape(rows + 3, 2).T
    idm = jnp.stack([halves[j % 2, j // 2 : j // 2 + rows] for j in range(8)])
    pos = jnp.stack([start, limit, jnp.full_like(start, total)]).astype(jnp.int32)

    part = jnp.dot(
        conv_weight * score_weight, table.astype(F32).T, precision=lax.Precision.HIGHEST
    )
    p = jnp.pad(lax.psum(part, "tensor"), ((0, 5), (0, 0)))

    vm = pl.BlockSpec(memory_space=pltpu.VMEM)
    sm = pl.BlockSpec(memory_space=pltpu.SMEM)
    sw = score_weight[None, :]
    gain = norm_gain[None, :]
    pooled, ng, wt, sums, probs, grads = pl.pallas_call(
        forward_kernel,
        out_shape=(
            jax.ShapeDtypeStruct((rows, chans), F32),
            jax.ShapeDtypeStruct((rows, chans), F32),
            jax.ShapeDtypeStruct((3, vocab, rows), BF16),
            jax.ShapeDtypeStruct((16, rows), F32),
            jax.ShapeDtypeStruct((8, rows), F32),
            jax.ShapeDtypeStruct((rows, width), BF16),
        ),
        in_specs=[sm] + [vm] * 7,
        out_specs=(vm,) * 6,
        scratch_shapes=[
            pltpu.VMEM((3, rows, vocab), BF16),
            pltpu.VMEM((3, rows, vocab), BF16),
            pltpu.VMEM((3, vocab, rows), F32),
            pltpu.VMEM((3, vocab, rows), F32),
            pltpu.VMEM((rows, 128), F32),
            pltpu.VMEM((rows, 128), F32),
        ],
        name="forward",
    )(pos, idm, p, table, conv_weight, gain, query_weight, query_grad[0])
    sums = lax.psum(sums, "tensor")
    query, tab, small = pl.pallas_call(
        backward_kernel,
        out_shape=(
            jax.ShapeDtypeStruct((chans, width), BF16),
            jax.ShapeDtypeStruct((vocab, chans), BF16),
            jax.ShapeDtypeStruct((8, chans), F32),
        ),
        in_specs=[sm] + [vm] * 11,
        out_specs=(vm,) * 3,
        name="backward",
    )(pos, idm, sums, probs, table, conv_weight, sw, gain, pooled, ng, wt, grads)

    share = lax.psum_scatter(query, "seq", scatter_dimension=1, tiled=True)
    query_out = lax.psum(share, "dp")
    tab_out = lax.psum(tab, ("dp", "seq"))
    small_out = lax.psum(small, ("dp", "seq"))
    return (tab_out, small_out[0:3], small_out[3], small_out[4], query_out)


MESH = pl.DeviceIdType.MESH
BLOCK = 16
TILE = 256


def stacked(value):
    hi = value.astype(BF16)
    rest = value - hi.astype(F32)
    mid = rest.astype(BF16)
    low = (rest - mid.astype(F32)).astype(BF16)
    return jnp.concatenate([hi.astype(F32), mid.astype(F32), low.astype(F32)], axis=0).astype(BF16)


def packed_weights(start, total, rows):
    n = lax.broadcasted_iota(jnp.int32, (8, rows), 0)
    i = lax.broadcasted_iota(jnp.int32, (8, rows), 1)
    b, p = n // 2, n % 2
    even = (i % 2) == 0
    r = (start + 2 * i + p) % 3
    table = []
    for o in OFFS:
        at = start + 2 * i + o
        inside = (at >= 0) & (at < total)
        d = o - p
        near = (d >= -2) & (d <= 2) & (r >= -d) & (r <= 2 - d)
        w = jnp.where((b == 2) & near, 1.0 / 3.0, 0.0)
        w = jnp.where((b == 0) & (p == o), 1.0, w)
        if o in (0, 1):
            w = jnp.where(b == 1, 0.5, w)
            w = jnp.where(b == 3, 0.25, w)
        else:
            w = jnp.where((b == 3) & (even if o > 1 else ~even), 0.25, w)
        table.append(jnp.where(inside, w, 0.0))
    return table


def over_blocks(value):
    return value + pltpu.roll(value, 2, 0) + pltpu.roll(value, 4, 0) + pltpu.roll(value, 6, 0)


def fused_kernel(
    pad_ref, ids_ref, table_ref, cw_ref, sw_ref, gain_ref, wq_hbm, g_hbm,
    tab_ref, small_ref, query_ref,
    wq, g, tk, wt, wcat, pooled, ng, gb, pb, q, idm_s, w8_s, probs_s, hist, rr, lanes,
    p_own, p_in, halo, x1_own, x1_in, x2_own, x2_in,
    r1, s2, r2, zb, zr, own_z, tb, tr, ts, tz, sm, sz, sd,
    in_sem, s_halo, r_halo, s_core, r_core, s_p1, r_p1, s_p2, r_p2, s_z, r_z, s_ag, r_ag,
    s_t, r_t, s_sm, r_sm,
):
    d, s, t = lax.axis_index("dp"), lax.axis_index("seq"), lax.axis_index("tensor")
    n_seq = lax.axis_size("seq")
    x, y = d % 2, d // 2
    x_near = y * 2 + (1 - x)
    y_near = (1 - y) * 2 + x
    corner = (1 - y) * 2 + (1 - x)
    dp_peers = (x_near, y_near, corner)
    seq_peers = [(s + e) % n_seq for e in range(1, n_seq)]
    count = ids_ref.shape[1]
    rows = count // 2
    vocab, chans = table_ref.shape
    width = g.shape[1]
    total = count * n_seq
    start = s * count
    limit = total - pad_ref[0]
    half, quarter, eighth = chans // 2, chans // 4, chans // 8
    cols = width // n_seq
    t_dp, t_seq = vocab // 4, vocab // 4 // n_seq

    def remote(src, dst, send, recv, to):
        return pltpu.make_async_remote_copy(
            src_ref=src, dst_ref=dst, send_sem=send, recv_sem=recv,
            device_id=to, device_id_type=MESH,
        )

    take_g = pltpu.make_async_copy(g_hbm, g, in_sem.at[0])
    take_w = pltpu.make_async_copy(wq_hbm, wq, in_sem.at[1])
    take_g.start()
    take_w.start()

    barrier = pltpu.get_barrier_semaphore()
    peers = [(dd, s, t) for dd in dp_peers] + [(d, ss, t) for ss in seq_peers] + [(d, s, 1 - t)]
    for peer in peers:
        pl.semaphore_signal(barrier, inc=1, device_id=peer, device_id_type=MESH)

    cs = cw_ref[...] * sw_ref[...]
    p_own[...] = sum_parts(mm(stacked(pad8(cs)), table_ref[...], NT))
    pl.semaphore_wait(barrier, len(peers))

    put_p = remote(p_own, p_in, s_core.at[0], r_core.at[0], (d, s, 1 - t))
    put_p.start()
    to_left = remote(
        ids_ref.at[:, pl.ds(0, 128)], halo.at[1], s_halo.at[0], r_halo.at[1],
        (d, jnp.maximum(s - 1, 0), t),
    )
    to_right = remote(
        ids_ref.at[:, pl.ds(count - 128, 128)], halo.at[0], s_halo.at[1], r_halo.at[0],
        (d, jnp.minimum(s + 1, n_seq - 1), t),
    )

    @pl.when(s > 0)
    def _():
        to_left.start()

    @pl.when(s < n_seq - 1)
    def _():
        to_right.start()

    @pl.when(s == 0)
    def _():
        halo[0] = jnp.zeros((1, 128), jnp.int32)

    @pl.when(s == n_seq - 1)
    def _():
        halo[1] = jnp.zeros((1, 128), jnp.int32)

    for k in range(3):
        def spell(c, carry, k=k):
            at = pl.ds(pl.multiple_of(c * TILE, TILE), TILE)
            tk[k * vocab : (k + 1) * vocab, at] = (
                table_ref[:, at].astype(F32) * cw_ref[k : k + 1, at]
            ).astype(BF16)
            return carry

        lax.fori_loop(0, chans // TILE, spell, 0)
    take_g.wait()

    def mask(c, carry):
        at = pl.ds(pl.multiple_of(c * 64, 64), 64)
        i = lax.broadcasted_iota(jnp.int32, (64, width), 0) + c * 64
        g[at, :] = jnp.where(start + 2 * i < limit, g[at, :].astype(F32), 0.0).astype(BF16)
        return carry

    lax.fori_loop(0, rows // 64, mask, 0)

    @pl.when(s > 0)
    def _():
        to_right.wait_recv()
        to_left.wait_send()

    @pl.when(s < n_seq - 1)
    def _():
        to_left.wait_recv()
        to_right.wait_send()

    put_p.wait()

    wide = rows + 128
    line = jnp.concatenate([halo[0], ids_ref[...], halo[1]], axis=1).astype(F32)
    pieces = wide // 128
    line = jnp.concatenate(
        [line[:, n * 256 : (n + 1) * 256] for n in range(pieces)]
        + [jnp.zeros((8 - pieces % 8, 256), F32)] * (pieces % 8 > 0),
        axis=0,
    )
    r = lax.broadcasted_iota(jnp.int32, (256, 256), 0)
    c = lax.broadcasted_iota(jnp.int32, (256, 256), 1)
    sift = jnp.where(r == jnp.where(c < 128, 2 * c, 2 * c - 255), 1.0, 0.0).astype(BF16)
    sifted = mm(line.astype(BF16), sift, NN)
    cat = jnp.concatenate(
        [
            jnp.concatenate([sifted[n : n + 1, p * 128 : (p + 1) * 128] for n in range(pieces)], axis=1)
            for p in range(2)
        ]
        + [jnp.zeros((6, wide), F32)],
        axis=0,
    ).astype(jnp.int32)
    lane = lax.broadcasted_iota(jnp.int32, cat.shape, 1)
    row = lax.broadcasted_iota(jnp.int32, cat.shape, 0)
    at_byte = start + 2 * (lane - 64) + row
    cat = jnp.where((at_byte >= 0) & (at_byte < limit) & (row < 2), cat, -1)

    def shifted(value, n):
        return pltpu.roll(value, wide - 64 - n, 1)[:, 0:rows]

    p3 = stacked(p_own[...] + p_in[...])
    v_wide = lax.broadcasted_iota(jnp.int32, (vocab, wide), 0)

    def picked(line):
        hot = jnp.where(line == v_wide, 1.0, 0.0).astype(BF16)
        return sum_parts(mm(p3, hot, NN))

    even, odd = picked(cat[0:1]), picked(cat[1:2])
    sc_even = pltpu.roll(odd, 1, 1)[0:1] + even[1:2] + odd[2:3]
    sc_odd = even[0:1] + odd[1:2] + pltpu.roll(even, wide - 1, 1)[2:3]
    se = jnp.broadcast_to(sc_even, (8, wide))
    so = jnp.broadcast_to(sc_odd, (8, wide))
    scores = [shifted(value, n) for n in (-1, 0, 1) for value in (se, so)]
    w8 = packed_weights(start, total, rows)
    score = w8[0] * scores[0]
    for n in range(1, 6):
        score = score + w8[n] * scores[n]
    expo = jnp.exp(score)
    probs = expo / over_blocks(expo)
    a = [0.5 * jnp.sum(probs * w, axis=0, keepdims=True) for w in w8]
    probs_s[...] = probs
    for n in range(6):
        w8_s[n] = w8[n]
    near = [shifted(cat, n) for n in (-2, -1, 0, 1, 2)]
    idm_s[...] = jnp.concatenate(
        [near[0][1:2], near[1][0:2], near[2][0:2], near[3][0:2], near[4][0:1]], axis=0
    )

    def spread_in(n, carry):
        at = pl.ds(pl.multiple_of(n * BLOCK, BLOCK), BLOCK)
        v = lax.broadcasted_iota(jnp.int32, (BLOCK, rows), 0) + n * BLOCK
        hits = [idm_s[j : j + 1, :] == v for j in range(8)]
        for k in range(3):
            acc = jnp.where(hits[k], a[0], 0.0)
            for o in range(1, 6):
                acc = acc + jnp.where(hits[o + k], a[o], 0.0)
            wt[k, at, :] = acc.astype(BF16)
        return carry

    lax.fori_loop(0, vocab // BLOCK, spread_in, 0)
    for k in range(3):
        wcat[:, k * vocab : (k + 1) * vocab] = wt[k].astype(F32).T.astype(BF16)

    lanes[...] = jnp.zeros_like(lanes)

    def pool(c, carry):
        at = pl.ds(pl.multiple_of(c * TILE, TILE), TILE)
        part = mm(wcat[...], tk[:, at], NN)
        pooled[:, at] = part
        pb[:, at] = part.astype(BF16)
        square = part * part
        lanes[...] += square[:, 0:128] + square[:, 128:256]
        return carry

    lax.fori_loop(0, chans // TILE, pool, 0)
    x1_own[...] = jnp.broadcast_to(jnp.sum(lanes[...].T, axis=0, keepdims=True), (8, rows))
    put_1 = remote(x1_own, x1_in, s_core.at[1], r_core.at[1], (d, s, 1 - t))
    put_1.start()
    put_1.wait()
    scale = lax.rsqrt((x1_own[...] + x1_in[...]) / D + EPS)
    scale_c = scale.T[:, 0:1]

    def product(at_row):
        at = pl.ds(pl.multiple_of(at_row, 128), quarter)
        normed = (pooled[:, at] * scale_c * gain_ref[:, at]).astype(BF16)
        q[at, :] = mm(normed, g[...], TN).astype(BF16)

    bit1, bit2 = (x, y), (y, x)
    near1 = ((x_near, s, t), (y_near, s, t))
    near2 = ((y_near, s, t), (x_near, s, t))

    def q_rows(h, first, second):
        return pl.ds(pl.multiple_of(h * half + first * quarter + second * eighth, eighth), eighth)

    p1 = {}
    for h in range(2):
        product(h * half + (1 - bit1[h]) * quarter)
        for part in range(2):
            second = bit2[h] if part else 1 - bit2[h]
            p1[h, part] = remote(
                q.at[q_rows(h, 1 - bit1[h], second)], r1.at[h, part],
                s_p1.at[h, part], r_p1.at[h, part], near1[h],
            )
            p1[h, part].start()
    for h in range(2):
        product(h * half + bit1[h] * quarter)

    take_w.wait()
    lanes[...] = jnp.zeros_like(lanes)

    def pull_back(c, carry):
        at = pl.ds(pl.multiple_of(c * TILE, TILE), TILE)
        part = mm(g[...], wq[at, :], NT)
        ng[:, at] = part
        gained = part * gain_ref[:, at]
        gb[:, at] = gained.astype(BF16)
        inner = pooled[:, at] * gained
        lanes[...] += inner[:, 0:128] + inner[:, 128:256]
        return carry

    lax.fori_loop(0, chans // TILE, pull_back, 0)
    found = []
    for source in (gb, pb):
        sums = tuple(jnp.zeros((8, rows), F32) for o in range(6))
        for k in range(3):
            rr[...] = mm(tk[k * vocab : (k + 1) * vocab, :], source[...], NT)

            def select(n, accs, k=k):
                line = rr[pl.ds(pl.multiple_of(n * 8, 8), 8), :]
                v = lax.broadcasted_iota(jnp.int32, (8, rows), 0) + n * 8
                return tuple(
                    accs[o] + jnp.where(idm_s[o + k : o + k + 1, :] == v, line, 0.0)
                    for o in range(6)
                )

            sums = lax.fori_loop(0, vocab // 8, select, sums)
        found += [jnp.sum(acc, axis=0, keepdims=True) for acc in sums]
    found.append(jnp.sum(lanes[...].T, axis=0, keepdims=True))
    found.append(jnp.zeros((3, rows), F32))
    x2_own[...] = jnp.concatenate(found, axis=0)
    put_2 = remote(x2_own, x2_in, s_core.at[2], r_core.at[2], (d, s, 1 - t))
    put_2.start()

    p2 = {}
    for h in range(2):
        p1[h, 0].wait_recv()
        rows_h = q_rows(h, bit1[h], 1 - bit2[h])
        s2[h] = (q[rows_h, :].astype(F32) + r1[h, 0].astype(F32)).astype(BF16)
        for e in range(n_seq):
            at = pl.ds(pl.multiple_of((s + e + 1) % n_seq * cols, 128), cols)
            p2[h, e] = remote(
                s2.at[h, :, at], r2.at[h, :, at], s_p2.at[h, e], r_p2.at[h, e], near2[h]
            )
            p2[h, e].start()

    put_2.wait()
    sums = x2_own[...] + x2_in[...]
    pull = scale[0:1] * scale[0:1] * scale[0:1] * (sums[12:13] / D)
    w8 = [w8_s[n] for n in range(6)]
    probs = probs_s[...]
    pgrad = None
    for o in range(6):
        term = w8[o] * (scale[0:1] * sums[o : o + 1] - pull * sums[o + 6 : o + 7])
        pgrad = term if pgrad is None else pgrad + term
    pgrad = 0.5 * pgrad
    sgrad = probs * (pgrad - over_blocks(probs * pgrad))
    ds = [jnp.sum(sgrad * w, axis=0, keepdims=True) for w in w8]

    def count_in(n, carry):
        at = pl.ds(pl.multiple_of(n * BLOCK, BLOCK), BLOCK)
        v = lax.broadcasted_iota(jnp.int32, (BLOCK, rows), 0) + n * BLOCK
        hits = [idm_s[j : j + 1, :] == v for j in range(8)]
        for k in range(3):
            acc = jnp.where(hits[k], ds[0], 0.0)
            for o in range(1, 6):
                acc = acc + jnp.where(hits[o + k], ds[o], 0.0)
            hist[k, at, :] = jnp.broadcast_to(jnp.sum(acc, axis=1, keepdims=True), (BLOCK, 128))
        return carry

    lax.fori_loop(0, vocab // BLOCK, count_in, 0)
    pull_c = jnp.broadcast_to(pull, (8, rows)).T[:, 0:1]

    def table_step(c, carry):
        at = pl.ds(pl.multiple_of(c * TILE, TILE), TILE)
        tab = table_ref[:, at].astype(F32)
        cw, sw, gain = cw_ref[:, at], sw_ref[:, at], gain_ref[:, at]
        ngc, pc = ng[:, at], pooled[:, at]
        scaled = ngc * scale_c
        gain_term = jnp.sum(scaled * pc, axis=0, keepdims=True)
        pg = (scaled * gain - pull_c * pc).astype(BF16)
        whole, outs, score = None, [], None
        for k in range(3):
            hist_k = hist[k][:, 0:1]
            full = mm(wt[k], pg, NN) + hist_k * sw
            term = cw[k : k + 1] * full
            whole = term if whole is None else whole + term
            outs.append(jnp.sum(full * tab, axis=0, keepdims=True))
            term = cw[k : k + 1] * jnp.sum(hist_k * tab, axis=0, keepdims=True)
            score = term if score is None else score + term
        tb[:, at] = whole.astype(BF16)
        sm[:, at] = jnp.concatenate(outs + [score, gain_term, jnp.zeros((3, TILE), F32)], axis=0)
        return carry

    lax.fori_loop(0, chans // TILE, table_step, 0)

    t_rs, sm_z = [], []
    for e, dd in enumerate(dp_peers):
        block = tb.at[pl.ds(pl.multiple_of(dd * t_dp, t_dp), t_dp)]
        t_rs.append(remote(block, tr.at[d], s_t.at[e], r_t.at[e], (dd, s, t)))
        t_rs[-1].start()
    for e, ss in enumerate(seq_peers):
        sm_z.append(remote(sm, sz.at[s], s_sm.at[e], r_sm.at[e], (d, ss, t)))
        sm_z[-1].start()
    tr[d] = tb[pl.ds(pl.multiple_of(d * t_dp, t_dp), t_dp), :]
    sz[s] = sm[...]

    for h in range(2):
        p1[h, 1].wait_recv()
    q_z = {}
    for e in range(n_seq):
        j = (s + e + 1) % n_seq
        at = pl.ds(pl.multiple_of(j * cols, 128), cols)
        for h in range(2):
            p2[h, e].wait_recv()
            rows_h = q_rows(h, bit1[h], bit2[h])
            block = q[rows_h, at].astype(F32) + r1[h, 1, :, at].astype(F32)
            block = block + r2[h, :, at].astype(F32)
            if e < n_seq - 1:
                zb[h, e] = block.astype(BF16)
                q_z[h, e] = remote(
                    zb.at[h, e], zr.at[h, e], s_z.at[h, e], r_z.at[h, e], (d, j, t)
                )
                q_z[h, e].start()
            else:
                own_z[h] = block

    for copy in t_rs:
        copy.wait_recv()
    acc = tr[0].astype(F32)
    for n in range(1, 4):
        acc = acc + tr[n].astype(F32)
    ts[...] = acc.astype(BF16)
    t_z = []
    for e, ss in enumerate(seq_peers):
        block = ts.at[pl.ds(pl.multiple_of(ss * t_seq, t_seq), t_seq)]
        t_z.append(remote(block, tz.at[s], s_t.at[3 + e], r_t.at[3 + e], (d, ss, t)))
        t_z[-1].start()
    tz[s] = ts[pl.ds(pl.multiple_of(s * t_seq, t_seq), t_seq), :]

    for copy in sm_z:
        copy.wait_recv()
    acc = sz[0]
    for n in range(1, n_seq):
        acc = acc + sz[n]
    sd[d] = acc
    sm_d = []
    for e, dd in enumerate(dp_peers):
        sm_d.append(remote(sd.at[d], sd.at[d], s_sm.at[3 + e], r_sm.at[3 + e], (dd, s, t)))
        sm_d[-1].start()

    q_ag = []
    for h in range(2):
        block = own_z[h]
        for e in range(n_seq - 1):
            q_z[h, e].wait_recv()
            block = block + zr[h, e].astype(F32)
        mine = q_rows(h, bit1[h], bit2[h])
        query_ref[mine, :] = block.astype(BF16)
        for e, dd in enumerate(dp_peers):
            q_ag.append(
                remote(
                    query_ref.at[mine], query_ref.at[mine], s_ag.at[h, e], r_ag.at[h, e], (dd, s, t)
                )
            )
            q_ag[-1].start()

    for copy in t_z:
        copy.wait_recv()
    acc = tz[0].astype(F32)
    for n in range(1, n_seq):
        acc = acc + tz[n].astype(F32)
    mine = pl.ds(pl.multiple_of(d * t_dp + s * t_seq, t_seq), t_seq)
    tab_ref[mine, :] = acc.astype(BF16)
    t_back = []
    for e, ss in enumerate(seq_peers):
        t_back.append(
            remote(tab_ref.at[mine], tab_ref.at[mine], s_t.at[6 + e], r_t.at[6 + e], (d, ss, t))
        )
        t_back[-1].start()
    for copy in t_back:
        copy.wait_recv()
    t_ag = []
    mine = pl.ds(pl.multiple_of(d * t_dp, t_dp), t_dp)
    for e, dd in enumerate(dp_peers):
        t_ag.append(
            remote(tab_ref.at[mine], tab_ref.at[mine], s_t.at[9 + e], r_t.at[9 + e], (dd, s, t))
        )
        t_ag[-1].start()

    for copy in sm_d:
        copy.wait_recv()
    small_ref[...] = (sd[0] + sd[1]) + (sd[2] + sd[3])
    for copy in q_ag + t_ag:
        copy.wait_recv()
    started = list(p1.values()) + list(p2.values()) + list(q_z.values())
    for copy in started + t_rs + t_z + t_back + t_ag + sm_z + sm_d + q_ag:
        copy.wait_send()


def finish_kernel(tab_ref, small_ref, query_ref, tab_out, conv_out, score_out, gain_out, query_out):
    conv_out[...] = small_ref[0:3]
    score_out[...] = small_ref[3:4]
    gain_out[...] = small_ref[4:5]
    tab_out[...] = tab_ref[...]
    query_out[...] = query_ref[...]


def pad8(value):
    return jnp.concatenate([value, jnp.zeros((8 - value.shape[0], value.shape[1]), F32)], axis=0)


def sum_parts(value):
    return value[0:8] + value[8:16] + value[16:24]


def fused_body(
    byte_ids, pad_lengths, table, conv_weight, score_weight, norm_gain, query_weight, query_grad
):
    count = byte_ids.shape[1]
    rows = count // 2
    vocab, chans = table.shape
    width = query_grad.shape[2]
    n_seq = lax.axis_size("seq")
    cols = width // n_seq
    part, t_dp = chans // 8, vocab // 4
    vm = pl.BlockSpec(memory_space=pltpu.VMEM)
    sm = pl.BlockSpec(memory_space=pltpu.SMEM)
    hbm = pl.BlockSpec(memory_space=pl.ANY)
    V, DMA = pltpu.VMEM, pltpu.SemaphoreType.DMA
    tab, small, query = pl.pallas_call(
        fused_kernel,
        out_shape=(
            jax.ShapeDtypeStruct((vocab, chans), BF16),
            jax.ShapeDtypeStruct((8, chans), F32),
            jax.ShapeDtypeStruct((chans, cols), BF16),
        ),
        in_specs=[sm] + [vm] * 5 + [hbm] * 2,
        out_specs=(vm,) * 3,
        scratch_shapes=[
            V((chans, width), BF16), V((rows, width), BF16), V((3 * vocab, chans), BF16),
            V((3, vocab, rows), BF16), V((rows, 3 * vocab), BF16), V((rows, chans), F32),
            V((rows, chans), F32), V((rows, chans), BF16), V((rows, chans), BF16),
            V((chans, width), BF16), V((8, rows), jnp.int32), V((6, 8, rows), F32),
            V((8, rows), F32), V((3, vocab, 128), F32), V((vocab, rows), F32), V((rows, 128), F32),
            V((8, vocab), F32), V((8, vocab), F32), V((2, 1, 128), jnp.int32),
            V((8, rows), F32), V((8, rows), F32), V((16, rows), F32), V((16, rows), F32),
            V((2, 2, part, width), BF16), V((2, part, width), BF16), V((2, part, width), BF16),
            V((2, n_seq - 1, part, cols), BF16), V((2, n_seq - 1, part, cols), BF16),
            V((2, part, cols), F32), V((vocab, chans), BF16), V((4, t_dp, chans), BF16),
            V((t_dp, chans), BF16), V((n_seq, t_dp // n_seq, chans), BF16),
            V((8, chans), F32), V((n_seq, 8, chans), F32), V((4, 8, chans), F32),
            DMA((2,)), DMA((2,)), DMA((2,)), DMA((3,)), DMA((3,)),
            DMA((2, 2)), DMA((2, 2)), DMA((2, n_seq)), DMA((2, n_seq)),
            DMA((2, n_seq - 1)), DMA((2, n_seq - 1)), DMA((2, 3)), DMA((2, 3)),
            DMA((12,)), DMA((12,)), DMA((6,)), DMA((6,)),
        ],
        compiler_params=pltpu.CompilerParams(collective_id=0, has_side_effects=True),
        name="fused",
    )(
        pad_lengths, byte_ids, table, conv_weight, score_weight[None, :], norm_gain[None, :],
        query_weight, query_grad[0],
    )
    return pl.pallas_call(
        finish_kernel,
        out_shape=(
            jax.ShapeDtypeStruct((vocab, chans), BF16),
            jax.ShapeDtypeStruct((3, chans), F32),
            jax.ShapeDtypeStruct((1, chans), F32),
            jax.ShapeDtypeStruct((1, chans), F32),
            jax.ShapeDtypeStruct((chans, cols), BF16),
        ),
        in_specs=[vm] * 3,
        out_specs=(vm,) * 5,
        name="finish",
    )(tab, small, query)


def fused_outer(*args):
    tab, conv, score, gain, query = fused_body(*args)
    return (tab, conv, score.reshape(-1), gain.reshape(-1), query)


def fits(mesh):
    return mesh.shape["dp"] == 4 and mesh.shape["seq"] == 4 and mesh.shape["tensor"] == 2


def solution(mesh):
    return jax.shard_map(
        fused_outer if fits(mesh) else body,
        mesh=mesh,
        in_specs=(
            P("dp", "seq"),
            P("dp"),
            P(None, "tensor"),
            P(None, "tensor"),
            P("tensor"),
            P("tensor"),
            P("tensor", None),
            P("dp", "seq", None),
        ),
        out_specs=(
            P(None, "tensor"),
            P(None, "tensor"),
            P("tensor"),
            P("tensor"),
            P("tensor", "seq"),
        ),
        check_vma=False,
    )
```

```python
import functools

import jax
import jax.numpy as jnp
from jax import lax
from jax.experimental import pallas as pl
from jax.experimental.pallas import tpu as pltpu
from jax.sharding import PartitionSpec as P

D = 2048
EPS = 1e-06
F32 = jnp.float32
BF16 = jnp.bfloat16
OFFS = range(-2, 4)
CHUNK = 256

NN = (((1,), (0,)), ((), ()))
NT = (((1,), (1,)), ((), ()))
TN = (((0,), (0,)), ((), ()))


def mm(lhs, rhs, dims):
    return lax.dot_general(lhs, rhs, dims, preferred_element_type=F32)


def block_weights(start, total, rows):
    i = lax.broadcasted_iota(jnp.int32, (1, rows), 1)
    even = (i % 2) == 0
    inside = {o: (start + 2 * i + o >= 0) & (start + 2 * i + o < total) for o in OFFS}
    table = []
    for b in range(4):
        for p in range(2):
            row = {}
            for o in OFFS:
                if b == 0:
                    if o == p:
                        row[o] = jnp.where(inside[o], 1.0, 0.0)
                elif b == 1:
                    if o in (0, 1):
                        row[o] = jnp.where(inside[o], 0.5, 0.0)
                elif b == 3:
                    if o in (0, 1):
                        row[o] = jnp.where(inside[o], 0.25, 0.0)
                    else:
                        row[o] = jnp.where(inside[o] & (even if o > 1 else ~even), 0.25, 0.0)
                else:
                    d = o - p
                    if -2 <= d <= 2:
                        r = (start + 2 * i + p) % 3
                        row[o] = jnp.where(inside[o] & (r >= -d) & (r <= 2 - d), 1.0 / 3.0, 0.0)
            table.append(row)
    return table


def spread(idm, rows_of, tap):
    rows = idm.shape[1]
    v = lax.broadcasted_iota(jnp.int32, (256, rows), 0)
    acc = None
    for o in OFFS:
        at = o + tap + 2
        term = jnp.where(idm[at : at + 1, :] == v, rows_of[o], 0.0)
        acc = term if acc is None else acc + term
    return acc


def forward_kernel(
    pos_ref, idm_ref, p_ref, table_ref, cw_ref, gain_ref, wq_ref, g_ref,
    pooled_ref, ng_ref, wt_ref, sums_ref, rows_ref, grads_ref,
    wh, wl, r1, r2, sq, rd,
):
    start, limit, total = pos_ref[0], pos_ref[1], pos_ref[2]
    rows = idm_ref.shape[1]
    chans = table_ref.shape[1]
    idm = idm_ref[...]
    v = lax.broadcasted_iota(jnp.int32, (256, rows), 0)
    p = p_ref[...]
    hi = p.astype(BF16)
    rest = p - hi.astype(F32)
    mid = rest.astype(BF16)
    low = (rest - mid.astype(F32)).astype(BF16)
    p3 = jnp.concatenate([hi.astype(F32), mid.astype(F32), low.astype(F32)], axis=0).astype(BF16)
    picks = []
    for j in range(8):
        hot = jnp.where(idm[j : j + 1, :] == v, 1.0, 0.0).astype(BF16)
        g = mm(p3, hot, NN)
        picks.append(g[0:8] + g[8:16] + g[16:24])
    s = {o: picks[o + 2][0:1] + picks[o + 3][1:2] + picks[o + 4][2:3] for o in OFFS}
    weights = block_weights(start, total, rows)
    expo = []
    for row in weights:
        score = None
        for o in row:
            score = row[o] * s[o] if score is None else score + row[o] * s[o]
        expo.append(jnp.exp(score))
    probs = []
    for n in range(8):
        whole = expo[n % 2] + expo[2 + n % 2] + expo[4 + n % 2] + expo[6 + n % 2]
        probs.append(expo[n] / whole)
    a = {}
    for o in OFFS:
        acc = None
        for n in range(8):
            if o in weights[n]:
                term = probs[n] * weights[n][o]
                acc = term if acc is None else acc + term
        a[o] = 0.5 * acc
    rows_ref[...] = jnp.concatenate(probs, axis=0)
    for k in range(3):
        w = spread(idm, a, k)
        wt_ref[k] = w.astype(BF16)
        wf = w.T
        top = wf.astype(BF16)
        wh[k] = top
        wl[k] = (wf - top.astype(F32)).astype(BF16)
    keep = (start + 2 * lax.broadcasted_iota(jnp.int32, g_ref.shape, 0)) < limit
    grads_ref[...] = jnp.where(keep, g_ref[...].astype(F32), 0.0).astype(BF16)
    r1[...] = jnp.zeros_like(r1)
    r2[...] = jnp.zeros_like(r2)
    sq[...] = jnp.zeros_like(sq)
    rd[...] = jnp.zeros_like(rd)

    def step(c, carry):
        at = pl.ds(pl.multiple_of(c * CHUNK, CHUNK), CHUNK)
        tab = table_ref[:, at]
        cw = cw_ref[:, at]
        ng = mm(grads_ref[...], wq_ref[at, :], NT)
        pooled = None
        for k in range(3):
            part = cw[k : k + 1] * (mm(wh[k], tab, NN) + mm(wl[k], tab, NN))
            pooled = part if pooled is None else pooled + part
        pooled_ref[:, at] = pooled
        ng_ref[:, at] = ng
        gained = ng * gain_ref[:, at]
        square = pooled * pooled
        inner = pooled * gained
        sq[...] += square[:, 0:128] + square[:, 128:256]
        rd[...] += inner[:, 0:128] + inner[:, 128:256]
        gb = gained.astype(BF16)
        pb = pooled.astype(BF16)
        for k in range(3):
            tk = (tab.astype(F32) * cw[k : k + 1]).astype(BF16)
            r1[k] += mm(tk, gb, NT)
            r2[k] += mm(tk, pb, NT)
        return carry

    lax.fori_loop(0, chans // CHUNK, step, 0)
    out = []
    for r in (r1, r2):
        for o in OFFS:
            acc = None
            for k in range(3):
                at = o + k + 2
                term = jnp.where(idm[at : at + 1, :] == v, r[k], 0.0)
                acc = term if acc is None else acc + term
            out.append(jnp.sum(acc, axis=0, keepdims=True))
    out.append(jnp.sum(sq[...].T, axis=0, keepdims=True))
    out.append(jnp.sum(rd[...].T, axis=0, keepdims=True))
    out.append(jnp.zeros((2, rows), F32))
    sums_ref[...] = jnp.concatenate(out, axis=0)


def backward_kernel(
    pos_ref, idm_ref, sums_ref, rows_ref, table_ref, cw_ref, sw_ref, gain_ref,
    pooled_ref, ng_ref, wt_ref, grads_ref,
    query_ref, tab_ref, small_ref,
):
    start, total = pos_ref[0], pos_ref[2]
    rows = idm_ref.shape[1]
    chans = table_ref.shape[1]
    idm = idm_ref[...]
    sums = sums_ref[...]
    probs = rows_ref[...]
    square, inner = sums[12:13], sums[13:14]
    scale = lax.rsqrt(square / D + EPS)
    pull = scale * scale * scale * (inner / D)
    q = {o: scale * sums[o + 2 : o + 3] - pull * sums[o + 8 : o + 9] for o in OFFS}
    weights = block_weights(start, total, rows)
    pgrad = []
    for row in weights:
        acc = None
        for o in row:
            acc = row[o] * q[o] if acc is None else acc + row[o] * q[o]
        pgrad.append(0.5 * acc)
    sgrad = []
    for n in range(8):
        mean = None
        for m in range(n % 2, 8, 2):
            term = probs[m : m + 1] * pgrad[m]
            mean = term if mean is None else mean + term
        sgrad.append(probs[n : n + 1] * (pgrad[n] - mean))
    ds = {}
    for o in OFFS:
        acc = None
        for n in range(8):
            if o in weights[n]:
                term = sgrad[n] * weights[n][o]
                acc = term if acc is None else acc + term
        ds[o] = acc
    hist = [jnp.sum(spread(idm, ds, k), axis=1, keepdims=True) for k in range(3)]
    cols = jnp.concatenate([scale, pull, jnp.zeros((6, rows), F32)], axis=0).T
    scale_c, pull_c = cols[:, 0:1], cols[:, 1:2]

    for c in range(chans // CHUNK):
        at = pl.ds(c * CHUNK, CHUNK)
        tab = table_ref[:, at].astype(F32)
        cw = cw_ref[:, at]
        sw = sw_ref[:, at]
        gain = gain_ref[:, at]
        ps = pooled_ref[:, at] * scale_c
        ng = ng_ref[:, at]
        gain_term = jnp.sum(ng * ps, axis=0, keepdims=True)
        normed = (ps * gain).astype(BF16)
        query_ref[at, :] = mm(normed, grads_ref[...], TN).astype(query_ref.dtype)
        pg = (ng * gain * scale_c - pull_c * pooled_ref[:, at]).astype(BF16)
        total_t = None
        outs = []
        score = None
        for k in range(3):
            full = mm(wt_ref[k], pg, NN) + hist[k] * sw
            term = cw[k : k + 1] * full
            total_t = term if total_t is None else total_t + term
            outs.append(jnp.sum(full * tab, axis=0, keepdims=True))
            term = cw[k : k + 1] * jnp.sum(hist[k] * tab, axis=0, keepdims=True)
            score = term if score is None else score + term
        tab_ref[:, at] = total_t.astype(tab_ref.dtype)
        small_ref[:, at] = jnp.concatenate(
            outs + [score, gain_term, jnp.zeros((3, CHUNK), F32)], axis=0
        )


def body(
    byte_ids, pad_lengths, table, conv_weight, score_weight, norm_gain, query_weight, query_grad
):
    ids = byte_ids[0]
    count = ids.shape[0]
    rows = count // 2
    vocab, chans = table.shape
    width = query_grad.shape[2]
    n_seq = lax.axis_size("seq")
    total = count * n_seq
    start = lax.axis_index("seq") * count
    limit = total - pad_lengths[0]
    ends = n_seq - 1
    up = [(i, i + 1) for i in range(ends)]
    down = [(i + 1, i) for i in range(ends)]
    ids_ext = jnp.concatenate(
        [lax.ppermute(ids[count - 3 :], "seq", up), ids, lax.ppermute(ids[:3], "seq", down)]
    )
    pos_e = start + jnp.arange(-3, count + 3, dtype=jnp.int32)
    ids_ext = jnp.where((pos_e >= 0) & (pos_e < limit), ids_ext, -1)
    halves = ids_ext.reshape(rows + 3, 2).T
    idm = jnp.stack([halves[j % 2, j // 2 : j // 2 + rows] for j in range(8)])
    pos = jnp.stack([start, limit, jnp.full_like(start, total)]).astype(jnp.int32)

    part = jnp.dot(
        conv_weight * score_weight, table.astype(F32).T, precision=lax.Precision.HIGHEST
    )
    p = jnp.pad(lax.psum(part, "tensor"), ((0, 5), (0, 0)))

    vm = pl.BlockSpec(memory_space=pltpu.VMEM)
    sm = pl.BlockSpec(memory_space=pltpu.SMEM)
    sw = score_weight[None, :]
    gain = norm_gain[None, :]
    pooled, ng, wt, sums, probs, grads = pl.pallas_call(
        forward_kernel,
        out_shape=(
            jax.ShapeDtypeStruct((rows, chans), F32),
            jax.ShapeDtypeStruct((rows, chans), F32),
            jax.ShapeDtypeStruct((3, vocab, rows), BF16),
            jax.ShapeDtypeStruct((16, rows), F32),
            jax.ShapeDtypeStruct((8, rows), F32),
            jax.ShapeDtypeStruct((rows, width), BF16),
        ),
        in_specs=[sm] + [vm] * 7,
        out_specs=(vm,) * 6,
        scratch_shapes=[
            pltpu.VMEM((3, rows, vocab), BF16),
            pltpu.VMEM((3, rows, vocab), BF16),
            pltpu.VMEM((3, vocab, rows), F32),
            pltpu.VMEM((3, vocab, rows), F32),
            pltpu.VMEM((rows, 128), F32),
            pltpu.VMEM((rows, 128), F32),
        ],
        name="forward",
    )(pos, idm, p, table, conv_weight, gain, query_weight, query_grad[0])
    sums = lax.psum(sums, "tensor")
    query, tab, small = pl.pallas_call(
        backward_kernel,
        out_shape=(
            jax.ShapeDtypeStruct((chans, width), BF16),
            jax.ShapeDtypeStruct((vocab, chans), BF16),
            jax.ShapeDtypeStruct((8, chans), F32),
        ),
        in_specs=[sm] + [vm] * 11,
        out_specs=(vm,) * 3,
        name="backward",
    )(pos, idm, sums, probs, table, conv_weight, sw, gain, pooled, ng, wt, grads)

    share = lax.psum_scatter(query, "seq", scatter_dimension=1, tiled=True)
    query_out = lax.psum(share, "dp")
    tab_out = lax.psum(tab, ("dp", "seq"))
    small_out = lax.psum(small, ("dp", "seq"))
    return (tab_out, small_out[0:3], small_out[3], small_out[4], query_out)


MESH = pl.DeviceIdType.MESH
BLOCK = 16
TILE = 256


def stacked(value):
    hi = value.astype(BF16)
    rest = value - hi.astype(F32)
    mid = rest.astype(BF16)
    low = (rest - mid.astype(F32)).astype(BF16)
    return jnp.concatenate([hi.astype(F32), mid.astype(F32), low.astype(F32)], axis=0).astype(BF16)


def packed_weights(start, total, rows):
    n = lax.broadcasted_iota(jnp.int32, (8, rows), 0)
    i = lax.broadcasted_iota(jnp.int32, (8, rows), 1)
    b, p = n // 2, n % 2
    even = (i % 2) == 0
    r = (start + 2 * i + p) % 3
    table = []
    for o in OFFS:
        at = start + 2 * i + o
        inside = (at >= 0) & (at < total)
        d = o - p
        near = (d >= -2) & (d <= 2) & (r >= -d) & (r <= 2 - d)
        w = jnp.where((b == 2) & near, 1.0 / 3.0, 0.0)
        w = jnp.where((b == 0) & (p == o), 1.0, w)
        if o in (0, 1):
            w = jnp.where(b == 1, 0.5, w)
            w = jnp.where(b == 3, 0.25, w)
        else:
            w = jnp.where((b == 3) & (even if o > 1 else ~even), 0.25, w)
        table.append(jnp.where(inside, w, 0.0))
    return table


def over_blocks(value):
    return value + pltpu.roll(value, 2, 0) + pltpu.roll(value, 4, 0) + pltpu.roll(value, 6, 0)


def fused_kernel(
    pad_ref, ids_ref, table_ref, cw_ref, sw_ref, gain_ref, wq_hbm, g_hbm,
    tab_ref, small_ref, query_ref,
    wq, g, tk, wt, wcat, pooled, ng, gb, pb, q, idm_s, a_s, w8_s, probs_s, hist, rr, lanes,
    p_own, p_in, halo, x1_own, x1_in, x2_own, x2_in,
    r1, s2, r2, zb, zr, own_z, zq, zs, zd, tb, tr, ts, tz, own_t, sm, sz, sd,
    in_sem, s_halo, r_halo, s_core, r_core, s_p1, r_p1, s_p2, r_p2, s_z, r_z, s_ag, r_ag,
    s_zq, r_zq, s_zd, r_zd, s_trs, r_trs, s_tz, r_tz, s_tb, r_tb, s_ta, r_ta, s_sm, r_sm,
):
    d, s, t = lax.axis_index("dp"), lax.axis_index("seq"), lax.axis_index("tensor")
    n_seq = lax.axis_size("seq")
    x, y = d % 2, d // 2
    x_near = y * 2 + (1 - x)
    y_near = (1 - y) * 2 + x
    corner = (1 - y) * 2 + (1 - x)
    dp_peers = (x_near, y_near, corner)
    seq_peers = [(s + e) % n_seq for e in range(1, n_seq)]
    count = ids_ref.shape[1]
    rows = count // 2
    vocab, chans = table_ref.shape
    width = g.shape[1]
    total = count * n_seq
    start = s * count
    limit = total - pad_ref[0]
    first_z = 3 * chans // 4
    half, quarter, eighth = first_z // 2, first_z // 4, first_z // 8
    step_z = (chans - first_z) // 4
    cols = width // n_seq
    t_dp, t_seq = vocab // 4, vocab // 4 // n_seq

    def remote(src, dst, send, recv, to):
        return pltpu.make_async_remote_copy(
            src_ref=src, dst_ref=dst, send_sem=send, recv_sem=recv,
            device_id=to, device_id_type=MESH,
        )

    take_g = pltpu.make_async_copy(g_hbm, g, in_sem.at[0])
    take_w = pltpu.make_async_copy(wq_hbm, wq, in_sem.at[1])
    take_g.start()
    take_w.start()

    barrier = pltpu.get_barrier_semaphore()
    peers = [(dd, s, t) for dd in dp_peers] + [(d, ss, t) for ss in seq_peers] + [(d, s, 1 - t)]
    for peer in peers:
        pl.semaphore_signal(barrier, inc=1, device_id=peer, device_id_type=MESH)

    cs = cw_ref[...] * sw_ref[...]
    p_own[...] = sum_parts(mm(stacked(pad8(cs)), table_ref[...], NT))
    pl.semaphore_wait(barrier, len(peers))

    put_p = remote(p_own, p_in, s_core.at[0], r_core.at[0], (d, s, 1 - t))
    put_p.start()
    to_left = remote(
        ids_ref.at[:, pl.ds(0, 128)], halo.at[1], s_halo.at[0], r_halo.at[1],
        (d, jnp.maximum(s - 1, 0), t),
    )
    to_right = remote(
        ids_ref.at[:, pl.ds(count - 128, 128)], halo.at[0], s_halo.at[1], r_halo.at[0],
        (d, jnp.minimum(s + 1, n_seq - 1), t),
    )

    @pl.when(s > 0)
    def _():
        to_left.start()

    @pl.when(s < n_seq - 1)
    def _():
        to_right.start()

    @pl.when(s == 0)
    def _():
        halo[0] = jnp.zeros((1, 128), jnp.int32)

    @pl.when(s == n_seq - 1)
    def _():
        halo[1] = jnp.zeros((1, 128), jnp.int32)

    for k in range(3):
        def spell(c, carry, k=k):
            at = pl.ds(pl.multiple_of(c * TILE, TILE), TILE)
            tk[k * vocab : (k + 1) * vocab, at] = (
                table_ref[:, at].astype(F32) * cw_ref[k : k + 1, at]
            ).astype(BF16)
            return carry

        lax.fori_loop(0, chans // TILE, spell, 0)
    take_g.wait()

    def mask(c, carry):
        at = pl.ds(pl.multiple_of(c * 64, 64), 64)
        i = lax.broadcasted_iota(jnp.int32, (64, width), 0) + c * 64
        g[at, :] = jnp.where(start + 2 * i < limit, g[at, :].astype(F32), 0.0).astype(BF16)
        return carry

    lax.fori_loop(0, rows // 64, mask, 0)
    take_w.wait()

    def pull_back(c, carry):
        at = pl.ds(pl.multiple_of(c * TILE, TILE), TILE)
        part = mm(g[...], wq[at, :], NT)
        ng[:, at] = part
        gb[:, at] = (part * gain_ref[:, at]).astype(BF16)
        return carry

    split_at = chans // TILE // 2
    lax.fori_loop(0, split_at, pull_back, 0)

    @pl.when(s > 0)
    def _():
        to_right.wait_recv()
        to_left.wait_send()

    @pl.when(s < n_seq - 1)
    def _():
        to_left.wait_recv()
        to_right.wait_send()

    put_p.wait()

    wide = rows + 128
    line = jnp.concatenate([halo[0], ids_ref[...], halo[1]], axis=1).astype(F32)
    pieces = wide // 128
    line = jnp.concatenate(
        [line[:, n * 256 : (n + 1) * 256] for n in range(pieces)]
        + [jnp.zeros((8 - pieces % 8, 256), F32)] * (pieces % 8 > 0),
        axis=0,
    )
    r = lax.broadcasted_iota(jnp.int32, (256, 256), 0)
    c = lax.broadcasted_iota(jnp.int32, (256, 256), 1)
    sift = jnp.where(r == jnp.where(c < 128, 2 * c, 2 * c - 255), 1.0, 0.0).astype(BF16)
    sifted = mm(line.astype(BF16), sift, NN)
    cat = jnp.concatenate(
        [
            jnp.concatenate([sifted[n : n + 1, p * 128 : (p + 1) * 128] for n in range(pieces)], axis=1)
            for p in range(2)
        ]
        + [jnp.zeros((6, wide), F32)],
        axis=0,
    ).astype(jnp.int32)
    lane = lax.broadcasted_iota(jnp.int32, cat.shape, 1)
    row = lax.broadcasted_iota(jnp.int32, cat.shape, 0)
    at_byte = start + 2 * (lane - 64) + row
    cat = jnp.where((at_byte >= 0) & (at_byte < limit) & (row < 2), cat, -1)

    def shifted(value, n):
        return pltpu.roll(value, wide - 64 - n, 1)[:, 0:rows]

    p3 = stacked(p_own[...] + p_in[...])
    v_wide = lax.broadcasted_iota(jnp.int32, (vocab, wide), 0)

    def picked(line):
        hot = jnp.where(line == v_wide, 1.0, 0.0).astype(BF16)
        return sum_parts(mm(p3, hot, NN))

    even, odd = picked(cat[0:1]), picked(cat[1:2])
    sc_even = pltpu.roll(odd, 1, 1)[0:1] + even[1:2] + odd[2:3]
    sc_odd = even[0:1] + odd[1:2] + pltpu.roll(even, wide - 1, 1)[2:3]
    se = jnp.broadcast_to(sc_even, (8, wide))
    so = jnp.broadcast_to(sc_odd, (8, wide))
    scores = [shifted(value, n) for n in (-1, 0, 1) for value in (se, so)]
    w8 = packed_weights(start, total, rows)
    score = w8[0] * scores[0]
    for n in range(1, 6):
        score = score + w8[n] * scores[n]
    expo = jnp.exp(score)
    probs = expo / over_blocks(expo)
    a = [0.5 * jnp.sum(probs * w, axis=0, keepdims=True) for w in w8]
    probs_s[...] = probs
    for n in range(6):
        w8_s[n] = w8[n]
    near = [shifted(cat, n) for n in (-2, -1, 0, 1, 2)]
    idm = [near[0][1:2], near[1][0:1], near[1][1:2], near[2][0:1], near[2][1:2],
           near[3][0:1], near[3][1:2], near[4][0:1]]
    for j in range(8):
        idm_s[j] = jnp.broadcast_to(idm[j], (8, rows))
    for o in range(6):
        a_s[o] = jnp.broadcast_to(a[o], (8, rows))

    def spread_rows(n):
        v = lax.broadcasted_iota(jnp.int32, (8, rows), 0) + n
        hits = [idm_s[j] == v for j in range(8)]
        accs = []
        for k in range(3):
            acc = jnp.where(hits[k], a_s[0], 0.0)
            for o in range(1, 6):
                acc = acc + jnp.where(hits[o + k], a_s[o], 0.0)
            accs.append(acc)
        return accs

    def spread_in(n, carry):
        at = pl.ds(pl.multiple_of(n * BLOCK, BLOCK), BLOCK)
        top, low = spread_rows(n * BLOCK), spread_rows(n * BLOCK + 8)
        for k in range(3):
            wt[k, at, :] = jnp.concatenate([top[k], low[k]], axis=0).astype(BF16)
        return carry

    lax.fori_loop(0, vocab // BLOCK, spread_in, 0)
    for k in range(3):
        wcat[:, k * vocab : (k + 1) * vocab] = wt[k].astype(F32).T.astype(BF16)

    lanes[...] = jnp.zeros_like(lanes)

    def pool(c, carry):
        at = pl.ds(pl.multiple_of(c * TILE, TILE), TILE)
        part = mm(wcat[...], tk[:, at], NN)
        pooled[:, at] = part
        pb[:, at] = part.astype(BF16)
        square = part * part
        lanes[...] += square[:, 0:128] + square[:, 128:256]
        return carry

    lax.fori_loop(0, chans // TILE, pool, 0)
    x1_own[...] = jnp.broadcast_to(jnp.sum(lanes[...].T, axis=0, keepdims=True), (8, rows))
    put_1 = remote(x1_own, x1_in, s_core.at[1], r_core.at[1], (d, s, 1 - t))
    put_1.start()
    lax.fori_loop(split_at, chans // TILE, pull_back, 0)
    put_1.wait()
    scale = lax.rsqrt((x1_own[...] + x1_in[...]) / D + EPS)
    scale_c = scale.T[:, 0:1]

    def product(c):
        at = pl.ds(c * TILE, TILE)
        normed = (pooled[:, at] * scale_c * gain_ref[:, at]).astype(BF16)
        q[at, :] = mm(normed, g[...], TN).astype(BF16)

    bit1, bit2 = (x, y), (y, x)
    near1 = ((x_near, s, t), (y_near, s, t))
    near2 = ((y_near, s, t), (x_near, s, t))

    def q_rows(h, first, second):
        return pl.ds(pl.multiple_of(h * half + first * quarter + second * eighth, BLOCK), eighth)

    p1, done = {}, 0
    for h in range(2):
        while done * TILE < (h + 1) * half:
            product(done)
            done += 1
        for part in range(2):
            second = bit2[h] if part else 1 - bit2[h]
            p1[h, part] = remote(
                q.at[q_rows(h, 1 - bit1[h], second)], r1.at[h, part],
                s_p1.at[h, part], r_p1.at[h, part], near1[h],
            )
            p1[h, part].start()
    while done * TILE < chans:
        product(done)
        done += 1
    late = slice(first_z, chans)
    z_first = []
    for e, ss in enumerate(seq_peers):
        at = pl.ds(pl.multiple_of(ss * cols, 128), cols)
        z_first.append(remote(q.at[late, at], zq.at[e], s_zq.at[e], r_zq.at[e], (d, ss, t)))
        z_first[-1].start()

    lanes[...] = jnp.zeros_like(lanes)

    def inner_in(c, carry):
        at = pl.ds(pl.multiple_of(c * TILE, TILE), TILE)
        inner = pooled[:, at] * (ng[:, at] * gain_ref[:, at])
        lanes[...] += inner[:, 0:128] + inner[:, 128:256]
        return carry

    lax.fori_loop(0, chans // TILE, inner_in, 0)
    found = []
    for source in (gb, pb):
        rr[...] = mm(tk[...], source[...], NT)

        def select(n, accs):
            at = pl.multiple_of(n * 8, 8)
            v = lax.broadcasted_iota(jnp.int32, (8, rows), 0) + n * 8
            accs = list(accs)
            lines = [rr[pl.ds(k * vocab + at, 8), :] for k in range(3)]
            for j in range(8):
                hit = idm_s[j] == v
                for k in range(3):
                    if 0 <= j - k < 6:
                        accs[j - k] = accs[j - k] + jnp.where(hit, lines[k], 0.0)
            return tuple(accs)

        sums = tuple(jnp.zeros((8, rows), F32) for o in range(6))
        sums = lax.fori_loop(0, vocab // 8, select, sums)
        found += [jnp.sum(acc, axis=0, keepdims=True) for acc in sums]
    found.append(jnp.sum(lanes[...].T, axis=0, keepdims=True))
    found.append(jnp.zeros((3, rows), F32))
    x2_own[...] = jnp.concatenate(found, axis=0)
    put_2 = remote(x2_own, x2_in, s_core.at[2], r_core.at[2], (d, s, 1 - t))
    put_2.start()

    p2 = {}
    for h in range(2):
        p1[h, 0].wait_recv()
        rows_h = q_rows(h, bit1[h], 1 - bit2[h])
        s2[h] = (q[rows_h, :].astype(F32) + r1[h, 0].astype(F32)).astype(BF16)
        for e in range(n_seq):
            at = pl.ds(pl.multiple_of((s + e + 1) % n_seq * cols, 128), cols)
            p2[h, e] = remote(
                s2.at[h, :, at], r2.at[h, :, at], s_p2.at[h, e], r_p2.at[h, e], near2[h]
            )
            p2[h, e].start()

    put_2.wait()
    sums = x2_own[...] + x2_in[...]
    pull = scale[0:1] * scale[0:1] * scale[0:1] * (sums[12:13] / D)
    w8 = [w8_s[n] for n in range(6)]
    probs = probs_s[...]
    pgrad = None
    for o in range(6):
        term = w8[o] * (scale[0:1] * sums[o : o + 1] - pull * sums[o + 6 : o + 7])
        pgrad = term if pgrad is None else pgrad + term
    pgrad = 0.5 * pgrad
    sgrad = probs * (pgrad - over_blocks(probs * pgrad))
    ds = [jnp.sum(sgrad * w, axis=0, keepdims=True) for w in w8]

    for o in range(6):
        a_s[o] = jnp.broadcast_to(ds[o], (8, rows))

    def count_in(n, carry):
        at = pl.ds(pl.multiple_of(n * 8, 8), 8)
        accs = spread_rows(n * 8)
        for k in range(3):
            hist[k, at, :] = jnp.broadcast_to(jnp.sum(accs[k], axis=1, keepdims=True), (8, 128))
        return carry

    lax.fori_loop(0, vocab // 8, count_in, 0)
    pull_c = jnp.broadcast_to(pull, (8, rows)).T[:, 0:1]

    def table_step(c, carry):
        at = pl.ds(pl.multiple_of(c * TILE, TILE), TILE)
        tab = table_ref[:, at].astype(F32)
        cw, sw, gain = cw_ref[:, at], sw_ref[:, at], gain_ref[:, at]
        ngc, pc = ng[:, at], pooled[:, at]
        scaled = ngc * scale_c
        gain_term = jnp.sum(scaled * pc, axis=0, keepdims=True)
        pg = (scaled * gain - pull_c * pc).astype(BF16)
        whole, outs, score = None, [], None
        for k in range(3):
            hist_k = hist[k][:, 0:1]
            full = mm(wt[k], pg, NN) + hist_k * sw
            term = cw[k : k + 1] * full
            whole = term if whole is None else whole + term
            outs.append(jnp.sum(full * tab, axis=0, keepdims=True))
            term = cw[k : k + 1] * jnp.sum(hist_k * tab, axis=0, keepdims=True)
            score = term if score is None else score + term
        tb[:, at] = whole.astype(BF16)
        sm[:, at] = jnp.concatenate(outs + [score, gain_term, jnp.zeros((3, TILE), F32)], axis=0)
        return carry

    lax.fori_loop(0, chans // TILE, table_step, 0)

    t_rs, sm_z = {}, []
    turns = [(s + e + 1) % n_seq for e in range(n_seq)]
    for e, j in enumerate(turns):
        for n, dd in enumerate(dp_peers):
            block = tb.at[pl.ds(pl.multiple_of(dd * t_dp + j * t_seq, t_seq), t_seq)]
            t_rs[e, n] = remote(block, tr.at[e, n], s_trs.at[e, n], r_trs.at[e, n], (dd, s, t))
            t_rs[e, n].start()
    for e, ss in enumerate(seq_peers):
        sm_z.append(remote(sm, sz.at[s], s_sm.at[e], r_sm.at[e], (d, ss, t)))
        sm_z[-1].start()
    sz[s] = sm[...]

    for h in range(2):
        p1[h, 1].wait_recv()
    q_z = {}
    for e, j in enumerate(turns):
        at = pl.ds(pl.multiple_of(j * cols, 128), cols)
        for h in range(2):
            p2[h, e].wait_recv()
            rows_h = q_rows(h, bit1[h], bit2[h])
            block = q[rows_h, at].astype(F32) + r1[h, 1, :, at].astype(F32)
            block = block + r2[h, :, at].astype(F32)
            if e < n_seq - 1:
                zb[h, e] = block.astype(BF16)
                q_z[h, e] = remote(
                    zb.at[h, e], zr.at[h, e], s_z.at[h, e], r_z.at[h, e], (d, j, t)
                )
                q_z[h, e].start()
            else:
                own_z[h] = block

    for copy in z_first:
        copy.wait_recv()
    block = q[late, pl.ds(pl.multiple_of(s * cols, 128), cols)].astype(F32)
    for e in range(n_seq - 1):
        block = block + zq[e].astype(F32)
    zs[...] = block.astype(BF16)
    z_rs = []
    for n, dd in enumerate(dp_peers):
        rows_n = pl.ds(pl.multiple_of(dd * step_z, BLOCK), step_z)
        z_rs.append(remote(zs.at[rows_n], zd.at[n], s_zd.at[n], r_zd.at[n], (dd, s, t)))
        z_rs[-1].start()

    t_z = {}
    for e, j in enumerate(turns):
        acc = tb[pl.ds(pl.multiple_of(d * t_dp + j * t_seq, t_seq), t_seq), :].astype(F32)
        for n in range(3):
            t_rs[e, n].wait_recv()
            acc = acc + tr[e, n].astype(F32)
        if e < n_seq - 1:
            ts[e] = acc.astype(BF16)
            t_z[e] = remote(ts.at[e], tz.at[e], s_tz.at[e], r_tz.at[e], (d, j, t))
            t_z[e].start()
        else:
            own_t[...] = acc

    for copy in sm_z:
        copy.wait_recv()
    acc = sz[0]
    for n in range(1, n_seq):
        acc = acc + sz[n]
    sd[d] = acc
    sm_d = []
    for n, dd in enumerate(dp_peers):
        sm_d.append(remote(sd.at[d], sd.at[d], s_sm.at[3 + n], r_sm.at[3 + n], (dd, s, t)))
        sm_d[-1].start()

    ag = []

    def share(out, mine, send, recv):
        for n, dd in enumerate(dp_peers):
            ag.append(remote(out.at[mine], out.at[mine], send.at[n], recv.at[n], (dd, s, t)))
            ag[-1].start()

    block = zs[pl.ds(pl.multiple_of(d * step_z, BLOCK), step_z), :].astype(F32)
    for n in range(3):
        z_rs[n].wait_recv()
        block = block + zd[n].astype(F32)
    mine = pl.ds(pl.multiple_of(first_z + d * step_z, BLOCK), step_z)
    query_ref[mine, :] = block.astype(BF16)
    share(query_ref, mine, s_ag.at[2], r_ag.at[2])

    for h in range(2):
        block = own_z[h]
        for e in range(n_seq - 1):
            q_z[h, e].wait_recv()
            block = block + zr[h, e].astype(F32)
        mine = q_rows(h, bit1[h], bit2[h])
        query_ref[mine, :] = block.astype(BF16)
        share(query_ref, mine, s_ag.at[h], r_ag.at[h])

    acc = own_t[...]
    for e in range(n_seq - 1):
        t_z[e].wait_recv()
        acc = acc + tz[e].astype(F32)

    def table_rows(j):
        return pl.ds(pl.multiple_of(d * t_dp + j * t_seq, t_seq), t_seq)

    mine = table_rows(s)
    tab_ref[mine, :] = acc.astype(BF16)
    t_back = []
    for e, ss in enumerate(seq_peers):
        t_back.append(
            remote(tab_ref.at[mine], tab_ref.at[mine], s_tb.at[e], r_tb.at[e], (d, ss, t))
        )
        t_back[-1].start()
    share(tab_ref, mine, s_ta.at[n_seq - 1], r_ta.at[n_seq - 1])
    for e in range(n_seq - 1):
        t_back[e].wait_recv()
        share(tab_ref, table_rows((s + n_seq - 1 - e) % n_seq), s_ta.at[e], r_ta.at[e])

    for copy in sm_d:
        copy.wait_recv()
    small_ref[...] = (sd[0] + sd[1]) + (sd[2] + sd[3])
    for copy in ag:
        copy.wait_recv()
    for group in (p1, p2, q_z, t_rs, t_z):
        for copy in group.values():
            copy.wait_send()
    for copy in z_first + z_rs + t_back + sm_z + sm_d + ag:
        copy.wait_send()


def finish_kernel(tab_ref, small_ref, query_ref, tab_out, conv_out, score_out, gain_out, query_out):
    conv_out[...] = small_ref[0:3]
    score_out[...] = small_ref[3:4]
    gain_out[...] = small_ref[4:5]
    tab_out[...] = tab_ref[...]
    query_out[...] = query_ref[...]


def pad8(value):
    return jnp.concatenate([value, jnp.zeros((8 - value.shape[0], value.shape[1]), F32)], axis=0)


def sum_parts(value):
    return value[0:8] + value[8:16] + value[16:24]


def fused_body(
    byte_ids, pad_lengths, table, conv_weight, score_weight, norm_gain, query_weight, query_grad
):
    count = byte_ids.shape[1]
    rows = count // 2
    vocab, chans = table.shape
    width = query_grad.shape[2]
    n_seq = lax.axis_size("seq")
    cols = width // n_seq
    first_z = 3 * chans // 4
    part, t_dp = first_z // 8, vocab // 4
    t_seq, step_z, others = t_dp // n_seq, (chans - first_z) // 4, n_seq - 1
    vm = pl.BlockSpec(memory_space=pltpu.VMEM)
    sm = pl.BlockSpec(memory_space=pltpu.SMEM)
    hbm = pl.BlockSpec(memory_space=pl.ANY)
    V, DMA = pltpu.VMEM, pltpu.SemaphoreType.DMA
    tab, small, query = pl.pallas_call(
        fused_kernel,
        out_shape=(
            jax.ShapeDtypeStruct((vocab, chans), BF16),
            jax.ShapeDtypeStruct((8, chans), F32),
            jax.ShapeDtypeStruct((chans, cols), BF16),
        ),
        in_specs=[sm] + [vm] * 5 + [hbm] * 2,
        out_specs=(vm,) * 3,
        scratch_shapes=[
            V((chans, width), BF16), V((rows, width), BF16), V((3 * vocab, chans), BF16),
            V((3, vocab, rows), BF16), V((rows, 3 * vocab), BF16), V((rows, chans), F32),
            V((rows, chans), F32), V((rows, chans), BF16), V((rows, chans), BF16),
            V((chans, width), BF16), V((8, 8, rows), jnp.int32), V((6, 8, rows), F32),
            V((6, 8, rows), F32), V((8, rows), F32), V((3, vocab, 128), F32),
            V((3 * vocab, rows), F32), V((rows, 128), F32),
            V((8, vocab), F32), V((8, vocab), F32), V((2, 1, 128), jnp.int32),
            V((8, rows), F32), V((8, rows), F32), V((16, rows), F32), V((16, rows), F32),
            V((2, 2, part, width), BF16), V((2, part, width), BF16), V((2, part, width), BF16),
            V((2, others, part, cols), BF16), V((2, others, part, cols), BF16),
            V((2, part, cols), F32), V((others, chans - first_z, cols), BF16),
            V((chans - first_z, cols), BF16), V((3, step_z, cols), BF16),
            V((vocab, chans), BF16), V((n_seq, 3, t_seq, chans), BF16),
            V((others, t_seq, chans), BF16), V((others, t_seq, chans), BF16),
            V((t_seq, chans), F32), V((8, chans), F32), V((n_seq, 8, chans), F32),
            V((4, 8, chans), F32),
            DMA((2,)), DMA((2,)), DMA((2,)), DMA((3,)), DMA((3,)),
            DMA((2, 2)), DMA((2, 2)), DMA((2, n_seq)), DMA((2, n_seq)),
            DMA((2, others)), DMA((2, others)), DMA((3, 3)), DMA((3, 3)),
            DMA((others,)), DMA((others,)), DMA((3,)), DMA((3,)),
            DMA((n_seq, 3)), DMA((n_seq, 3)), DMA((others,)), DMA((others,)),
            DMA((others,)), DMA((others,)), DMA((n_seq, 3)), DMA((n_seq, 3)),
            DMA((6,)), DMA((6,)),
        ],
        compiler_params=pltpu.CompilerParams(collective_id=0, has_side_effects=True),
        name="fused",
    )(
        pad_lengths, byte_ids, table, conv_weight, score_weight[None, :], norm_gain[None, :],
        query_weight, query_grad[0],
    )
    return pl.pallas_call(
        finish_kernel,
        out_shape=(
            jax.ShapeDtypeStruct((vocab, chans), BF16),
            jax.ShapeDtypeStruct((3, chans), F32),
            jax.ShapeDtypeStruct((1, chans), F32),
            jax.ShapeDtypeStruct((1, chans), F32),
            jax.ShapeDtypeStruct((chans, cols), BF16),
        ),
        in_specs=[vm] * 3,
        out_specs=(vm,) * 5,
        name="finish",
    )(tab, small, query)


def fused_outer(*args):
    tab, conv, score, gain, query = fused_body(*args)
    return (tab, conv, score.reshape(-1), gain.reshape(-1), query)


def fits(mesh):
    return mesh.shape["dp"] == 4 and mesh.shape["seq"] == 4 and mesh.shape["tensor"] == 2


def solution(mesh):
    return jax.shard_map(
        fused_outer if fits(mesh) else body,
        mesh=mesh,
        in_specs=(
            P("dp", "seq"),
            P("dp"),
            P(None, "tensor"),
            P(None, "tensor"),
            P("tensor"),
            P("tensor"),
            P("tensor", None),
            P("dp", "seq", None),
        ),
        out_specs=(
            P(None, "tensor"),
            P(None, "tensor"),
            P("tensor"),
            P("tensor"),
            P("tensor", "seq"),
        ),
        check_vma=False,
    )
```

```python
import functools

import jax
import jax.numpy as jnp
from jax import lax
from jax.experimental import pallas as pl
from jax.experimental.pallas import tpu as pltpu
from jax.sharding import PartitionSpec as P

D = 2048
EPS = 1e-06
F32 = jnp.float32
BF16 = jnp.bfloat16
OFFS = range(-2, 4)
CHUNK = 256

NN = (((1,), (0,)), ((), ()))
NT = (((1,), (1,)), ((), ()))
TN = (((0,), (0,)), ((), ()))


def mm(lhs, rhs, dims):
    return lax.dot_general(lhs, rhs, dims, preferred_element_type=F32)


def block_weights(start, total, rows):
    i = lax.broadcasted_iota(jnp.int32, (1, rows), 1)
    even = (i % 2) == 0
    inside = {o: (start + 2 * i + o >= 0) & (start + 2 * i + o < total) for o in OFFS}
    table = []
    for b in range(4):
        for p in range(2):
            row = {}
            for o in OFFS:
                if b == 0:
                    if o == p:
                        row[o] = jnp.where(inside[o], 1.0, 0.0)
                elif b == 1:
                    if o in (0, 1):
                        row[o] = jnp.where(inside[o], 0.5, 0.0)
                elif b == 3:
                    if o in (0, 1):
                        row[o] = jnp.where(inside[o], 0.25, 0.0)
                    else:
                        row[o] = jnp.where(inside[o] & (even if o > 1 else ~even), 0.25, 0.0)
                else:
                    d = o - p
                    if -2 <= d <= 2:
                        r = (start + 2 * i + p) % 3
                        row[o] = jnp.where(inside[o] & (r >= -d) & (r <= 2 - d), 1.0 / 3.0, 0.0)
            table.append(row)
    return table


def spread(idm, rows_of, tap):
    rows = idm.shape[1]
    v = lax.broadcasted_iota(jnp.int32, (256, rows), 0)
    acc = None
    for o in OFFS:
        at = o + tap + 2
        term = jnp.where(idm[at : at + 1, :] == v, rows_of[o], 0.0)
        acc = term if acc is None else acc + term
    return acc


def forward_kernel(
    pos_ref, idm_ref, p_ref, table_ref, cw_ref, gain_ref, wq_ref, g_ref,
    pooled_ref, ng_ref, wt_ref, sums_ref, rows_ref, grads_ref,
    wh, wl, r1, r2, sq, rd,
):
    start, limit, total = pos_ref[0], pos_ref[1], pos_ref[2]
    rows = idm_ref.shape[1]
    chans = table_ref.shape[1]
    idm = idm_ref[...]
    v = lax.broadcasted_iota(jnp.int32, (256, rows), 0)
    p = p_ref[...]
    hi = p.astype(BF16)
    rest = p - hi.astype(F32)
    mid = rest.astype(BF16)
    low = (rest - mid.astype(F32)).astype(BF16)
    p3 = jnp.concatenate([hi.astype(F32), mid.astype(F32), low.astype(F32)], axis=0).astype(BF16)
    picks = []
    for j in range(8):
        hot = jnp.where(idm[j : j + 1, :] == v, 1.0, 0.0).astype(BF16)
        g = mm(p3, hot, NN)
        picks.append(g[0:8] + g[8:16] + g[16:24])
    s = {o: picks[o + 2][0:1] + picks[o + 3][1:2] + picks[o + 4][2:3] for o in OFFS}
    weights = block_weights(start, total, rows)
    expo = []
    for row in weights:
        score = None
        for o in row:
            score = row[o] * s[o] if score is None else score + row[o] * s[o]
        expo.append(jnp.exp(score))
    probs = []
    for n in range(8):
        whole = expo[n % 2] + expo[2 + n % 2] + expo[4 + n % 2] + expo[6 + n % 2]
        probs.append(expo[n] / whole)
    a = {}
    for o in OFFS:
        acc = None
        for n in range(8):
            if o in weights[n]:
                term = probs[n] * weights[n][o]
                acc = term if acc is None else acc + term
        a[o] = 0.5 * acc
    rows_ref[...] = jnp.concatenate(probs, axis=0)
    for k in range(3):
        w = spread(idm, a, k)
        wt_ref[k] = w.astype(BF16)
        wf = w.T
        top = wf.astype(BF16)
        wh[k] = top
        wl[k] = (wf - top.astype(F32)).astype(BF16)
    keep = (start + 2 * lax.broadcasted_iota(jnp.int32, g_ref.shape, 0)) < limit
    grads_ref[...] = jnp.where(keep, g_ref[...].astype(F32), 0.0).astype(BF16)
    r1[...] = jnp.zeros_like(r1)
    r2[...] = jnp.zeros_like(r2)
    sq[...] = jnp.zeros_like(sq)
    rd[...] = jnp.zeros_like(rd)

    def step(c, carry):
        at = pl.ds(pl.multiple_of(c * CHUNK, CHUNK), CHUNK)
        tab = table_ref[:, at]
        cw = cw_ref[:, at]
        ng = mm(grads_ref[...], wq_ref[at, :], NT)
        pooled = None
        for k in range(3):
            part = cw[k : k + 1] * (mm(wh[k], tab, NN) + mm(wl[k], tab, NN))
            pooled = part if pooled is None else pooled + part
        pooled_ref[:, at] = pooled
        ng_ref[:, at] = ng
        gained = ng * gain_ref[:, at]
        square = pooled * pooled
        inner = pooled * gained
        sq[...] += square[:, 0:128] + square[:, 128:256]
        rd[...] += inner[:, 0:128] + inner[:, 128:256]
        gb = gained.astype(BF16)
        pb = pooled.astype(BF16)
        for k in range(3):
            tk = (tab.astype(F32) * cw[k : k + 1]).astype(BF16)
            r1[k] += mm(tk, gb, NT)
            r2[k] += mm(tk, pb, NT)
        return carry

    lax.fori_loop(0, chans // CHUNK, step, 0)
    out = []
    for r in (r1, r2):
        for o in OFFS:
            acc = None
            for k in range(3):
                at = o + k + 2
                term = jnp.where(idm[at : at + 1, :] == v, r[k], 0.0)
                acc = term if acc is None else acc + term
            out.append(jnp.sum(acc, axis=0, keepdims=True))
    out.append(jnp.sum(sq[...].T, axis=0, keepdims=True))
    out.append(jnp.sum(rd[...].T, axis=0, keepdims=True))
    out.append(jnp.zeros((2, rows), F32))
    sums_ref[...] = jnp.concatenate(out, axis=0)


def backward_kernel(
    pos_ref, idm_ref, sums_ref, rows_ref, table_ref, cw_ref, sw_ref, gain_ref,
    pooled_ref, ng_ref, wt_ref, grads_ref,
    query_ref, tab_ref, small_ref,
):
    start, total = pos_ref[0], pos_ref[2]
    rows = idm_ref.shape[1]
    chans = table_ref.shape[1]
    idm = idm_ref[...]
    sums = sums_ref[...]
    probs = rows_ref[...]
    square, inner = sums[12:13], sums[13:14]
    scale = lax.rsqrt(square / D + EPS)
    pull = scale * scale * scale * (inner / D)
    q = {o: scale * sums[o + 2 : o + 3] - pull * sums[o + 8 : o + 9] for o in OFFS}
    weights = block_weights(start, total, rows)
    pgrad = []
    for row in weights:
        acc = None
        for o in row:
            acc = row[o] * q[o] if acc is None else acc + row[o] * q[o]
        pgrad.append(0.5 * acc)
    sgrad = []
    for n in range(8):
        mean = None
        for m in range(n % 2, 8, 2):
            term = probs[m : m + 1] * pgrad[m]
            mean = term if mean is None else mean + term
        sgrad.append(probs[n : n + 1] * (pgrad[n] - mean))
    ds = {}
    for o in OFFS:
        acc = None
        for n in range(8):
            if o in weights[n]:
                term = sgrad[n] * weights[n][o]
                acc = term if acc is None else acc + term
        ds[o] = acc
    hist = [jnp.sum(spread(idm, ds, k), axis=1, keepdims=True) for k in range(3)]
    cols = jnp.concatenate([scale, pull, jnp.zeros((6, rows), F32)], axis=0).T
    scale_c, pull_c = cols[:, 0:1], cols[:, 1:2]

    for c in range(chans // CHUNK):
        at = pl.ds(c * CHUNK, CHUNK)
        tab = table_ref[:, at].astype(F32)
        cw = cw_ref[:, at]
        sw = sw_ref[:, at]
        gain = gain_ref[:, at]
        ps = pooled_ref[:, at] * scale_c
        ng = ng_ref[:, at]
        gain_term = jnp.sum(ng * ps, axis=0, keepdims=True)
        normed = (ps * gain).astype(BF16)
        query_ref[at, :] = mm(normed, grads_ref[...], TN).astype(query_ref.dtype)
        pg = (ng * gain * scale_c - pull_c * pooled_ref[:, at]).astype(BF16)
        total_t = None
        outs = []
        score = None
        for k in range(3):
            full = mm(wt_ref[k], pg, NN) + hist[k] * sw
            term = cw[k : k + 1] * full
            total_t = term if total_t is None else total_t + term
            outs.append(jnp.sum(full * tab, axis=0, keepdims=True))
            term = cw[k : k + 1] * jnp.sum(hist[k] * tab, axis=0, keepdims=True)
            score = term if score is None else score + term
        tab_ref[:, at] = total_t.astype(tab_ref.dtype)
        small_ref[:, at] = jnp.concatenate(
            outs + [score, gain_term, jnp.zeros((3, CHUNK), F32)], axis=0
        )


def body(
    byte_ids, pad_lengths, table, conv_weight, score_weight, norm_gain, query_weight, query_grad
):
    ids = byte_ids[0]
    count = ids.shape[0]
    rows = count // 2
    vocab, chans = table.shape
    width = query_grad.shape[2]
    n_seq = lax.axis_size("seq")
    total = count * n_seq
    start = lax.axis_index("seq") * count
    limit = total - pad_lengths[0]
    ends = n_seq - 1
    up = [(i, i + 1) for i in range(ends)]
    down = [(i + 1, i) for i in range(ends)]
    ids_ext = jnp.concatenate(
        [lax.ppermute(ids[count - 3 :], "seq", up), ids, lax.ppermute(ids[:3], "seq", down)]
    )
    pos_e = start + jnp.arange(-3, count + 3, dtype=jnp.int32)
    ids_ext = jnp.where((pos_e >= 0) & (pos_e < limit), ids_ext, -1)
    halves = ids_ext.reshape(rows + 3, 2).T
    idm = jnp.stack([halves[j % 2, j // 2 : j // 2 + rows] for j in range(8)])
    pos = jnp.stack([start, limit, jnp.full_like(start, total)]).astype(jnp.int32)

    part = jnp.dot(
        conv_weight * score_weight, table.astype(F32).T, precision=lax.Precision.HIGHEST
    )
    p = jnp.pad(lax.psum(part, "tensor"), ((0, 5), (0, 0)))

    vm = pl.BlockSpec(memory_space=pltpu.VMEM)
    sm = pl.BlockSpec(memory_space=pltpu.SMEM)
    sw = score_weight[None, :]
    gain = norm_gain[None, :]
    pooled, ng, wt, sums, probs, grads = pl.pallas_call(
        forward_kernel,
        out_shape=(
            jax.ShapeDtypeStruct((rows, chans), F32),
            jax.ShapeDtypeStruct((rows, chans), F32),
            jax.ShapeDtypeStruct((3, vocab, rows), BF16),
            jax.ShapeDtypeStruct((16, rows), F32),
            jax.ShapeDtypeStruct((8, rows), F32),
            jax.ShapeDtypeStruct((rows, width), BF16),
        ),
        in_specs=[sm] + [vm] * 7,
        out_specs=(vm,) * 6,
        scratch_shapes=[
            pltpu.VMEM((3, rows, vocab), BF16),
            pltpu.VMEM((3, rows, vocab), BF16),
            pltpu.VMEM((3, vocab, rows), F32),
            pltpu.VMEM((3, vocab, rows), F32),
            pltpu.VMEM((rows, 128), F32),
            pltpu.VMEM((rows, 128), F32),
        ],
        name="forward",
    )(pos, idm, p, table, conv_weight, gain, query_weight, query_grad[0])
    sums = lax.psum(sums, "tensor")
    query, tab, small = pl.pallas_call(
        backward_kernel,
        out_shape=(
            jax.ShapeDtypeStruct((chans, width), BF16),
            jax.ShapeDtypeStruct((vocab, chans), BF16),
            jax.ShapeDtypeStruct((8, chans), F32),
        ),
        in_specs=[sm] + [vm] * 11,
        out_specs=(vm,) * 3,
        name="backward",
    )(pos, idm, sums, probs, table, conv_weight, sw, gain, pooled, ng, wt, grads)

    share = lax.psum_scatter(query, "seq", scatter_dimension=1, tiled=True)
    query_out = lax.psum(share, "dp")
    tab_out = lax.psum(tab, ("dp", "seq"))
    small_out = lax.psum(small, ("dp", "seq"))
    return (tab_out, small_out[0:3], small_out[3], small_out[4], query_out)


MESH = pl.DeviceIdType.MESH
BLOCK = 16
TILE = 256


def stacked(value):
    hi = value.astype(BF16)
    rest = value - hi.astype(F32)
    mid = rest.astype(BF16)
    low = (rest - mid.astype(F32)).astype(BF16)
    return jnp.concatenate([hi.astype(F32), mid.astype(F32), low.astype(F32)], axis=0).astype(BF16)


def packed_weights(start, total, rows):
    n = lax.broadcasted_iota(jnp.int32, (8, rows), 0)
    i = lax.broadcasted_iota(jnp.int32, (8, rows), 1)
    b, p = n // 2, n % 2
    even = (i % 2) == 0
    r = (start + 2 * i + p) % 3
    table = []
    for o in OFFS:
        at = start + 2 * i + o
        inside = (at >= 0) & (at < total)
        d = o - p
        near = (d >= -2) & (d <= 2) & (r >= -d) & (r <= 2 - d)
        w = jnp.where((b == 2) & near, 1.0 / 3.0, 0.0)
        w = jnp.where((b == 0) & (p == o), 1.0, w)
        if o in (0, 1):
            w = jnp.where(b == 1, 0.5, w)
            w = jnp.where(b == 3, 0.25, w)
        else:
            w = jnp.where((b == 3) & (even if o > 1 else ~even), 0.25, w)
        table.append(jnp.where(inside, w, 0.0))
    return table


def over_blocks(value):
    return value + pltpu.roll(value, 2, 0) + pltpu.roll(value, 4, 0) + pltpu.roll(value, 6, 0)


def fused_kernel(
    pad_ref, ids_ref, table_hbm, cw_ref, sw_ref, gain_ref, wq_hbm, g_hbm,
    tab_ref, small_ref, query_ref,
    table_ref, wq, g, tk, wt, wcat, pooled, ng, gb, pb, q, idm_s, a_s, w8_s, probs_s, hist, rr, lanes,
    p_own, p_in, halo, x1_own, x1_in, x2_own, x2_in,
    r1, s2, r2, zb, zr, own_z, late, zq, zs, zd, tb, tr, ts, tz, own_t, sm, sz, sd,
    in_sem, s_halo, r_halo, s_core, r_core, s_p1, r_p1, s_p2, r_p2, s_z, r_z, s_ag, r_ag,
    s_zq, r_zq, s_zd, r_zd, s_trs, r_trs, s_tz, r_tz, s_tb, r_tb, s_ta, r_ta, s_sm, r_sm,
):
    d, s, t = lax.axis_index("dp"), lax.axis_index("seq"), lax.axis_index("tensor")
    n_seq = lax.axis_size("seq")
    x, y = d % 2, d // 2
    x_near = y * 2 + (1 - x)
    y_near = (1 - y) * 2 + x
    corner = (1 - y) * 2 + (1 - x)
    dp_peers = (x_near, y_near, corner)
    seq_peers = [(s + e) % n_seq for e in range(1, n_seq)]
    count = ids_ref.shape[1]
    rows = count // 2
    vocab, chans = table_ref.shape
    width = g.shape[1]
    total = count * n_seq
    start = s * count
    limit = total - pad_ref[0]
    first_z = 3 * chans // 4
    half, quarter, eighth = first_z // 2, first_z // 4, first_z // 8
    step_z = (chans - first_z) // 4
    cols = width // n_seq
    t_dp, t_seq = vocab // 4, vocab // 4 // n_seq

    def remote(src, dst, send, recv, to):
        return pltpu.make_async_remote_copy(
            src_ref=src, dst_ref=dst, send_sem=send, recv_sem=recv,
            device_id=to, device_id_type=MESH,
        )

    take_g = pltpu.make_async_copy(g_hbm, g, in_sem.at[0])
    take_w = pltpu.make_async_copy(wq_hbm, wq, in_sem.at[1])
    take_t = pltpu.make_async_copy(table_hbm, table_ref, in_sem.at[2])
    take_t.start()
    take_g.start()
    take_w.start()

    barrier = pltpu.get_barrier_semaphore()
    peers = [(dd, s, t) for dd in dp_peers] + [(d, ss, t) for ss in seq_peers] + [(d, s, 1 - t)]
    for peer in peers:
        pl.semaphore_signal(barrier, inc=1, device_id=peer, device_id_type=MESH)

    cs = cw_ref[...] * sw_ref[...]
    take_t.wait()
    p_own[...] = sum_parts(mm(stacked(pad8(cs)), table_ref[...], NT))
    pl.semaphore_wait(barrier, len(peers))

    put_p = remote(p_own, p_in, s_core.at[0], r_core.at[0], (d, s, 1 - t))
    put_p.start()
    to_left = remote(
        ids_ref.at[:, pl.ds(0, 128)], halo.at[1], s_halo.at[0], r_halo.at[1],
        (d, jnp.maximum(s - 1, 0), t),
    )
    to_right = remote(
        ids_ref.at[:, pl.ds(count - 128, 128)], halo.at[0], s_halo.at[1], r_halo.at[0],
        (d, jnp.minimum(s + 1, n_seq - 1), t),
    )

    @pl.when(s > 0)
    def _():
        to_left.start()

    @pl.when(s < n_seq - 1)
    def _():
        to_right.start()

    @pl.when(s == 0)
    def _():
        halo[0] = jnp.zeros((1, 128), jnp.int32)

    @pl.when(s == n_seq - 1)
    def _():
        halo[1] = jnp.zeros((1, 128), jnp.int32)

    for k in range(3):
        def spell(c, carry, k=k):
            at = pl.ds(pl.multiple_of(c * TILE, TILE), TILE)
            tk[k * vocab : (k + 1) * vocab, at] = (
                table_ref[:, at].astype(F32) * cw_ref[k : k + 1, at]
            ).astype(BF16)
            return carry

        lax.fori_loop(0, chans // TILE, spell, 0)
    take_g.wait()

    def mask(c, carry):
        at = pl.ds(pl.multiple_of(c * 64, 64), 64)
        i = lax.broadcasted_iota(jnp.int32, (64, width), 0) + c * 64
        g[at, :] = jnp.where(start + 2 * i < limit, g[at, :].astype(F32), 0.0).astype(BF16)
        return carry

    lax.fori_loop(0, rows // 64, mask, 0)
    take_w.wait()

    def pull_back(c, carry):
        at = pl.ds(pl.multiple_of(c * TILE, TILE), TILE)
        part = mm(g[...], wq[at, :], NT)
        ng[:, at] = part
        gb[:, at] = (part * gain_ref[:, at]).astype(BF16)
        return carry

    split_at = chans // TILE // 2
    lax.fori_loop(0, split_at, pull_back, 0)

    @pl.when(s > 0)
    def _():
        to_right.wait_recv()
        to_left.wait_send()

    @pl.when(s < n_seq - 1)
    def _():
        to_left.wait_recv()
        to_right.wait_send()

    put_p.wait()

    wide = rows + 128
    line = jnp.concatenate([halo[0], ids_ref[...], halo[1]], axis=1).astype(F32)
    pieces = wide // 128
    line = jnp.concatenate(
        [line[:, n * 256 : (n + 1) * 256] for n in range(pieces)]
        + [jnp.zeros((8 - pieces % 8, 256), F32)] * (pieces % 8 > 0),
        axis=0,
    )
    r = lax.broadcasted_iota(jnp.int32, (256, 256), 0)
    c = lax.broadcasted_iota(jnp.int32, (256, 256), 1)
    sift = jnp.where(r == jnp.where(c < 128, 2 * c, 2 * c - 255), 1.0, 0.0).astype(BF16)
    sifted = mm(line.astype(BF16), sift, NN)
    cat = jnp.concatenate(
        [
            jnp.concatenate([sifted[n : n + 1, p * 128 : (p + 1) * 128] for n in range(pieces)], axis=1)
            for p in range(2)
        ]
        + [jnp.zeros((6, wide), F32)],
        axis=0,
    ).astype(jnp.int32)
    lane = lax.broadcasted_iota(jnp.int32, cat.shape, 1)
    row = lax.broadcasted_iota(jnp.int32, cat.shape, 0)
    at_byte = start + 2 * (lane - 64) + row
    cat = jnp.where((at_byte >= 0) & (at_byte < limit) & (row < 2), cat, -1)

    def shifted(value, n):
        return pltpu.roll(value, wide - 64 - n, 1)[:, 0:rows]

    p3 = stacked(p_own[...] + p_in[...])
    v_wide = lax.broadcasted_iota(jnp.int32, (vocab, wide), 0)

    def picked(line):
        hot = jnp.where(line == v_wide, 1.0, 0.0).astype(BF16)
        return sum_parts(mm(p3, hot, NN))

    even, odd = picked(cat[0:1]), picked(cat[1:2])
    sc_even = pltpu.roll(odd, 1, 1)[0:1] + even[1:2] + odd[2:3]
    sc_odd = even[0:1] + odd[1:2] + pltpu.roll(even, wide - 1, 1)[2:3]
    se = jnp.broadcast_to(sc_even, (8, wide))
    so = jnp.broadcast_to(sc_odd, (8, wide))
    scores = [shifted(value, n) for n in (-1, 0, 1) for value in (se, so)]
    w8 = packed_weights(start, total, rows)
    score = w8[0] * scores[0]
    for n in range(1, 6):
        score = score + w8[n] * scores[n]
    expo = jnp.exp(score)
    probs = expo / over_blocks(expo)
    a = [0.5 * jnp.sum(probs * w, axis=0, keepdims=True) for w in w8]
    probs_s[...] = probs
    for n in range(6):
        w8_s[n] = w8[n]
    near = [shifted(cat, n) for n in (-2, -1, 0, 1, 2)]
    idm = [near[0][1:2], near[1][0:1], near[1][1:2], near[2][0:1], near[2][1:2],
           near[3][0:1], near[3][1:2], near[4][0:1]]
    for j in range(8):
        idm_s[j] = jnp.broadcast_to(idm[j], (8, rows))
    for o in range(6):
        a_s[o] = jnp.broadcast_to(a[o], (8, rows))

    def spread_rows(n):
        v = lax.broadcasted_iota(jnp.int32, (8, rows), 0) + n
        hits = [idm_s[j] == v for j in range(8)]
        accs = []
        for k in range(3):
            acc = jnp.where(hits[k], a_s[0], 0.0)
            for o in range(1, 6):
                acc = acc + jnp.where(hits[o + k], a_s[o], 0.0)
            accs.append(acc)
        return accs

    def spread_in(n, carry):
        at = pl.ds(pl.multiple_of(n * BLOCK, BLOCK), BLOCK)
        top, low = spread_rows(n * BLOCK), spread_rows(n * BLOCK + 8)
        for k in range(3):
            wt[k, at, :] = jnp.concatenate([top[k], low[k]], axis=0).astype(BF16)
        return carry

    lax.fori_loop(0, vocab // BLOCK, spread_in, 0, unroll=2)
    for k in range(3):
        wcat[:, k * vocab : (k + 1) * vocab] = wt[k].astype(F32).T.astype(BF16)

    lanes[...] = jnp.zeros_like(lanes)

    def pool(c, carry):
        at = pl.ds(pl.multiple_of(c * TILE, TILE), TILE)
        part = mm(wcat[...], tk[:, at], NN)
        pooled[:, at] = part
        pb[:, at] = part.astype(BF16)
        square = part * part
        lanes[...] += square[:, 0:128] + square[:, 128:256]
        return carry

    lax.fori_loop(0, chans // TILE, pool, 0)
    x1_own[...] = jnp.broadcast_to(jnp.sum(lanes[...].T, axis=0, keepdims=True), (8, rows))
    put_1 = remote(x1_own, x1_in, s_core.at[1], r_core.at[1], (d, s, 1 - t))
    put_1.start()
    lax.fori_loop(split_at, chans // TILE, pull_back, 0)
    put_1.wait()
    scale = lax.rsqrt((x1_own[...] + x1_in[...]) / D + EPS)
    scale_c = scale.T[:, 0:1]

    def product(c):
        at = pl.ds(c * TILE, TILE)
        normed = (pooled[:, at] * scale_c * gain_ref[:, at]).astype(BF16)
        q[at, :] = mm(normed, g[...], TN).astype(BF16)

    bit1, bit2 = (x, y), (y, x)
    near1 = ((x_near, s, t), (y_near, s, t))
    near2 = ((y_near, s, t), (x_near, s, t))

    def q_rows(h, first, second):
        return pl.ds(pl.multiple_of(h * half + first * quarter + second * eighth, BLOCK), eighth)

    p1, done = {}, 0
    for h in range(2):
        while done * TILE < (h + 1) * half:
            product(done)
            done += 1
        for part in range(2):
            second = bit2[h] if part else 1 - bit2[h]
            p1[h, part] = remote(
                q.at[q_rows(h, 1 - bit1[h], second)], r1.at[h, part],
                s_p1.at[h, part], r_p1.at[h, part], near1[h],
            )
        p1[h, 0].start()
    for c in range(done, chans // TILE):
        at = pl.ds(c * TILE, TILE)
        normed = (pooled[:, at] * scale_c * gain_ref[:, at]).astype(BF16)
        whole = mm(normed, g[...], TN).astype(BF16)
        for j in range(n_seq):
            late[j, (c - done) * TILE : (c - done + 1) * TILE] = whole[:, j * cols : (j + 1) * cols]
    z_first = []
    for e, ss in enumerate(seq_peers):
        z_first.append(remote(late.at[ss], zq.at[e], s_zq.at[e], r_zq.at[e], (d, ss, t)))
        z_first[-1].start()

    lanes[...] = jnp.zeros_like(lanes)

    def inner_in(c, carry):
        at = pl.ds(pl.multiple_of(c * TILE, TILE), TILE)
        inner = pooled[:, at] * (ng[:, at] * gain_ref[:, at])
        lanes[...] += inner[:, 0:128] + inner[:, 128:256]
        return carry

    lax.fori_loop(0, chans // TILE, inner_in, 0)
    found = []
    for source in (gb, pb):
        rr[...] = mm(tk[...], source[...], NT)

        def select(n, accs):
            at = pl.multiple_of(n * 8, 8)
            v = lax.broadcasted_iota(jnp.int32, (8, rows), 0) + n * 8
            accs = list(accs)
            lines = [rr[pl.ds(k * vocab + at, 8), :] for k in range(3)]
            for j in range(8):
                hit = idm_s[j] == v
                for k in range(3):
                    if 0 <= j - k < 6:
                        accs[j - k] = accs[j - k] + jnp.where(hit, lines[k], 0.0)
            return tuple(accs)

        sums = tuple(jnp.zeros((8, rows), F32) for o in range(6))
        sums = lax.fori_loop(0, vocab // 8, select, sums, unroll=2)
        found += [jnp.sum(acc, axis=0, keepdims=True) for acc in sums]
    found.append(jnp.sum(lanes[...].T, axis=0, keepdims=True))
    found.append(jnp.zeros((3, rows), F32))
    x2_own[...] = jnp.concatenate(found, axis=0)
    put_2 = remote(x2_own, x2_in, s_core.at[2], r_core.at[2], (d, s, 1 - t))
    put_2.start()
    for h in range(2):
        p1[h, 0].wait_send()
        p1[h, 1].start()

    p2 = {}
    for h in range(2):
        p1[h, 0].wait_recv()
        rows_h = q_rows(h, bit1[h], 1 - bit2[h])
        for e in range(n_seq):
            at = pl.ds(pl.multiple_of((s + e + 1) % n_seq * cols, 128), cols)
            s2[h, e] = (q[rows_h, at].astype(F32) + r1[h, 0, :, at].astype(F32)).astype(BF16)
            p2[h, e] = remote(
                s2.at[h, e], r2.at[h, e], s_p2.at[h, e], r_p2.at[h, e], near2[h]
            )
            p2[h, e].start()

    put_2.wait()
    sums = x2_own[...] + x2_in[...]
    pull = scale[0:1] * scale[0:1] * scale[0:1] * (sums[12:13] / D)
    w8 = [w8_s[n] for n in range(6)]
    probs = probs_s[...]
    pgrad = None
    for o in range(6):
        term = w8[o] * (scale[0:1] * sums[o : o + 1] - pull * sums[o + 6 : o + 7])
        pgrad = term if pgrad is None else pgrad + term
    pgrad = 0.5 * pgrad
    sgrad = probs * (pgrad - over_blocks(probs * pgrad))
    ds = [jnp.sum(sgrad * w, axis=0, keepdims=True) for w in w8]

    for o in range(6):
        a_s[o] = jnp.broadcast_to(ds[o], (8, rows))

    def count_in(n, carry):
        at = pl.ds(pl.multiple_of(n * 8, 8), 8)
        accs = spread_rows(n * 8)
        for k in range(3):
            fold = accs[k][:, 0:128]
            for n in range(1, rows // 128):
                fold = fold + accs[k][:, n * 128 : (n + 1) * 128]
            hist[k, at, :] = fold
        return carry

    lax.fori_loop(0, vocab // 8, count_in, 0, unroll=2)
    for k in range(3):
        hist[k] = jnp.broadcast_to(jnp.sum(hist[k], axis=1, keepdims=True), (vocab, 128))
    pull_c = jnp.broadcast_to(pull, (8, rows)).T[:, 0:1]

    def table_step(c, carry):
        at = pl.ds(pl.multiple_of(c * TILE, TILE), TILE)
        tab = table_ref[:, at].astype(F32)
        cw, sw, gain = cw_ref[:, at], sw_ref[:, at], gain_ref[:, at]
        ngc, pc = ng[:, at], pooled[:, at]
        scaled = ngc * scale_c
        gain_term = jnp.sum(scaled * pc, axis=0, keepdims=True)
        pg = (scaled * gain - pull_c * pc).astype(BF16)
        whole, outs, score = None, [], None
        for k in range(3):
            hist_k = hist[k][:, 0:1]
            full = mm(wt[k], pg, NN) + hist_k * sw
            term = cw[k : k + 1] * full
            whole = term if whole is None else whole + term
            outs.append(jnp.sum(full * tab, axis=0, keepdims=True))
            term = cw[k : k + 1] * jnp.sum(hist_k * tab, axis=0, keepdims=True)
            score = term if score is None else score + term
        tb[:, at] = whole.astype(BF16)
        sm[:, at] = jnp.concatenate(outs + [score, gain_term, jnp.zeros((3, TILE), F32)], axis=0)
        return carry

    lax.fori_loop(0, chans // TILE, table_step, 0)

    t_rs, sm_z = {}, []
    turns = [(s + e + 1) % n_seq for e in range(n_seq)]
    chunk = chans // n_seq

    def part_of(j):
        return pl.ds(pl.multiple_of(j * chunk, 128), chunk)

    def send_table(e):
        for n, dd in enumerate(dp_peers):
            block = tb.at[pl.ds(pl.multiple_of(dd * t_dp + turns[e] * t_seq, t_seq), t_seq)]
            t_rs[e, n] = remote(block, tr.at[e, n], s_trs.at[e, n], r_trs.at[e, n], (dd, s, t))
            t_rs[e, n].start()

    send_table(0)
    for e, ss in enumerate(seq_peers):
        sm_z.append(
            remote(sm.at[:, part_of(ss)], sz.at[e], s_sm.at[e], r_sm.at[e], (d, ss, t))
        )
        sm_z[-1].start()

    for h in range(2):
        p1[h, 1].wait_recv()
    q_z = {}
    for e, j in enumerate(turns):
        at = pl.ds(pl.multiple_of(j * cols, 128), cols)
        for h in range(2):
            p2[h, e].wait_recv()
            rows_h = q_rows(h, bit1[h], bit2[h])
            block = q[rows_h, at].astype(F32) + r1[h, 1, :, at].astype(F32)
            block = block + r2[h, e].astype(F32)
            if e < n_seq - 1:
                zb[h, e] = block.astype(BF16)
                q_z[h, e] = remote(
                    zb.at[h, e], zr.at[h, e], s_z.at[h, e], r_z.at[h, e], (d, j, t)
                )
                q_z[h, e].start()
            else:
                own_z[h] = block
        if e % 2:
            send_table(e // 2 + 1)
    for e in range(n_seq // 2 + 1, n_seq):
        send_table(e)

    for copy in z_first:
        copy.wait_recv()
    block = late[s].astype(F32)
    for e in range(n_seq - 1):
        block = block + zq[e].astype(F32)
    zs[...] = block.astype(BF16)
    z_rs = []
    for n, dd in enumerate(dp_peers):
        rows_n = pl.ds(pl.multiple_of(dd * step_z, BLOCK), step_z)
        z_rs.append(remote(zs.at[rows_n], zd.at[n], s_zd.at[n], r_zd.at[n], (dd, s, t)))
        z_rs[-1].start()

    t_z = {}
    for e, j in enumerate(turns):
        acc = tb[pl.ds(pl.multiple_of(d * t_dp + j * t_seq, t_seq), t_seq), :].astype(F32)
        for n in range(3):
            t_rs[e, n].wait_recv()
            acc = acc + tr[e, n].astype(F32)
        if e < n_seq - 1:
            ts[e] = acc.astype(BF16)
            t_z[e] = remote(ts.at[e], tz.at[e], s_tz.at[e], r_tz.at[e], (d, j, t))
            t_z[e].start()
        else:
            own_t[...] = acc

    acc = sm[:, part_of(s)]
    for e, copy in enumerate(sm_z):
        copy.wait_recv()
        acc = acc + sz[e]
    sd[d] = acc
    sm_d = []
    for n, dd in enumerate(dp_peers):
        sm_d.append(remote(sd.at[d], sd.at[d], s_sm.at[3 + n], r_sm.at[3 + n], (dd, s, t)))
        sm_d[-1].start()

    ag = []

    def share(out, rows_of, send, recv, via=None):
        targets = dp_peers if via is None else dp_peers[:2]
        copies = []
        for n, dd in enumerate(targets):
            mine = out.at[rows_of(d)]
            copies.append(remote(mine, mine, send.at[n], recv.at[n], (dd, s, t)))
            copies[-1].start()
        ag.extend(copy for n, copy in enumerate(copies) if n != via)
        if via is None:
            return None

        def relay():
            copies[via].wait_recv()
            passed.append(copies[via])
            theirs = out.at[rows_of(dp_peers[via])]
            ag.append(
                remote(theirs, theirs, send.at[2], recv.at[2], (dp_peers[1 - via], s, t))
            )
            ag[-1].start()

        return relay

    passed = []

    block = zs[pl.ds(pl.multiple_of(d * step_z, BLOCK), step_z), :].astype(F32)
    for n in range(3):
        z_rs[n].wait_recv()
        block = block + zd[n].astype(F32)
    def late_rows(dd):
        return pl.ds(pl.multiple_of(first_z + dd * step_z, BLOCK), step_z)

    query_ref[late_rows(d), :] = block.astype(BF16)
    share(query_ref, late_rows, s_ag.at[2], r_ag.at[2])

    relays = []
    for h in range(2):
        block = own_z[h]
        for e in range(n_seq - 1):
            q_z[h, e].wait_recv()
            block = block + zr[h, e].astype(F32)

        def early_rows(dd, h=h):
            bits = (dd % 2, dd // 2)
            return q_rows(h, bits[h], bits[1 - h])

        query_ref[early_rows(d), :] = block.astype(BF16)
        relays.append(share(query_ref, early_rows, s_ag.at[h], r_ag.at[h], h))

    acc = own_t[...]
    for e in range(n_seq - 1):
        t_z[e].wait_recv()
        acc = acc + tz[e].astype(F32)

    def table_rows(j):
        return lambda dd: pl.ds(pl.multiple_of(dd * t_dp + j * t_seq, t_seq), t_seq)

    mine = table_rows(s)(d)
    tab_ref[mine, :] = acc.astype(BF16)
    t_back = []
    for e, ss in enumerate(seq_peers):
        t_back.append(
            remote(tab_ref.at[mine], tab_ref.at[mine], s_tb.at[e], r_tb.at[e], (d, ss, t))
        )
        t_back[-1].start()
    late_relay = share(tab_ref, table_rows(s), s_ta.at[n_seq - 1], r_ta.at[n_seq - 1], 0)
    for copy in sm_d:
        copy.wait_recv()
    small_ref[:, part_of(s)] = (sd[0] + sd[1]) + (sd[2] + sd[3])
    for e, ss in enumerate(seq_peers):
        block = small_ref.at[:, part_of(s)]
        sm_d.append(remote(block, block, s_sm.at[6 + e], r_sm.at[6 + e], (d, ss, t)))
        sm_d[-1].start()
    for e in range(n_seq - 1):
        t_back[e].wait_recv()
        share(tab_ref, table_rows((s + n_seq - 1 - e) % n_seq), s_ta.at[e], r_ta.at[e])
        if e < 2:
            relays.pop(0)()
    late_relay()

    for copy in sm_d[3:] + ag:
        copy.wait_recv()
    for h in range(2):
        p1[h, 1].wait_send()
    for group in (p2, q_z, t_rs, t_z):
        for copy in group.values():
            copy.wait_send()
    for copy in z_first + z_rs + t_back + sm_z + sm_d + ag + passed:
        copy.wait_send()


def finish_kernel(tab_ref, small_ref, query_ref, tab_out, conv_out, score_out, gain_out, query_out):
    conv_out[...] = small_ref[0:3]
    score_out[...] = small_ref[3:4]
    gain_out[...] = small_ref[4:5]
    tab_out[...] = tab_ref[...]
    query_out[...] = query_ref[...]


def pad8(value):
    return jnp.concatenate([value, jnp.zeros((8 - value.shape[0], value.shape[1]), F32)], axis=0)


def sum_parts(value):
    return value[0:8] + value[8:16] + value[16:24]


def fused_body(
    byte_ids, pad_lengths, table, conv_weight, score_weight, norm_gain, query_weight, query_grad
):
    count = byte_ids.shape[1]
    rows = count // 2
    vocab, chans = table.shape
    width = query_grad.shape[2]
    n_seq = lax.axis_size("seq")
    cols = width // n_seq
    first_z = 3 * chans // 4
    part, t_dp = first_z // 8, vocab // 4
    t_seq, step_z, others = t_dp // n_seq, (chans - first_z) // 4, n_seq - 1
    vm = pl.BlockSpec(memory_space=pltpu.VMEM)
    sm = pl.BlockSpec(memory_space=pltpu.SMEM)
    hbm = pl.BlockSpec(memory_space=pl.ANY)
    V, DMA = pltpu.VMEM, pltpu.SemaphoreType.DMA
    tab, small, query = pl.pallas_call(
        fused_kernel,
        out_shape=(V((vocab, chans), BF16), V((8, chans), F32), V((chans, cols), BF16)),
        in_specs=[sm, vm, hbm] + [vm] * 3 + [hbm] * 2,
        out_specs=(vm,) * 3,
        scratch_shapes=[
            V((vocab, chans), BF16),
            V((chans, width), BF16), V((rows, width), BF16), V((3 * vocab, chans), BF16),
            V((3, vocab, rows), BF16), V((rows, 3 * vocab), BF16), V((rows, chans), F32),
            V((rows, chans), F32), V((rows, chans), BF16), V((rows, chans), BF16),
            V((first_z, width), BF16), V((8, 8, rows), jnp.int32), V((6, 8, rows), F32),
            V((6, 8, rows), F32), V((8, rows), F32), V((3, vocab, 128), F32),
            V((3 * vocab, rows), F32), V((rows, 128), F32),
            V((8, vocab), F32), V((8, vocab), F32), V((2, 1, 128), jnp.int32),
            V((8, rows), F32), V((8, rows), F32), V((16, rows), F32), V((16, rows), F32),
            V((2, 2, part, width), BF16), V((2, n_seq, part, cols), BF16), V((2, n_seq, part, cols), BF16),
            V((2, others, part, cols), BF16), V((2, others, part, cols), BF16),
            V((2, part, cols), F32), V((n_seq, chans - first_z, cols), BF16), V((others, chans - first_z, cols), BF16),
            V((chans - first_z, cols), BF16), V((3, step_z, cols), BF16),
            V((vocab, chans), BF16), V((n_seq, 3, t_seq, chans), BF16),
            V((others, t_seq, chans), BF16), V((others, t_seq, chans), BF16),
            V((t_seq, chans), F32), V((8, chans), F32), V((others, 8, chans // n_seq), F32),
            V((4, 8, chans // n_seq), F32),
            DMA((3,)), DMA((2,)), DMA((2,)), DMA((3,)), DMA((3,)),
            DMA((2, 2)), DMA((2, 2)), DMA((2, n_seq)), DMA((2, n_seq)),
            DMA((2, others)), DMA((2, others)), DMA((3, 3)), DMA((3, 3)),
            DMA((others,)), DMA((others,)), DMA((3,)), DMA((3,)),
            DMA((n_seq, 3)), DMA((n_seq, 3)), DMA((others,)), DMA((others,)),
            DMA((others,)), DMA((others,)), DMA((n_seq, 3)), DMA((n_seq, 3)),
            DMA((9,)), DMA((9,)),
        ],
        compiler_params=pltpu.CompilerParams(collective_id=0, has_side_effects=True),
        name="fused",
    )(
        pad_lengths, byte_ids, table, conv_weight, score_weight[None, :], norm_gain[None, :],
        query_weight, query_grad[0],
    )
    return pl.pallas_call(
        finish_kernel,
        out_shape=(
            jax.ShapeDtypeStruct((vocab, chans), BF16),
            jax.ShapeDtypeStruct((3, chans), F32),
            jax.ShapeDtypeStruct((1, chans), F32),
            jax.ShapeDtypeStruct((1, chans), F32),
            jax.ShapeDtypeStruct((chans, cols), BF16),
        ),
        in_specs=[vm] * 3,
        out_specs=(vm,) * 5,
        name="finish",
    )(*(pltpu.with_memory_space_constraint(part, pltpu.VMEM) for part in (tab, small, query)))


def fused_outer(*args):
    tab, conv, score, gain, query = fused_body(*args)
    return (tab, conv, score.reshape(-1), gain.reshape(-1), query)


def fits(mesh):
    return mesh.shape["dp"] == 4 and mesh.shape["seq"] == 4 and mesh.shape["tensor"] == 2


def solution(mesh):
    return jax.shard_map(
        fused_outer if fits(mesh) else body,
        mesh=mesh,
        in_specs=(
            P("dp", "seq"),
            P("dp"),
            P(None, "tensor"),
            P(None, "tensor"),
            P("tensor"),
            P("tensor"),
            P("tensor", None),
            P("dp", "seq", None),
        ),
        out_specs=(
            P(None, "tensor"),
            P(None, "tensor"),
            P("tensor"),
            P("tensor"),
            P("tensor", "seq"),
        ),
        check_vma=False,
    )
```

```python
import functools

import jax
import jax.numpy as jnp
from jax import lax
from jax.experimental import pallas as pl
from jax.experimental.pallas import tpu as pltpu
from jax.sharding import PartitionSpec as P

D = 2048
EPS = 1e-06
F32 = jnp.float32
BF16 = jnp.bfloat16
OFFS = range(-2, 4)
CHUNK = 256

NN = (((1,), (0,)), ((), ()))
NT = (((1,), (1,)), ((), ()))
TN = (((0,), (0,)), ((), ()))


def mm(lhs, rhs, dims):
    return lax.dot_general(lhs, rhs, dims, preferred_element_type=F32)


def block_weights(start, total, rows):
    i = lax.broadcasted_iota(jnp.int32, (1, rows), 1)
    even = (i % 2) == 0
    inside = {o: (start + 2 * i + o >= 0) & (start + 2 * i + o < total) for o in OFFS}
    table = []
    for b in range(4):
        for p in range(2):
            row = {}
            for o in OFFS:
                if b == 0:
                    if o == p:
                        row[o] = jnp.where(inside[o], 1.0, 0.0)
                elif b == 1:
                    if o in (0, 1):
                        row[o] = jnp.where(inside[o], 0.5, 0.0)
                elif b == 3:
                    if o in (0, 1):
                        row[o] = jnp.where(inside[o], 0.25, 0.0)
                    else:
                        row[o] = jnp.where(inside[o] & (even if o > 1 else ~even), 0.25, 0.0)
                else:
                    d = o - p
                    if -2 <= d <= 2:
                        r = (start + 2 * i + p) % 3
                        row[o] = jnp.where(inside[o] & (r >= -d) & (r <= 2 - d), 1.0 / 3.0, 0.0)
            table.append(row)
    return table


def spread(idm, rows_of, tap):
    rows = idm.shape[1]
    v = lax.broadcasted_iota(jnp.int32, (256, rows), 0)
    acc = None
    for o in OFFS:
        at = o + tap + 2
        term = jnp.where(idm[at : at + 1, :] == v, rows_of[o], 0.0)
        acc = term if acc is None else acc + term
    return acc


def forward_kernel(
    pos_ref, idm_ref, p_ref, table_ref, cw_ref, gain_ref, wq_ref, g_ref,
    pooled_ref, ng_ref, wt_ref, sums_ref, rows_ref, grads_ref,
    wh, wl, r1, r2, sq, rd,
):
    start, limit, total = pos_ref[0], pos_ref[1], pos_ref[2]
    rows = idm_ref.shape[1]
    chans = table_ref.shape[1]
    idm = idm_ref[...]
    v = lax.broadcasted_iota(jnp.int32, (256, rows), 0)
    p = p_ref[...]
    hi = p.astype(BF16)
    rest = p - hi.astype(F32)
    mid = rest.astype(BF16)
    low = (rest - mid.astype(F32)).astype(BF16)
    p3 = jnp.concatenate([hi.astype(F32), mid.astype(F32), low.astype(F32)], axis=0).astype(BF16)
    picks = []
    for j in range(8):
        hot = jnp.where(idm[j : j + 1, :] == v, 1.0, 0.0).astype(BF16)
        g = mm(p3, hot, NN)
        picks.append(g[0:8] + g[8:16] + g[16:24])
    s = {o: picks[o + 2][0:1] + picks[o + 3][1:2] + picks[o + 4][2:3] for o in OFFS}
    weights = block_weights(start, total, rows)
    expo = []
    for row in weights:
        score = None
        for o in row:
            score = row[o] * s[o] if score is None else score + row[o] * s[o]
        expo.append(jnp.exp(score))
    probs = []
    for n in range(8):
        whole = expo[n % 2] + expo[2 + n % 2] + expo[4 + n % 2] + expo[6 + n % 2]
        probs.append(expo[n] / whole)
    a = {}
    for o in OFFS:
        acc = None
        for n in range(8):
            if o in weights[n]:
                term = probs[n] * weights[n][o]
                acc = term if acc is None else acc + term
        a[o] = 0.5 * acc
    rows_ref[...] = jnp.concatenate(probs, axis=0)
    for k in range(3):
        w = spread(idm, a, k)
        wt_ref[k] = w.astype(BF16)
        wf = w.T
        top = wf.astype(BF16)
        wh[k] = top
        wl[k] = (wf - top.astype(F32)).astype(BF16)
    keep = (start + 2 * lax.broadcasted_iota(jnp.int32, g_ref.shape, 0)) < limit
    grads_ref[...] = jnp.where(keep, g_ref[...].astype(F32), 0.0).astype(BF16)
    r1[...] = jnp.zeros_like(r1)
    r2[...] = jnp.zeros_like(r2)
    sq[...] = jnp.zeros_like(sq)
    rd[...] = jnp.zeros_like(rd)

    def step(c, carry):
        at = pl.ds(pl.multiple_of(c * CHUNK, CHUNK), CHUNK)
        tab = table_ref[:, at]
        cw = cw_ref[:, at]
        ng = mm(grads_ref[...], wq_ref[at, :], NT)
        pooled = None
        for k in range(3):
            part = cw[k : k + 1] * (mm(wh[k], tab, NN) + mm(wl[k], tab, NN))
            pooled = part if pooled is None else pooled + part
        pooled_ref[:, at] = pooled
        ng_ref[:, at] = ng
        gained = ng * gain_ref[:, at]
        square = pooled * pooled
        inner = pooled * gained
        sq[...] += square[:, 0:128] + square[:, 128:256]
        rd[...] += inner[:, 0:128] + inner[:, 128:256]
        gb = gained.astype(BF16)
        pb = pooled.astype(BF16)
        for k in range(3):
            tk = (tab.astype(F32) * cw[k : k + 1]).astype(BF16)
            r1[k] += mm(tk, gb, NT)
            r2[k] += mm(tk, pb, NT)
        return carry

    lax.fori_loop(0, chans // CHUNK, step, 0)
    out = []
    for r in (r1, r2):
        for o in OFFS:
            acc = None
            for k in range(3):
                at = o + k + 2
                term = jnp.where(idm[at : at + 1, :] == v, r[k], 0.0)
                acc = term if acc is None else acc + term
            out.append(jnp.sum(acc, axis=0, keepdims=True))
    out.append(jnp.sum(sq[...].T, axis=0, keepdims=True))
    out.append(jnp.sum(rd[...].T, axis=0, keepdims=True))
    out.append(jnp.zeros((2, rows), F32))
    sums_ref[...] = jnp.concatenate(out, axis=0)


def backward_kernel(
    pos_ref, idm_ref, sums_ref, rows_ref, table_ref, cw_ref, sw_ref, gain_ref,
    pooled_ref, ng_ref, wt_ref, grads_ref,
    query_ref, tab_ref, small_ref,
):
    start, total = pos_ref[0], pos_ref[2]
    rows = idm_ref.shape[1]
    chans = table_ref.shape[1]
    idm = idm_ref[...]
    sums = sums_ref[...]
    probs = rows_ref[...]
    square, inner = sums[12:13], sums[13:14]
    scale = lax.rsqrt(square / D + EPS)
    pull = scale * scale * scale * (inner / D)
    q = {o: scale * sums[o + 2 : o + 3] - pull * sums[o + 8 : o + 9] for o in OFFS}
    weights = block_weights(start, total, rows)
    pgrad = []
    for row in weights:
        acc = None
        for o in row:
            acc = row[o] * q[o] if acc is None else acc + row[o] * q[o]
        pgrad.append(0.5 * acc)
    sgrad = []
    for n in range(8):
        mean = None
        for m in range(n % 2, 8, 2):
            term = probs[m : m + 1] * pgrad[m]
            mean = term if mean is None else mean + term
        sgrad.append(probs[n : n + 1] * (pgrad[n] - mean))
    ds = {}
    for o in OFFS:
        acc = None
        for n in range(8):
            if o in weights[n]:
                term = sgrad[n] * weights[n][o]
                acc = term if acc is None else acc + term
        ds[o] = acc
    hist = [jnp.sum(spread(idm, ds, k), axis=1, keepdims=True) for k in range(3)]
    cols = jnp.concatenate([scale, pull, jnp.zeros((6, rows), F32)], axis=0).T
    scale_c, pull_c = cols[:, 0:1], cols[:, 1:2]

    for c in range(chans // CHUNK):
        at = pl.ds(c * CHUNK, CHUNK)
        tab = table_ref[:, at].astype(F32)
        cw = cw_ref[:, at]
        sw = sw_ref[:, at]
        gain = gain_ref[:, at]
        ps = pooled_ref[:, at] * scale_c
        ng = ng_ref[:, at]
        gain_term = jnp.sum(ng * ps, axis=0, keepdims=True)
        normed = (ps * gain).astype(BF16)
        query_ref[at, :] = mm(normed, grads_ref[...], TN).astype(query_ref.dtype)
        pg = (ng * gain * scale_c - pull_c * pooled_ref[:, at]).astype(BF16)
        total_t = None
        outs = []
        score = None
        for k in range(3):
            full = mm(wt_ref[k], pg, NN) + hist[k] * sw
            term = cw[k : k + 1] * full
            total_t = term if total_t is None else total_t + term
            outs.append(jnp.sum(full * tab, axis=0, keepdims=True))
            term = cw[k : k + 1] * jnp.sum(hist[k] * tab, axis=0, keepdims=True)
            score = term if score is None else score + term
        tab_ref[:, at] = total_t.astype(tab_ref.dtype)
        small_ref[:, at] = jnp.concatenate(
            outs + [score, gain_term, jnp.zeros((3, CHUNK), F32)], axis=0
        )


def body(
    byte_ids, pad_lengths, table, conv_weight, score_weight, norm_gain, query_weight, query_grad
):
    ids = byte_ids[0]
    count = ids.shape[0]
    rows = count // 2
    vocab, chans = table.shape
    width = query_grad.shape[2]
    n_seq = lax.axis_size("seq")
    total = count * n_seq
    start = lax.axis_index("seq") * count
    limit = total - pad_lengths[0]
    ends = n_seq - 1
    up = [(i, i + 1) for i in range(ends)]
    down = [(i + 1, i) for i in range(ends)]
    ids_ext = jnp.concatenate(
        [lax.ppermute(ids[count - 3 :], "seq", up), ids, lax.ppermute(ids[:3], "seq", down)]
    )
    pos_e = start + jnp.arange(-3, count + 3, dtype=jnp.int32)
    ids_ext = jnp.where((pos_e >= 0) & (pos_e < limit), ids_ext, -1)
    halves = ids_ext.reshape(rows + 3, 2).T
    idm = jnp.stack([halves[j % 2, j // 2 : j // 2 + rows] for j in range(8)])
    pos = jnp.stack([start, limit, jnp.full_like(start, total)]).astype(jnp.int32)

    part = jnp.dot(
        conv_weight * score_weight, table.astype(F32).T, precision=lax.Precision.HIGHEST
    )
    p = jnp.pad(lax.psum(part, "tensor"), ((0, 5), (0, 0)))

    vm = pl.BlockSpec(memory_space=pltpu.VMEM)
    sm = pl.BlockSpec(memory_space=pltpu.SMEM)
    sw = score_weight[None, :]
    gain = norm_gain[None, :]
    pooled, ng, wt, sums, probs, grads = pl.pallas_call(
        forward_kernel,
        out_shape=(
            jax.ShapeDtypeStruct((rows, chans), F32),
            jax.ShapeDtypeStruct((rows, chans), F32),
            jax.ShapeDtypeStruct((3, vocab, rows), BF16),
            jax.ShapeDtypeStruct((16, rows), F32),
            jax.ShapeDtypeStruct((8, rows), F32),
            jax.ShapeDtypeStruct((rows, width), BF16),
        ),
        in_specs=[sm] + [vm] * 7,
        out_specs=(vm,) * 6,
        scratch_shapes=[
            pltpu.VMEM((3, rows, vocab), BF16),
            pltpu.VMEM((3, rows, vocab), BF16),
            pltpu.VMEM((3, vocab, rows), F32),
            pltpu.VMEM((3, vocab, rows), F32),
            pltpu.VMEM((rows, 128), F32),
            pltpu.VMEM((rows, 128), F32),
        ],
        name="forward",
    )(pos, idm, p, table, conv_weight, gain, query_weight, query_grad[0])
    sums = lax.psum(sums, "tensor")
    query, tab, small = pl.pallas_call(
        backward_kernel,
        out_shape=(
            jax.ShapeDtypeStruct((chans, width), BF16),
            jax.ShapeDtypeStruct((vocab, chans), BF16),
            jax.ShapeDtypeStruct((8, chans), F32),
        ),
        in_specs=[sm] + [vm] * 11,
        out_specs=(vm,) * 3,
        name="backward",
    )(pos, idm, sums, probs, table, conv_weight, sw, gain, pooled, ng, wt, grads)

    share = lax.psum_scatter(query, "seq", scatter_dimension=1, tiled=True)
    query_out = lax.psum(share, "dp")
    tab_out = lax.psum(tab, ("dp", "seq"))
    small_out = lax.psum(small, ("dp", "seq"))
    return (tab_out, small_out[0:3], small_out[3], small_out[4], query_out)


MESH = pl.DeviceIdType.MESH
BLOCK = 16
TILE = 256


def stacked(value):
    hi = value.astype(BF16)
    rest = value - hi.astype(F32)
    mid = rest.astype(BF16)
    low = (rest - mid.astype(F32)).astype(BF16)
    return jnp.concatenate([hi.astype(F32), mid.astype(F32), low.astype(F32)], axis=0).astype(BF16)


def packed_weights(start, total, rows):
    n = lax.broadcasted_iota(jnp.int32, (8, rows), 0)
    i = lax.broadcasted_iota(jnp.int32, (8, rows), 1)
    b, p = n // 2, n % 2
    even = (i % 2) == 0
    r = (start + 2 * i + p) % 3
    table = []
    for o in OFFS:
        at = start + 2 * i + o
        inside = (at >= 0) & (at < total)
        d = o - p
        near = (d >= -2) & (d <= 2) & (r >= -d) & (r <= 2 - d)
        w = jnp.where((b == 2) & near, 1.0 / 3.0, 0.0)
        w = jnp.where((b == 0) & (p == o), 1.0, w)
        if o in (0, 1):
            w = jnp.where(b == 1, 0.5, w)
            w = jnp.where(b == 3, 0.25, w)
        else:
            w = jnp.where((b == 3) & (even if o > 1 else ~even), 0.25, w)
        table.append(jnp.where(inside, w, 0.0))
    return table


def over_blocks(value):
    return value + pltpu.roll(value, 2, 0) + pltpu.roll(value, 4, 0) + pltpu.roll(value, 6, 0)


def fused_kernel(
    pad_ref, ids_ref, table_hbm, cw_ref, sw_ref, gain_ref, wq_hbm, g_hbm,
    tab_ref, small_ref, query_ref,
    table_ref, wq, g, tk, wt, wcat, pooled, ng, gb, pb, q, idm_s, a_s, w8_s, probs_s, hist, rr, lanes,
    p_own, p_in, halo, x1_own, x1_in, x2_own, x2_in,
    r1, s2, r2, zb, zr, own_z, late, zq, zs, zd, tb, tr, ts, tz, own_t, sm, sz, sd,
    in_sem, s_halo, r_halo, s_core, r_core, s_p1, r_p1, s_p2, r_p2, s_z, r_z, s_ag, r_ag,
    s_zq, r_zq, s_zd, r_zd, s_trs, r_trs, s_tz, r_tz, s_tb, r_tb, s_ta, r_ta, s_ca, r_ca, s_sm, r_sm,
):
    d, s, t = lax.axis_index("dp"), lax.axis_index("seq"), lax.axis_index("tensor")
    n_seq = lax.axis_size("seq")
    x, y = d % 2, d // 2
    x_near = y * 2 + (1 - x)
    y_near = (1 - y) * 2 + x
    corner = (1 - y) * 2 + (1 - x)
    dp_peers = (x_near, y_near, corner)
    seq_peers = [(s + e) % n_seq for e in range(1, n_seq)]
    count = ids_ref.shape[1]
    rows = count // 2
    vocab, chans = table_ref.shape
    width = g.shape[1]
    total = count * n_seq
    start = s * count
    limit = total - pad_ref[0]
    first_z = 3 * chans // 4
    half, quarter, eighth = first_z // 2, first_z // 4, first_z // 8
    step_z = (chans - first_z) // 4
    cols = width // n_seq
    t_dp, t_seq = vocab // 4, vocab // 4 // n_seq

    def remote(src, dst, send, recv, to):
        return pltpu.make_async_remote_copy(
            src_ref=src, dst_ref=dst, send_sem=send, recv_sem=recv,
            device_id=to, device_id_type=MESH,
        )

    take_g = pltpu.make_async_copy(g_hbm, g, in_sem.at[0])
    take_w = pltpu.make_async_copy(wq_hbm, wq, in_sem.at[1])
    take_t = pltpu.make_async_copy(table_hbm, table_ref, in_sem.at[2])
    take_t.start()
    take_g.start()
    take_w.start()

    barrier = pltpu.get_barrier_semaphore()
    peers = [(dd, s, t) for dd in dp_peers] + [(d, ss, t) for ss in seq_peers] + [(d, s, 1 - t)]
    for peer in peers:
        pl.semaphore_signal(barrier, inc=1, device_id=peer, device_id_type=MESH)

    cs = cw_ref[...] * sw_ref[...]
    take_t.wait()
    p_own[...] = sum_parts(mm(stacked(pad8(cs)), table_ref[...], NT))
    pl.semaphore_wait(barrier, len(peers))

    put_p = remote(p_own, p_in, s_core.at[0], r_core.at[0], (d, s, 1 - t))
    put_p.start()
    to_left = remote(
        ids_ref.at[:, pl.ds(0, 128)], halo.at[1], s_halo.at[0], r_halo.at[1],
        (d, jnp.maximum(s - 1, 0), t),
    )
    to_right = remote(
        ids_ref.at[:, pl.ds(count - 128, 128)], halo.at[0], s_halo.at[1], r_halo.at[0],
        (d, jnp.minimum(s + 1, n_seq - 1), t),
    )

    @pl.when(s > 0)
    def _():
        to_left.start()

    @pl.when(s < n_seq - 1)
    def _():
        to_right.start()

    @pl.when(s == 0)
    def _():
        halo[0] = jnp.zeros((1, 128), jnp.int32)

    @pl.when(s == n_seq - 1)
    def _():
        halo[1] = jnp.zeros((1, 128), jnp.int32)

    for k in range(3):
        def spell(c, carry, k=k):
            at = pl.ds(pl.multiple_of(c * TILE, TILE), TILE)
            tk[k * vocab : (k + 1) * vocab, at] = (
                table_ref[:, at].astype(F32) * cw_ref[k : k + 1, at]
            ).astype(BF16)
            return carry

        lax.fori_loop(0, chans // TILE, spell, 0)
    take_g.wait()

    def mask(c, carry):
        at = pl.ds(pl.multiple_of(c * 64, 64), 64)
        i = lax.broadcasted_iota(jnp.int32, (64, width), 0) + c * 64
        g[at, :] = jnp.where(start + 2 * i < limit, g[at, :].astype(F32), 0.0).astype(BF16)
        return carry

    lax.fori_loop(0, rows // 64, mask, 0)
    take_w.wait()

    def pull_back(c, carry):
        at = pl.ds(pl.multiple_of(c * TILE, TILE), TILE)
        part = mm(g[...], wq[at, :], NT)
        ng[:, at] = part
        gb[:, at] = (part * gain_ref[:, at]).astype(BF16)
        return carry

    split_at = chans // TILE // 2
    lax.fori_loop(0, split_at, pull_back, 0)

    @pl.when(s > 0)
    def _():
        to_right.wait_recv()
        to_left.wait_send()

    @pl.when(s < n_seq - 1)
    def _():
        to_left.wait_recv()
        to_right.wait_send()

    put_p.wait()

    wide = rows + 128
    line = jnp.concatenate([halo[0], ids_ref[...], halo[1]], axis=1).astype(F32)
    pieces = wide // 128
    line = jnp.concatenate(
        [line[:, n * 256 : (n + 1) * 256] for n in range(pieces)]
        + [jnp.zeros((8 - pieces % 8, 256), F32)] * (pieces % 8 > 0),
        axis=0,
    )
    r = lax.broadcasted_iota(jnp.int32, (256, 256), 0)
    c = lax.broadcasted_iota(jnp.int32, (256, 256), 1)
    sift = jnp.where(r == jnp.where(c < 128, 2 * c, 2 * c - 255), 1.0, 0.0).astype(BF16)
    sifted = mm(line.astype(BF16), sift, NN)
    cat = jnp.concatenate(
        [
            jnp.concatenate([sifted[n : n + 1, p * 128 : (p + 1) * 128] for n in range(pieces)], axis=1)
            for p in range(2)
        ]
        + [jnp.zeros((6, wide), F32)],
        axis=0,
    ).astype(jnp.int32)
    lane = lax.broadcasted_iota(jnp.int32, cat.shape, 1)
    row = lax.broadcasted_iota(jnp.int32, cat.shape, 0)
    at_byte = start + 2 * (lane - 64) + row
    cat = jnp.where((at_byte >= 0) & (at_byte < limit) & (row < 2), cat, -1)

    def shifted(value, n):
        return pltpu.roll(value, wide - 64 - n, 1)[:, 0:rows]

    p3 = stacked(p_own[...] + p_in[...])
    v_wide = lax.broadcasted_iota(jnp.int32, (vocab, wide), 0)

    def picked(line):
        hot = jnp.where(line == v_wide, 1.0, 0.0).astype(BF16)
        return sum_parts(mm(p3, hot, NN))

    even, odd = picked(cat[0:1]), picked(cat[1:2])
    sc_even = pltpu.roll(odd, 1, 1)[0:1] + even[1:2] + odd[2:3]
    sc_odd = even[0:1] + odd[1:2] + pltpu.roll(even, wide - 1, 1)[2:3]
    se = jnp.broadcast_to(sc_even, (8, wide))
    so = jnp.broadcast_to(sc_odd, (8, wide))
    scores = [shifted(value, n) for n in (-1, 0, 1) for value in (se, so)]
    w8 = packed_weights(start, total, rows)
    score = w8[0] * scores[0]
    for n in range(1, 6):
        score = score + w8[n] * scores[n]
    expo = jnp.exp(score)
    probs = expo / over_blocks(expo)
    a = [0.5 * jnp.sum(probs * w, axis=0, keepdims=True) for w in w8]
    probs_s[...] = probs
    for n in range(6):
        w8_s[n] = w8[n]
    near = [shifted(cat, n) for n in (-2, -1, 0, 1, 2)]
    idm = [near[0][1:2], near[1][0:1], near[1][1:2], near[2][0:1], near[2][1:2],
           near[3][0:1], near[3][1:2], near[4][0:1]]
    for j in range(8):
        idm_s[j] = jnp.broadcast_to(idm[j], (8, rows))
    for o in range(6):
        a_s[o] = jnp.broadcast_to(a[o], (8, rows))

    def spread_rows(n):
        v = lax.broadcasted_iota(jnp.int32, (8, rows), 0) + n
        hits = [idm_s[j] == v for j in range(8)]
        accs = []
        for k in range(3):
            acc = jnp.where(hits[k], a_s[0], 0.0)
            for o in range(1, 6):
                acc = acc + jnp.where(hits[o + k], a_s[o], 0.0)
            accs.append(acc)
        return accs

    def spread_in(n, carry):
        at = pl.ds(pl.multiple_of(n * BLOCK, BLOCK), BLOCK)
        top, low = spread_rows(n * BLOCK), spread_rows(n * BLOCK + 8)
        for k in range(3):
            wt[k, at, :] = jnp.concatenate([top[k], low[k]], axis=0).astype(BF16)
        return carry

    lax.fori_loop(0, vocab // BLOCK, spread_in, 0, unroll=2)
    for k in range(3):
        wcat[:, k * vocab : (k + 1) * vocab] = wt[k].astype(F32).T.astype(BF16)

    lanes[...] = jnp.zeros_like(lanes)

    def pool(c, carry):
        at = pl.ds(pl.multiple_of(c * TILE, TILE), TILE)
        part = mm(wcat[...], tk[:, at], NN)
        pooled[:, at] = part
        pb[:, at] = part.astype(BF16)
        square = part * part
        lanes[...] += square[:, 0:128] + square[:, 128:256]
        return carry

    lax.fori_loop(0, chans // TILE, pool, 0)
    x1_own[...] = jnp.broadcast_to(jnp.sum(lanes[...].T, axis=0, keepdims=True), (8, rows))
    put_1 = remote(x1_own, x1_in, s_core.at[1], r_core.at[1], (d, s, 1 - t))
    put_1.start()
    lax.fori_loop(split_at, chans // TILE, pull_back, 0)
    put_1.wait()
    scale = lax.rsqrt((x1_own[...] + x1_in[...]) / D + EPS)
    scale_c = scale.T[:, 0:1]

    def product(c):
        at = pl.ds(c * TILE, TILE)
        normed = (pooled[:, at] * scale_c * gain_ref[:, at]).astype(BF16)
        q[at, :] = mm(normed, g[...], TN).astype(BF16)

    bit1, bit2 = (x, y), (y, x)
    near1 = ((x_near, s, t), (y_near, s, t))
    near2 = ((y_near, s, t), (x_near, s, t))

    def q_rows(h, first, second):
        return pl.ds(pl.multiple_of(h * half + first * quarter + second * eighth, BLOCK), eighth)

    p1, done = {}, 0
    for h in range(2):
        while done * TILE < (h + 1) * half:
            product(done)
            done += 1
        for part in range(2):
            second = bit2[h] if part else 1 - bit2[h]
            p1[h, part] = remote(
                q.at[q_rows(h, 1 - bit1[h], second)], r1.at[h, part],
                s_p1.at[h, part], r_p1.at[h, part], near1[h],
            )
        p1[h, 0].start()
    for c in range(done, chans // TILE):
        at = pl.ds(c * TILE, TILE)
        normed = (pooled[:, at] * scale_c * gain_ref[:, at]).astype(BF16)
        whole = mm(normed, g[...], TN).astype(BF16)
        for j in range(n_seq):
            late[j, (c - done) * TILE : (c - done + 1) * TILE] = whole[:, j * cols : (j + 1) * cols]
    z_first = []
    for e, ss in enumerate(seq_peers):
        z_first.append(remote(late.at[ss], zq.at[e], s_zq.at[e], r_zq.at[e], (d, ss, t)))
        z_first[-1].start()

    lanes[...] = jnp.zeros_like(lanes)

    def inner_in(c, carry):
        at = pl.ds(pl.multiple_of(c * TILE, TILE), TILE)
        inner = pooled[:, at] * (ng[:, at] * gain_ref[:, at])
        lanes[...] += inner[:, 0:128] + inner[:, 128:256]
        return carry

    lax.fori_loop(0, chans // TILE, inner_in, 0)
    found = []
    for source in (gb, pb):
        rr[...] = mm(tk[...], source[...], NT)

        def select(n, accs):
            at = pl.multiple_of(n * 8, 8)
            v = lax.broadcasted_iota(jnp.int32, (8, rows), 0) + n * 8
            accs = list(accs)
            lines = [rr[pl.ds(k * vocab + at, 8), :] for k in range(3)]
            for j in range(8):
                hit = idm_s[j] == v
                for k in range(3):
                    if 0 <= j - k < 6:
                        accs[j - k] = accs[j - k] + jnp.where(hit, lines[k], 0.0)
            return tuple(accs)

        sums = tuple(jnp.zeros((8, rows), F32) for o in range(6))
        sums = lax.fori_loop(0, vocab // 8, select, sums, unroll=2)
        found += [jnp.sum(acc, axis=0, keepdims=True) for acc in sums]
    found.append(jnp.sum(lanes[...].T, axis=0, keepdims=True))
    found.append(jnp.zeros((3, rows), F32))
    x2_own[...] = jnp.concatenate(found, axis=0)
    put_2 = remote(x2_own, x2_in, s_core.at[2], r_core.at[2], (d, s, 1 - t))
    put_2.start()
    for h in range(2):
        p1[h, 0].wait_send()
        p1[h, 1].start()

    p2 = {}
    for h in range(2):
        p1[h, 0].wait_recv()
        rows_h = q_rows(h, bit1[h], 1 - bit2[h])
        for e in range(n_seq):
            at = pl.ds(pl.multiple_of((s + e + 1) % n_seq * cols, 128), cols)
            s2[h, e] = (q[rows_h, at].astype(F32) + r1[h, 0, :, at].astype(F32)).astype(BF16)
            p2[h, e] = remote(
                s2.at[h, e], r2.at[h, e], s_p2.at[h, e], r_p2.at[h, e], near2[h]
            )
            p2[h, e].start()

    put_2.wait()
    sums = x2_own[...] + x2_in[...]
    pull = scale[0:1] * scale[0:1] * scale[0:1] * (sums[12:13] / D)
    w8 = [w8_s[n] for n in range(6)]
    probs = probs_s[...]
    pgrad = None
    for o in range(6):
        term = w8[o] * (scale[0:1] * sums[o : o + 1] - pull * sums[o + 6 : o + 7])
        pgrad = term if pgrad is None else pgrad + term
    pgrad = 0.5 * pgrad
    sgrad = probs * (pgrad - over_blocks(probs * pgrad))
    ds = [jnp.sum(sgrad * w, axis=0, keepdims=True) for w in w8]

    for o in range(6):
        a_s[o] = jnp.broadcast_to(ds[o], (8, rows))

    def count_in(n, carry):
        at = pl.ds(pl.multiple_of(n * 8, 8), 8)
        accs = spread_rows(n * 8)
        for k in range(3):
            fold = accs[k][:, 0:128]
            for n in range(1, rows // 128):
                fold = fold + accs[k][:, n * 128 : (n + 1) * 128]
            hist[k, at, :] = fold
        return carry

    lax.fori_loop(0, vocab // 8, count_in, 0, unroll=2)
    for k in range(3):
        hist[k] = jnp.broadcast_to(jnp.sum(hist[k], axis=1, keepdims=True), (vocab, 128))
    pull_c = jnp.broadcast_to(pull, (8, rows)).T[:, 0:1]

    def table_step(c, carry):
        at = pl.ds(pl.multiple_of(c * TILE, TILE), TILE)
        tab = table_ref[:, at].astype(F32)
        cw, sw, gain = cw_ref[:, at], sw_ref[:, at], gain_ref[:, at]
        ngc, pc = ng[:, at], pooled[:, at]
        scaled = ngc * scale_c
        gain_term = jnp.sum(scaled * pc, axis=0, keepdims=True)
        pg = (scaled * gain - pull_c * pc).astype(BF16)
        whole, outs, score = None, [], None
        for k in range(3):
            hist_k = hist[k][:, 0:1]
            full = mm(wt[k], pg, NN) + hist_k * sw
            term = cw[k : k + 1] * full
            whole = term if whole is None else whole + term
            outs.append(jnp.sum(full * tab, axis=0, keepdims=True))
            term = cw[k : k + 1] * jnp.sum(hist_k * tab, axis=0, keepdims=True)
            score = term if score is None else score + term
        tb[:, at] = whole.astype(BF16)
        sm[:, at] = jnp.concatenate(outs + [score, gain_term, jnp.zeros((3, TILE), F32)], axis=0)
        return carry

    lax.fori_loop(0, chans // TILE, table_step, 0)

    t_rs, sm_z = {}, []
    turns = [(s + e + 1) % n_seq for e in range(n_seq)]
    chunk = chans // n_seq

    def part_of(j):
        return pl.ds(pl.multiple_of(j * chunk, 128), chunk)

    def send_table(e):
        for n, dd in enumerate(dp_peers):
            block = tb.at[pl.ds(pl.multiple_of(dd * t_dp + turns[e] * t_seq, t_seq), t_seq)]
            t_rs[e, n] = remote(block, tr.at[e, n], s_trs.at[e, n], r_trs.at[e, n], (dd, s, t))
            t_rs[e, n].start()

    def corner_rows(j):
        return pl.ds(pl.multiple_of(corner * t_dp + j * t_seq, t_seq), t_seq)

    send_table(0)
    for e, ss in enumerate(seq_peers):
        sm_z.append(
            remote(sm.at[:, part_of(ss)], sz.at[e], s_sm.at[e], r_sm.at[e], (d, ss, t))
        )
        sm_z[-1].start()

    for h in range(2):
        p1[h, 1].wait_recv()
    q_z = {}
    for e, j in enumerate(turns):
        at = pl.ds(pl.multiple_of(j * cols, 128), cols)
        for h in range(2):
            p2[h, e].wait_recv()
            rows_h = q_rows(h, bit1[h], bit2[h])
            block = q[rows_h, at].astype(F32) + r1[h, 1, :, at].astype(F32)
            block = block + r2[h, e].astype(F32)
            if e < n_seq - 1:
                zb[h, e] = block.astype(BF16)
                q_z[h, e] = remote(
                    zb.at[h, e], zr.at[h, e], s_z.at[h, e], r_z.at[h, e], (d, j, t)
                )
                q_z[h, e].start()
            else:
                own_z[h] = block
        if e % 2:
            send_table(e // 2 + 1)
    for e in range(n_seq // 2 + 1, n_seq):
        send_table(e)

    for copy in z_first:
        copy.wait_recv()
    block = late[s].astype(F32)
    for e in range(n_seq - 1):
        block = block + zq[e].astype(F32)
    zs[...] = block.astype(BF16)
    z_rs = []
    for n, dd in enumerate(dp_peers):
        rows_n = pl.ds(pl.multiple_of(dd * step_z, BLOCK), step_z)
        z_rs.append(remote(zs.at[rows_n], zd.at[n], s_zd.at[n], r_zd.at[n], (dd, s, t)))
        z_rs[-1].start()

    t_z = {}
    for e, j in enumerate(turns):
        acc = tb[pl.ds(pl.multiple_of(d * t_dp + j * t_seq, t_seq), t_seq), :].astype(F32)
        for n in range(3):
            t_rs[e, n].wait_recv()
            acc = acc + tr[e, n].astype(F32)
        if e < n_seq - 1:
            ts[e] = acc.astype(BF16)
            t_z[e] = remote(ts.at[e], tz.at[e], s_tz.at[e], r_tz.at[e], (d, j, t))
            t_z[e].start()
        else:
            own_t[...] = acc

    acc = sm[:, part_of(s)]
    for e, copy in enumerate(sm_z):
        copy.wait_recv()
        acc = acc + sz[e]
    sd[d] = acc
    sm_d = []
    for n, dd in enumerate(dp_peers):
        sm_d.append(remote(sd.at[d], sd.at[d], s_sm.at[3 + n], r_sm.at[3 + n], (dd, s, t)))
        sm_d[-1].start()

    ag = []

    def share(out, rows_of, send, recv, via=None, near=False):
        targets = dp_peers if via is None and not near else dp_peers[:2]
        copies = []
        for n, dd in enumerate(targets):
            mine = out.at[rows_of(d)]
            copies.append(remote(mine, mine, send.at[n], recv.at[n], (dd, s, t)))
            copies[-1].start()
        ag.extend(copy for n, copy in enumerate(copies) if n != via)
        if via is None:
            return None

        def relay():
            copies[via].wait_recv()
            passed.append(copies[via])
            theirs = out.at[rows_of(dp_peers[via])]
            ag.append(
                remote(theirs, theirs, send.at[2], recv.at[2], (dp_peers[1 - via], s, t))
            )
            ag[-1].start()

        return relay

    passed = []

    block = zs[pl.ds(pl.multiple_of(d * step_z, BLOCK), step_z), :].astype(F32)
    for n in range(3):
        z_rs[n].wait_recv()
        block = block + zd[n].astype(F32)
    def late_rows(dd):
        return pl.ds(pl.multiple_of(first_z + dd * step_z, BLOCK), step_z)

    query_ref[late_rows(d), :] = block.astype(BF16)
    share(query_ref, late_rows, s_ag.at[2], r_ag.at[2])

    relays = []
    for h in range(2):
        block = own_z[h]
        for e in range(n_seq - 1):
            q_z[h, e].wait_recv()
            block = block + zr[h, e].astype(F32)

        def early_rows(dd, h=h):
            bits = (dd % 2, dd // 2)
            return q_rows(h, bits[h], bits[1 - h])

        query_ref[early_rows(d), :] = block.astype(BF16)
        relays.append(share(query_ref, early_rows, s_ag.at[h], r_ag.at[h], h))

    acc = own_t[...]
    for e in range(n_seq - 1):
        t_z[e].wait_recv()
        acc = acc + tz[e].astype(F32)

    def table_rows(j):
        return lambda dd: pl.ds(pl.multiple_of(dd * t_dp + j * t_seq, t_seq), t_seq)

    mine = table_rows(s)(d)
    tab_ref[mine, :] = acc.astype(BF16)
    t_back = []
    for e, ss in enumerate(seq_peers):
        t_back.append(
            remote(tab_ref.at[mine], tab_ref.at[mine], s_tb.at[e], r_tb.at[e], (d, ss, t))
        )
        t_back[-1].start()
    share(tab_ref, table_rows(s), s_ta.at[n_seq - 1], r_ta.at[n_seq - 1])
    crossed = ag.pop()
    passed.append(crossed)
    for copy in sm_d:
        copy.wait_recv()
    small_ref[:, part_of(s)] = (sd[0] + sd[1]) + (sd[2] + sd[3])
    for e, ss in enumerate(seq_peers):
        block = small_ref.at[:, part_of(s)]
        sm_d.append(remote(block, block, s_sm.at[6 + e], r_sm.at[6 + e], (d, ss, t)))
        sm_d[-1].start()
    crossed.wait_recv()
    t_back_c = []
    for e, ss in enumerate(seq_peers):
        block = tab_ref.at[corner_rows(s)]
        t_back_c.append(remote(block, block, s_ca.at[e], r_ca.at[e], (d, ss, t)))
        t_back_c[-1].start()
    for e in range(n_seq - 1):
        t_back[e].wait_recv()
        share(
            tab_ref, table_rows((s + n_seq - 1 - e) % n_seq), s_ta.at[e], r_ta.at[e], near=True
        )
        if e < 2:
            relays.pop(0)()

    for copy in sm_d[3:] + ag + t_back_c:
        copy.wait_recv()
    for h in range(2):
        p1[h, 1].wait_send()
    for group in (p2, q_z, t_rs, t_z):
        for copy in group.values():
            copy.wait_send()
    for copy in z_first + z_rs + t_back + t_back_c + sm_z + sm_d + ag + passed:
        copy.wait_send()


def finish_kernel(tab_ref, small_ref, query_ref, tab_out, conv_out, score_out, gain_out, query_out):
    conv_out[...] = small_ref[0:3]
    score_out[...] = small_ref[3:4]
    gain_out[...] = small_ref[4:5]
    tab_out[...] = tab_ref[...]
    query_out[...] = query_ref[...]


def pad8(value):
    return jnp.concatenate([value, jnp.zeros((8 - value.shape[0], value.shape[1]), F32)], axis=0)


def sum_parts(value):
    return value[0:8] + value[8:16] + value[16:24]


def fused_body(
    byte_ids, pad_lengths, table, conv_weight, score_weight, norm_gain, query_weight, query_grad
):
    count = byte_ids.shape[1]
    rows = count // 2
    vocab, chans = table.shape
    width = query_grad.shape[2]
    n_seq = lax.axis_size("seq")
    cols = width // n_seq
    first_z = 3 * chans // 4
    part, t_dp = first_z // 8, vocab // 4
    t_seq, step_z, others = t_dp // n_seq, (chans - first_z) // 4, n_seq - 1
    vm = pl.BlockSpec(memory_space=pltpu.VMEM)
    sm = pl.BlockSpec(memory_space=pltpu.SMEM)
    hbm = pl.BlockSpec(memory_space=pl.ANY)
    V, DMA = pltpu.VMEM, pltpu.SemaphoreType.DMA
    tab, small, query = pl.pallas_call(
        fused_kernel,
        out_shape=(V((vocab, chans), BF16), V((8, chans), F32), V((chans, cols), BF16)),
        in_specs=[sm, vm, hbm] + [vm] * 3 + [hbm] * 2,
        out_specs=(vm,) * 3,
        scratch_shapes=[
            V((vocab, chans), BF16),
            V((chans, width), BF16), V((rows, width), BF16), V((3 * vocab, chans), BF16),
            V((3, vocab, rows), BF16), V((rows, 3 * vocab), BF16), V((rows, chans), F32),
            V((rows, chans), F32), V((rows, chans), BF16), V((rows, chans), BF16),
            V((first_z, width), BF16), V((8, 8, rows), jnp.int32), V((6, 8, rows), F32),
            V((6, 8, rows), F32), V((8, rows), F32), V((3, vocab, 128), F32),
            V((3 * vocab, rows), F32), V((rows, 128), F32),
            V((8, vocab), F32), V((8, vocab), F32), V((2, 1, 128), jnp.int32),
            V((8, rows), F32), V((8, rows), F32), V((16, rows), F32), V((16, rows), F32),
            V((2, 2, part, width), BF16), V((2, n_seq, part, cols), BF16), V((2, n_seq, part, cols), BF16),
            V((2, others, part, cols), BF16), V((2, others, part, cols), BF16),
            V((2, part, cols), F32), V((n_seq, chans - first_z, cols), BF16), V((others, chans - first_z, cols), BF16),
            V((chans - first_z, cols), BF16), V((3, step_z, cols), BF16),
            V((vocab, chans), BF16), V((n_seq, 3, t_seq, chans), BF16),
            V((others, t_seq, chans), BF16), V((others, t_seq, chans), BF16),
            V((t_seq, chans), F32), V((8, chans), F32), V((others, 8, chans // n_seq), F32),
            V((4, 8, chans // n_seq), F32),
            DMA((3,)), DMA((2,)), DMA((2,)), DMA((3,)), DMA((3,)),
            DMA((2, 2)), DMA((2, 2)), DMA((2, n_seq)), DMA((2, n_seq)),
            DMA((2, others)), DMA((2, others)), DMA((3, 3)), DMA((3, 3)),
            DMA((others,)), DMA((others,)), DMA((3,)), DMA((3,)),
            DMA((n_seq, 3)), DMA((n_seq, 3)), DMA((others,)), DMA((others,)),
            DMA((others,)), DMA((others,)), DMA((n_seq, 3)), DMA((n_seq, 3)),
            DMA((others,)), DMA((others,)),
            DMA((9,)), DMA((9,)),
        ],
        compiler_params=pltpu.CompilerParams(collective_id=0, has_side_effects=True),
        name="fused",
    )(
        pad_lengths, byte_ids, table, conv_weight, score_weight[None, :], norm_gain[None, :],
        query_weight, query_grad[0],
    )
    return pl.pallas_call(
        finish_kernel,
        out_shape=(
            jax.ShapeDtypeStruct((vocab, chans), BF16),
            jax.ShapeDtypeStruct((3, chans), F32),
            jax.ShapeDtypeStruct((1, chans), F32),
            jax.ShapeDtypeStruct((1, chans), F32),
            jax.ShapeDtypeStruct((chans, cols), BF16),
        ),
        in_specs=[vm] * 3,
        out_specs=(vm,) * 5,
        name="finish",
    )(*(pltpu.with_memory_space_constraint(part, pltpu.VMEM) for part in (tab, small, query)))


def fused_outer(*args):
    tab, conv, score, gain, query = fused_body(*args)
    return (tab, conv, score.reshape(-1), gain.reshape(-1), query)


def fits(mesh):
    return mesh.shape["dp"] == 4 and mesh.shape["seq"] == 4 and mesh.shape["tensor"] == 2


def solution(mesh):
    return jax.shard_map(
        fused_outer if fits(mesh) else body,
        mesh=mesh,
        in_specs=(
            P("dp", "seq"),
            P("dp"),
            P(None, "tensor"),
            P(None, "tensor"),
            P("tensor"),
            P("tensor"),
            P("tensor", None),
            P("dp", "seq", None),
        ),
        out_specs=(
            P(None, "tensor"),
            P(None, "tensor"),
            P("tensor"),
            P("tensor"),
            P("tensor", "seq"),
        ),
        check_vma=False,
    )
```
